32 devices in a mesh: clip: 2 (over y), frame: 4 (over x, core), tensor: 4 (over z).
Axes of the slice: x: 2, y: 2, z: 4, core: 2. Of those that a mesh axis runs over, the one named last changes fastest.
Arguments:
- x_in: bfloat16 [2, 16, 256, 1152], P('clip', 'frame', 'tensor'), may hold values from -6 to 6
- cond: bfloat16 [2, 1152], P('clip'), may hold values from -6 to 6
- mod_weight_one: float32 [1152, 6, 1152], P(('clip', 'frame'), None, 'tensor'), may hold values from -0.1875 to 0.1875
- qkv_weight_one: float32 [1152, 3, 1152], P(('clip', 'frame'), None, 'tensor'), may hold values from -0.1875 to 0.1875
- attn_out_one: float32 [1152, 1152], P('tensor', ('clip', 'frame')), may hold values from -0.75 to 0.75
- mlp_up_one: float32 [1152, 4608], P(('clip', 'frame'), 'tensor'), may hold values from -0.1875 to 0.1875
- mlp_down_one: float32 [4608, 1152], P('tensor', ('clip', 'frame')), may hold values from -0.09375 to 0.09375
- mod_weight_two: float32 [1152, 6, 1152], P(('clip', 'frame'), None, 'tensor'), may hold values from -0.1875 to 0.1875
- qkv_weight_two: float32 [1152, 3, 1152], P(('clip', 'frame'), None, 'tensor'), may hold values from -0.1875 to 0.1875
- attn_out_two: float32 [1152, 1152], P('tensor', ('clip', 'frame')), may hold values from -0.375 to 0.375
- mlp_up_two: float32 [1152, 4608], P(('clip', 'frame'), 'tensor'), may hold values from -0.1875 to 0.1875
- mlp_down_two: float32 [4608, 1152], P('tensor', ('clip', 'frame')), may hold values from -0.09375 to 0.09375
- out_cotangent: bfloat16 [2, 16, 256, 1152], P('clip', 'frame', 'tensor'), may hold values from -6 to 6
Outputs:
- layer_out: bfloat16 [2, 16, 256, 1152], P('clip', 'frame', 'tensor')
- input_grad: float32 [2, 16, 256, 1152], P('clip', 'frame', 'tensor')
- cond_grad: float32 [2, 1152], P('clip')
- grad_mod_one: float32 [1152, 6, 1152], P(('clip', 'frame'), None, 'tensor')
- grad_qkv_one: float32 [1152, 3, 1152], P(('clip', 'frame'), None, 'tensor')
- grad_attn_one: float32 [1152, 1152], P('tensor', ('clip', 'frame'))
- grad_up_one: float32 [1152, 4608], P(('clip', 'frame'), 'tensor')
- grad_down_one: float32 [4608, 1152], P('tensor', ('clip', 'frame'))
- grad_mod_two: float32 [1152, 6, 1152], P(('clip', 'frame'), None, 'tensor')
- grad_qkv_two: float32 [1152, 3, 1152], P(('clip', 'frame'), None, 'tensor')
- grad_attn_two: float32 [1152, 1152], P('tensor', ('clip', 'frame'))
- grad_up_two: float32 [1152, 4608], P(('clip', 'frame'), 'tensor')
- grad_down_two: float32 [4608, 1152], P('tensor', ('clip', 'frame'))
The draws below stay inside these ranges and needn't reach their ends.
All inputs are finite; a program needn't handle non-finite values.
Results may differ from the reference program's by a relative error of at most 0.02.
Values may be sent and summed in bfloat16 or wider, within the bound.
No kernel may reach another device: no remote copies, remote signals or barrier semaphores. Data moves between devices by JAX's collectives and lax.ppermute only.
A program may use at most 192 MiB of HBM per device.

```python
import jax
import jax.numpy as jnp
from jax import lax

D = 1152
HEADS = 16
HD = 72
FF = 4608
PLACES = 256
FRAMES = 16
CLIPS = 2


def spiked(array, rng, source, target, blocks, factor):
    def block_of(axis_at):
        return (jnp.arange(array.shape[axis_at]) // (array.shape[axis_at] // blocks)).reshape((-1,) + (1,) * (array.ndim - 1 - axis_at))

    near = jax.random.permutation(rng, blocks)[block_of(target)]
    other_side = (block_of(target) + blocks // 2) % blocks
    return jnp.where((block_of(source) == near) | (block_of(source) == other_side), factor * array, array)


def level_of(own_key, shape, split, smallest, high):
    gain = 1.0
    for axis_at, parts in split:
        steps = jax.random.uniform(jax.random.fold_in(jax.random.fold_in(own_key, 6), axis_at), (parts,), jnp.float32, smallest / len(split), high / len(split))
        gain = gain * jnp.repeat(jnp.exp(steps), shape[axis_at] // parts).reshape((-1,) + (1,) * (len(shape) - 1 - axis_at))
    return gain


def scatter_about(rng, extent, deviation, limit, shards=(), held_as=jnp.bfloat16):
    drawn = deviation * jax.random.normal(rng, extent, jnp.float32)
    if shards:
        drawn = drawn * level_of(rng, extent, shards, -0.22, 0.18)
    return jnp.clip(drawn, -limit, limit).astype(held_as)


def bell_draw_with(key, extent, width, reach, pieces, heavy, held_as=jnp.bfloat16):
    array = width * jax.random.normal(key, extent, jnp.float32)
    if pieces:
        array = array * level_of(key, extent, pieces, -0.22, 0.18)
    return jnp.clip(spiked(array, jax.random.fold_in(key, 3), *heavy), -reach, reach).astype(held_as)


def setup_inputs(seed: int = 0) -> dict:
    arg_keys = jax.random.split(jax.random.key(seed), 14)
    return {
        "x_in": scatter_about(arg_keys[0], (CLIPS, FRAMES, PLACES, D), 1.0, 6.0, ((0, 2), (1, 4), (2, 4))),
        "cond": scatter_about(arg_keys[1], (CLIPS, D), 1.0, 6.0, ((0, 2),)),
        "mod_weight_one": scatter_about(arg_keys[2], (D, 6, D), D ** -0.5, 0.1875, ((0, 8), (2, 4)), jnp.float32),
        "qkv_weight_one": scatter_about(arg_keys[3], (D, 3, D), D ** -0.5, 0.1875, ((0, 8), (2, 4)), jnp.float32),
        "attn_out_one": scatter_about(arg_keys[4], (D, D), (D // 16) ** -0.5, 0.75, ((0, 4), (1, 8)), jnp.float32),
        "mlp_up_one": scatter_about(arg_keys[5], (D, FF), D ** -0.5, 0.1875, ((0, 8), (1, 4)), jnp.float32),
        "mlp_down_one": scatter_about(arg_keys[6], (FF, D), FF ** -0.5, 0.09375, ((0, 4), (1, 8)), jnp.float32),
        "mod_weight_two": scatter_about(arg_keys[7], (D, 6, D), D ** -0.5, 0.1875, ((0, 8), (2, 4)), jnp.float32),
        "qkv_weight_two": scatter_about(arg_keys[8], (D, 3, D), D ** -0.5, 0.1875, ((0, 8), (2, 4)), jnp.float32),
        "attn_out_two": scatter_about(arg_keys[9], (D, D), (D // 4) ** -0.5, 0.375, ((0, 4), (1, 8)), jnp.float32),
        "mlp_up_two": scatter_about(arg_keys[10], (D, FF), D ** -0.5, 0.1875, ((0, 8), (1, 4)), jnp.float32),
        "mlp_down_two": scatter_about(arg_keys[11], (FF, D), FF ** -0.5, 0.09375, ((0, 4), (1, 8)), jnp.float32),
        "out_cotangent": bell_draw_with(arg_keys[12], (CLIPS, FRAMES, PLACES, D), 1.0, 6.0, ((0, 2), (1, 4), (2, 4)), (1, 3, 4, 2.0)),
    }


@jax.custom_vjp
def low(v):
    return lax.optimization_barrier(v.astype(jnp.bfloat16)).astype(jnp.float32)

@jax.custom_vjp
def low_back(v):
    return v

def low_keep(v):
    return (low(v), None)

def low_pass(kept, grad):
    return (grad,)

def back_keep(v):
    return (v, None)

def back_low(kept, grad):
    return (low(grad),)
low.defvjp(low_keep, low_pass)
low_back.defvjp(back_keep, back_low)
HIGHEST_PRECISION = lax.Precision.HIGHEST
SCORE_FORMS = {True: 'cfphe,cfqhe->cfhpq', False: 'cfphe,cgphe->cphfg'}
APPLY_FORMS = {True: 'cfhpq,cfqhe->cfphe', False: 'cphfg,cgphe->cfphe'}

def layer_norm(stream):
    centre = stream - lax.optimization_barrier(jnp.mean(stream, axis=-1, keepdims=True))
    return centre * lax.rsqrt(lax.optimization_barrier(jnp.mean(centre * centre, axis=-1, keepdims=True)) + 1e-06)

def gelu_tanh(inputs):
    return 0.5 * inputs * (1.0 + jnp.tanh(0.7978845608028654 * (inputs + 0.044715 * inputs * inputs * inputs)))

def choose(modulation, column):
    return modulation[:, column][:, None, None, :]

def block(stream, silu_cond, weights, spatial):
    mod_weight, qkv_weight, attn_weight, up_weight, down_weight = weights
    modulation = jnp.einsum('cd,dkz->ckz', silu_cond, low(mod_weight), precision=HIGHEST_PRECISION)
    modulated = low(layer_norm(stream) * (1.0 + choose(modulation, 1)) + choose(modulation, 0))
    projected = low_back(low(jnp.einsum('cfpd,dkz->cfpkz', modulated, low(qkv_weight), precision=HIGHEST_PRECISION)))
    leading = projected.shape[:3]
    queries = projected[:, :, :, 0].reshape(leading + (HEADS, HD))
    key_rows = projected[:, :, :, 1].reshape(leading + (HEADS, HD))
    values = projected[:, :, :, 2].reshape(leading + (HEADS, HD))
    scores = low_back(jnp.einsum(SCORE_FORMS[spatial], queries, key_rows, precision=HIGHEST_PRECISION) * HD ** (-0.5))
    probs = jax.nn.softmax(scores, axis=-1)
    attended = jnp.einsum(APPLY_FORMS[spatial], low(probs), values, precision=HIGHEST_PRECISION)
    attended = low_back(low(attended.reshape(leading + (D,))))
    branch_attn = low_back(jnp.einsum('cfpz,zd->cfpd', attended, low(attn_weight), precision=HIGHEST_PRECISION))
    middle = stream + choose(modulation, 2) * branch_attn
    modulated_mlp = low(layer_norm(middle) * (1.0 + choose(modulation, 4)) + choose(modulation, 3))
    hidden_pre = low_back(jnp.einsum('cfpd,dz->cfpz', modulated_mlp, low(up_weight), precision=HIGHEST_PRECISION))
    hidden_act = low(gelu_tanh(hidden_pre))
    branch_mlp = low_back(jnp.einsum('cfpz,zd->cfpd', hidden_act, low(down_weight), precision=HIGHEST_PRECISION))
    return middle + choose(modulation, 5) * branch_mlp

def forward(clip_input, clip_cond, *weights):
    silu_cond = low(jax.nn.silu(clip_cond))[None]
    first = block(clip_input[None], silu_cond, weights[:5], True)
    second = block(first, silu_cond, weights[5:], False)
    return second[0]

def reference(x_in, cond, mod_weight_one, qkv_weight_one, attn_out_one, mlp_up_one, mlp_down_one, mod_weight_two, qkv_weight_two, attn_out_two, mlp_up_two, mlp_down_two, out_cotangent):
    weights = (mod_weight_one, qkv_weight_one, attn_out_one, mlp_up_one, mlp_down_one, mod_weight_two, qkv_weight_two, attn_out_two, mlp_up_two, mlp_down_two)

    def per_clip(totals, clip_item):
        clip_input, clip_cond, clip_cotangent = clip_item
        result, pullback = jax.vjp(forward, clip_input.astype(jnp.float32), clip_cond.astype(jnp.float32), *weights)
        grads = pullback(clip_cotangent.astype(jnp.float32))
        totals = tuple((total + grad for total, grad in zip(totals, grads[2:])))
        return (totals, (result.astype(jnp.bfloat16), grads[0], grads[1]))
    initial = tuple((jnp.zeros(weight.shape, jnp.float32) for weight in weights))
    totals, (layer_out, input_grad, cond_grad) = lax.scan(per_clip, initial, (x_in, cond, out_cotangent))
    return (layer_out, input_grad, cond_grad, totals[0], totals[1], totals[2], totals[3], totals[4], totals[5], totals[6], totals[7], totals[8], totals[9])
```

```python
import functools

import jax
import jax.numpy as jnp
from jax import lax
from jax.experimental import pallas as pl
from jax.experimental.pallas import tpu as pltpu
from jax.sharding import PartitionSpec as P

HD = 72
FRAMES = 16
CLIP, FRAME, TENSOR = "clip", "frame", "tensor"
SHARDS = (CLIP, FRAME)


HIGHEST_PRECISION = lax.Precision.HIGHEST
SCORE_FORMS = {True: "cfphe,cfqhe->cfhpq", False: "cfphe,cgphe->cphfg"}
APPLY_FORMS = {True: "cfhpq,cfqhe->cfphe", False: "cphfg,cgphe->cfphe"}
BACK_FORMS = {True: "cfhpq,cfphe->cfqhe", False: "cphfg,cfphe->cgphe"}
GELU_COEFF = 0.7978845608028654
CUBIC_COEFF = 0.044715


def layer_norm(stream):
    centre = stream - jnp.mean(stream, axis=-1, keepdims=True)
    inv_scale = lax.rsqrt(jnp.mean(centre * centre, axis=-1, keepdims=True) + 1e-06)
    return (centre * inv_scale, inv_scale)


def norm_back(normed, inv_scale, upstream):
    return inv_scale * (
        upstream
        - jnp.mean(upstream, axis=-1, keepdims=True)
        - normed * jnp.mean(upstream * normed, axis=-1, keepdims=True)
    )


def gelu_tanh(inputs):
    return (
        0.5
        * inputs
        * (1.0 + jnp.tanh(GELU_COEFF * (inputs + CUBIC_COEFF * inputs * inputs * inputs)))
    )


def gelu_slope(inputs):
    tangent = jnp.tanh(GELU_COEFF * (inputs + CUBIC_COEFF * inputs * inputs * inputs))
    return 0.5 * (1.0 + tangent) + 0.5 * inputs * (1.0 - tangent * tangent) * GELU_COEFF * (
        1.0 + 3.0 * CUBIC_COEFF * inputs * inputs
    )


def choose(modulation, column):
    return modulation[:, column][:, None, None, :]


def split_heads(projected):
    leading = projected.shape[:3]
    row_width = projected.shape[-1]
    head_count = row_width // HD
    queries = projected[:, :, :, 0].reshape(leading + (head_count, HD))
    key_rows = projected[:, :, :, 1].reshape(leading + (head_count, HD))
    values = projected[:, :, :, 2].reshape(leading + (head_count, HD))
    return (queries, key_rows, values, leading, row_width)


def attend(projected, spatial):
    queries, key_rows, values, leading, row_width = split_heads(projected)
    scores = jnp.einsum(
        SCORE_FORMS[spatial], queries, key_rows, preferred_element_type=jnp.float32
    ) * HD ** (-0.5)
    highest = jnp.max(scores, axis=-1, keepdims=True)
    expo = jnp.exp(scores - highest)
    denominator = jnp.sum(expo, axis=-1, keepdims=True)
    probs = (expo / denominator).astype(jnp.bfloat16)
    log_total = highest + jnp.log(denominator)
    attended = jnp.einsum(APPLY_FORMS[spatial], probs, values, preferred_element_type=jnp.float32)
    return (attended.reshape(leading + (row_width,)).astype(jnp.bfloat16), log_total)


def attend_back(projected, log_total, d_attended, spatial):
    queries, key_rows, values, leading, row_width = split_heads(projected)
    scale_factor = HD ** (-0.5)
    scores = (
        jnp.einsum(SCORE_FORMS[spatial], queries, key_rows, preferred_element_type=jnp.float32)
        * scale_factor
    )
    probs = jnp.exp(scores - log_total)
    upstream = d_attended.reshape(leading + (row_width // HD, HD))
    d_probs = jnp.einsum(SCORE_FORMS[spatial], upstream, values, preferred_element_type=jnp.float32)
    d_values = jnp.einsum(
        BACK_FORMS[spatial],
        probs.astype(jnp.bfloat16),
        upstream,
        preferred_element_type=jnp.float32,
    )
    row_inner = jnp.sum(probs * d_probs, axis=-1, keepdims=True)
    d_scores = (probs * (d_probs - row_inner)).astype(jnp.bfloat16)
    d_queries = (
        jnp.einsum(APPLY_FORMS[spatial], d_scores, key_rows, preferred_element_type=jnp.float32)
        * scale_factor
    )
    d_keys = (
        jnp.einsum(BACK_FORMS[spatial], d_scores, queries, preferred_element_type=jnp.float32)
        * scale_factor
    )
    stacked = jnp.stack([d_queries, d_keys, d_values], axis=3)
    return stacked.reshape(leading + (3, row_width)).astype(jnp.bfloat16)


def fetch_weights(weights):
    cast = tuple((weight.astype(jnp.bfloat16) for weight in weights))
    return (
        lax.all_gather(cast[0], SHARDS, axis=0, tiled=True),
        lax.all_gather(cast[1], SHARDS, axis=0, tiled=True),
        lax.all_gather(cast[2], SHARDS, axis=1, tiled=True),
        lax.all_gather(cast[3], SHARDS, axis=0, tiled=True),
        lax.all_gather(cast[4], SHARDS, axis=1, tiled=True),
    )


def backward_weights(weights):
    cast = tuple((weight.astype(jnp.bfloat16) for weight in weights))
    return (
        lax.all_gather(cast[0], SHARDS, axis=0, tiled=True),
        lax.all_gather(cast[1], SHARDS, axis=0, tiled=True),
        lax.all_gather(cast[2], SHARDS, axis=1, tiled=True),
        lax.all_gather(cast[3], SHARDS, axis=0, tiled=True),
        lax.all_gather(cast[4], SHARDS, axis=1, tiled=True),
    )


def spread_rows(rows):
    return lax.all_gather(rows, TENSOR, axis=2, tiled=True)


def collect_rows(term):
    return lax.psum_scatter(term, TENSOR, scatter_dimension=2, tiled=True)


def attention_output(attended, attn_weight):
    return collect_rows(
        jnp.einsum("cfpz,zd->cfpd", attended, attn_weight, preferred_element_type=jnp.float32)
    )


def layer_forward(stream, silu_cond, gathered, spatial):
    mod_weight, qkv_weight, attn_weight, up_weight, down_weight = gathered
    partial_value = jnp.einsum(
        "cd,dkz->ckz", silu_cond, mod_weight, preferred_element_type=jnp.float32
    )
    modulation = lax.all_gather(partial_value, TENSOR, axis=2, tiled=True)
    normed, inv_scale = layer_norm(stream)
    modulated = (normed * (1.0 + choose(modulation, 1)) + choose(modulation, 0)).astype(
        jnp.bfloat16
    )
    gathered_rows = spread_rows(modulated)
    projected = jnp.einsum(
        "cfpd,dkz->cfpkz", gathered_rows, qkv_weight, preferred_element_type=jnp.float32
    ).astype(jnp.bfloat16)
    if spatial:
        project_held = projected
        attended, log_total = attend(project_held, True)
    else:
        project_held = lax.all_to_all(projected, FRAME, split_axis=2, concat_axis=1, tiled=True)
        placed, log_total = attend(project_held, False)
        attended = lax.all_to_all(placed, FRAME, split_axis=1, concat_axis=2, tiled=True)
    branch_attn = attention_output(attended, attn_weight)
    middle = stream + choose(modulation, 2) * branch_attn
    normed_mlp, inv_mlp = layer_norm(middle)
    modulated_mlp = (normed_mlp * (1.0 + choose(modulation, 4)) + choose(modulation, 3)).astype(
        jnp.bfloat16
    )
    gathered_mlp = spread_rows(modulated_mlp)
    hidden_pre = jnp.einsum(
        "cfpd,dz->cfpz", gathered_mlp, up_weight, preferred_element_type=jnp.float32
    )
    hidden_act = gelu_tanh(hidden_pre).astype(jnp.bfloat16)
    branch_mlp = collect_rows(
        jnp.einsum("cfpz,zd->cfpd", hidden_act, down_weight, preferred_element_type=jnp.float32)
    )
    result = middle + choose(modulation, 5) * branch_mlp
    stored = (
        modulation,
        normed,
        inv_scale,
        gathered_rows,
        project_held,
        log_total,
        attended,
        branch_attn,
        normed_mlp,
        inv_mlp,
        gathered_mlp,
        hidden_pre,
        hidden_act,
        branch_mlp,
    )
    return (result, stored)


def layer_backward(upstream, silu_cond, gathered, stored, spatial):
    mod_weight, qkv_weight, attn_weight, up_weight, down_weight = gathered
    (
        modulation,
        normed,
        inv_scale,
        gathered_rows,
        project_held,
        log_total,
        attended,
        branch_attn,
        normed_mlp,
        inv_mlp,
        gathered_mlp,
        hidden_pre,
        hidden_act,
        branch_mlp,
    ) = stored
    d_branch_mlp = (upstream * choose(modulation, 5)).astype(jnp.bfloat16)
    d_gate_mlp = jnp.sum(upstream * branch_mlp, axis=(1, 2))
    d_branch_all = spread_rows(d_branch_mlp)
    grad_down = jnp.einsum(
        "cfpz,cfpd->zd", hidden_act, d_branch_all, preferred_element_type=jnp.float32
    )
    d_act = jnp.einsum(
        "cfpd,zd->cfpz", d_branch_all, down_weight, preferred_element_type=jnp.float32
    )
    d_pre = (d_act * gelu_slope(hidden_pre)).astype(jnp.bfloat16)
    grad_up = jnp.einsum("cfpd,cfpz->dz", gathered_mlp, d_pre, preferred_element_type=jnp.float32)
    d_mod_mlp = collect_rows(
        jnp.einsum("cfpz,dz->cfpd", d_pre, up_weight, preferred_element_type=jnp.float32)
    )
    d_shift_mlp = jnp.sum(d_mod_mlp, axis=(1, 2))
    d_scale_mlp = jnp.sum(d_mod_mlp * normed_mlp, axis=(1, 2))
    d_middle = upstream + norm_back(normed_mlp, inv_mlp, d_mod_mlp * (1.0 + choose(modulation, 4)))
    d_branch_attn = (d_middle * choose(modulation, 2)).astype(jnp.bfloat16)
    d_gate_attn = jnp.sum(d_middle * branch_attn, axis=(1, 2))
    d_attn_all = spread_rows(d_branch_attn)
    grad_attn = jnp.einsum(
        "cfpz,cfpd->zd", attended, d_attn_all, preferred_element_type=jnp.float32
    )
    d_attended = jnp.einsum(
        "cfpd,zd->cfpz", d_attn_all, attn_weight, preferred_element_type=jnp.float32
    ).astype(jnp.bfloat16)
    if spatial:
        d_projected = attend_back(project_held, log_total, d_attended, True)
    else:
        d_placed = lax.all_to_all(d_attended, FRAME, split_axis=2, concat_axis=1, tiled=True)
        d_projected = lax.all_to_all(
            attend_back(project_held, log_total, d_placed, False),
            FRAME,
            split_axis=1,
            concat_axis=2,
            tiled=True,
        )
    grad_qkv = jnp.einsum(
        "cfpd,cfpkz->dkz", gathered_rows, d_projected, preferred_element_type=jnp.float32
    )
    d_modulated = collect_rows(
        jnp.einsum("cfpkz,dkz->cfpd", d_projected, qkv_weight, preferred_element_type=jnp.float32)
    )
    d_shift_attn = jnp.sum(d_modulated, axis=(1, 2))
    d_scale_attn = jnp.sum(d_modulated * normed, axis=(1, 2))
    d_stream = d_middle + norm_back(normed, inv_scale, d_modulated * (1.0 + choose(modulation, 1)))
    d_modulation = jnp.stack(
        [d_shift_attn, d_scale_attn, d_gate_attn, d_shift_mlp, d_scale_mlp, d_gate_mlp], axis=1
    )
    d_mod_own = lax.psum_scatter(d_modulation, TENSOR, scatter_dimension=2, tiled=True)
    grad_mod = jnp.einsum(
        "cd,ckz->dkz", silu_cond.astype(jnp.float32), d_mod_own, precision=HIGHEST_PRECISION
    )
    d_silu = jnp.einsum(
        "ckz,dkz->cd", d_mod_own, mod_weight.astype(jnp.float32), precision=HIGHEST_PRECISION
    )
    grads = (
        lax.psum_scatter(
            grad_mod.astype(jnp.bfloat16), SHARDS, scatter_dimension=0, tiled=True
        ).astype(jnp.float32),
        lax.psum_scatter(
            grad_qkv.astype(jnp.bfloat16), SHARDS, scatter_dimension=0, tiled=True
        ).astype(jnp.float32),
        lax.psum_scatter(
            grad_attn.astype(jnp.bfloat16), SHARDS, scatter_dimension=1, tiled=True
        ).astype(jnp.float32),
        lax.psum_scatter(
            grad_up.astype(jnp.bfloat16), SHARDS, scatter_dimension=0, tiled=True
        ).astype(jnp.float32),
        lax.psum_scatter(
            grad_down.astype(jnp.bfloat16), SHARDS, scatter_dimension=1, tiled=True
        ).astype(jnp.float32),
    )
    return (d_stream, d_silu, grads)


def local(
    x_in,
    cond,
    mod_weight_one,
    qkv_weight_one,
    attn_out_one,
    mlp_up_one,
    mlp_down_one,
    mod_weight_two,
    qkv_weight_two,
    attn_out_two,
    mlp_up_two,
    mlp_down_two,
    out_cotangent,
):
    weights_first = (mod_weight_one, qkv_weight_one, attn_out_one, mlp_up_one, mlp_down_one)
    weights_second = (mod_weight_two, qkv_weight_two, attn_out_two, mlp_up_two, mlp_down_two)
    cond_float = cond.astype(jnp.float32)
    silu_cond = jax.nn.silu(cond_float).astype(jnp.bfloat16)
    gathered_first = fetch_weights(weights_first)
    middle_stream, stored_first = layer_forward(
        x_in.astype(jnp.float32), silu_cond, gathered_first, True
    )
    gathered_second = fetch_weights(weights_second)
    result, stored_second = layer_forward(middle_stream, silu_cond, gathered_second, False)
    back_second = backward_weights(weights_second)
    d_middle_stream, d_silu_second, grads_second = layer_backward(
        out_cotangent.astype(jnp.float32), silu_cond, back_second, stored_second, False
    )
    back_first = backward_weights(weights_first)
    input_grad, d_silu_first, grads_first = layer_backward(
        d_middle_stream, silu_cond, back_first, stored_first, True
    )
    d_silu_total = lax.psum(d_silu_first + d_silu_second, (FRAME, TENSOR))
    sigmoid_cond = jax.nn.sigmoid(cond_float)
    cond_grad = d_silu_total * (sigmoid_cond * (1.0 + cond_float * (1.0 - sigmoid_cond)))
    return (
        result.astype(jnp.bfloat16),
        input_grad,
        cond_grad,
        grads_first[0],
        grads_first[1],
        grads_first[2],
        grads_first[3],
        grads_first[4],
        grads_second[0],
        grads_second[1],
        grads_second[2],
        grads_second[3],
        grads_second[4],
    )

def flip(array, axis, bit):
    count = lax.axis_size(axis)
    return lax.ppermute(array, axis, [(i, i ^ bit) for i in range(count)])


def exchange_sum(array, axis):
    bit = 1
    while bit < lax.axis_size(axis):
        array = array + flip(array, axis, bit)
        bit *= 2
    return array


def place_along(array, axis):
    count = lax.axis_size(axis)
    own = (jnp.arange(count) == lax.axis_index(axis)).reshape((count,) + (1,) * array.ndim)
    return exchange_sum(jnp.where(own, array[None], 0.0), axis)


def first_flip(shard):
    return 2 if shard % 2 == 0 else 4


def hop(array, which):
    if which == 0:
        pairs = [(i, i ^ 1) for i in range(8)]
    elif which == 1:
        pairs = [(i, i ^ first_flip(i)) for i in range(8)]
    else:
        pairs = [(i, i ^ (6 - first_flip(i))) for i in range(8)]
    return lax.ppermute(array, SHARDS, pairs)


def shard_index():
    return lax.axis_index(CLIP) * lax.axis_size(FRAME) + lax.axis_index(FRAME)


def piece_order():
    shard = shard_index()
    first = jnp.where(shard % 2 == 0, 2, 4)
    second = 6 - first
    masks = [0, first, second, 6, 1, 1 ^ second, 1 ^ first, 7]
    return jnp.stack([shard ^ mask for mask in masks]).astype(jnp.int32)


def gather_piece(piece):
    own = lax.all_gather(piece, TENSOR, axis=0, tiled=False)
    near = hop(own, 1)
    mine = (own, near, hop(own, 2), hop(near, 2))
    return mine + tuple(hop(array, 0) for array in mine)


def scatter_piece(grad):
    keep, send = grad
    got = hop(send, 0)
    wide = lambda array: array.astype(jnp.float32)
    low = lambda array: array.astype(jnp.bfloat16)
    far = hop(low(wide(keep[2:]) + wide(got[2:])), 2)
    near = hop(low(wide(keep[1]) + wide(got[1]) + wide(far[1])), 1)
    own = low(wide(keep[0]) + wide(got[0]) + wide(far[0]) + wide(near))
    return lax.psum_scatter(own, TENSOR, scatter_dimension=0, tiled=False)


def pack_layer(weights):
    qkv, attn, up, down = (weight.astype(jnp.bfloat16) for weight in weights)
    rows = qkv.shape[0]
    attn_part = jnp.concatenate([qkv.reshape(rows, -1), attn.T], axis=1)
    return attn_part, up, down.T


PIECES = 8
VMEM_BYTES = 48 << 20


def contract(left, right, left_dim, right_dim):
    return lax.dot_general(
        left, right, (((left_dim,), (right_dim,)), ((), ())), preferred_element_type=jnp.float32
    )


def assemble(order_ref, piece_refs, whole_ref):
    rows = piece_refs[0].shape[1]
    for j in range(PIECES):
        start = pl.multiple_of(order_ref[j] * rows, 16)
        whole_ref[pl.ds(start, rows), :] = piece_refs[j][0]


def up_kernel(order_ref, x_ref, *refs):
    pre_ref, act_ref, whole_ref = refs[PIECES:]
    assemble(order_ref, refs[:PIECES], whole_ref)
    pre = contract(x_ref[...], whole_ref[...], 1, 0)
    pre_ref[...] = pre
    act_ref[...] = gelu_tanh(pre).astype(jnp.bfloat16)


def slope_kernel(order_ref, x_ref, pre_ref, *refs):
    out_ref, whole_ref = refs[PIECES:]
    assemble(order_ref, refs[:PIECES], whole_ref)
    d_act = contract(x_ref[...], whole_ref[...], 1, 0)
    out_ref[...] = (d_act * gelu_slope(pre_ref[...])).astype(jnp.bfloat16)


def turned_kernel(low, high, order_ref, x_ref, *refs):
    out_ref, whole_ref = refs[PIECES:]
    assemble(order_ref, refs[:PIECES], whole_ref)
    whole = contract(x_ref[...], whole_ref[...], 1, 0)
    out_ref[0] = whole[:, low:high].astype(jnp.bfloat16).T


def collect_kernel(low, high, turned, order_ref, y_ref, *refs):
    out_ref, whole_ref = refs[PIECES:]
    assemble(order_ref, refs[:PIECES], whole_ref)
    rows = y_ref[0].T if turned else y_ref[...]
    term = contract(rows, whole_ref[:, low:high], 1, 1)

    @pl.when(pl.program_id(0) == 0)
    def _():
        out_ref[...] = term

    @pl.when(pl.program_id(0) > 0)
    def _():
        out_ref[...] += term


def deal_out(order_ref, whole_ref, keep_ref, send_ref):
    rows = keep_ref.shape[2]
    for j in range(PIECES):
        start = pl.multiple_of(order_ref[j] * rows, 16)
        to_ref = keep_ref if j < PIECES // 2 else send_ref
        to_ref[j % (PIECES // 2), 0] = whole_ref[pl.ds(start, rows), :]


def grad_kernel(order_ref, x_ref, y_ref, keep_ref, send_ref, whole_ref):
    whole_ref[...] = contract(x_ref[...], y_ref[...], 0, 0).astype(jnp.bfloat16)
    deal_out(order_ref, whole_ref, keep_ref, send_ref)


def attn_grad_kernel(order_ref, x_ref, y_ref, b_ref, a_ref, keep_ref, send_ref, whole_ref):
    split = y_ref.shape[1]
    whole_ref[:, :split] = contract(x_ref[...], y_ref[0].T, 0, 0).astype(jnp.bfloat16)
    whole_ref[:, split:] = contract(b_ref[...], a_ref[0].T, 0, 0).astype(jnp.bfloat16)
    deal_out(order_ref, whole_ref, keep_ref, send_ref)


def masked_scores(queries, keys, group):
    scores = contract(queries, keys, 0, 0) * HD ** (-0.5)
    if group:
        place = lax.broadcasted_iota(jnp.int32, scores.shape, 0) % group
        other = lax.broadcasted_iota(jnp.int32, scores.shape, 1) % group
        scores = jnp.where(place == other, scores, -3e38)
    expo = jnp.exp(scores - jnp.max(scores, axis=-1, keepdims=True))
    return expo / jnp.sum(expo, axis=-1, keepdims=True)


def attend_kernel(group, projected_ref, out_ref):
    part = out_ref.shape[1]
    for start in range(0, part, HD):
        queries, keys, values = (
            projected_ref[0, pl.ds(j * part + start, HD), :] for j in range(3)
        )
        probs = masked_scores(queries, keys, group).astype(jnp.bfloat16)
        out_ref[0, pl.ds(start, HD), :] = contract(values, probs, 1, 1).astype(jnp.bfloat16)


def attend_back_kernel(group, projected_ref, upstream_ref, out_ref):
    part = upstream_ref.shape[1]
    scale_factor = HD ** (-0.5)
    for start in range(0, part, HD):
        queries, keys, values = (
            projected_ref[0, pl.ds(j * part + start, HD), :] for j in range(3)
        )
        upstream = upstream_ref[0, pl.ds(start, HD), :]
        probs = masked_scores(queries, keys, group)
        d_probs = contract(upstream, values, 0, 0)
        row_inner = jnp.sum(probs * d_probs, axis=-1, keepdims=True)
        d_scores = (probs * (d_probs - row_inner)).astype(jnp.bfloat16)
        grads = (
            contract(keys, d_scores, 1, 1) * scale_factor,
            contract(queries, d_scores, 1, 0) * scale_factor,
            contract(upstream, probs.astype(jnp.bfloat16), 1, 0),
        )
        for j in range(3):
            out_ref[0, pl.ds(j * part + start, HD), :] = grads[j].astype(jnp.bfloat16)


def call(kernel, grid, in_specs, out_specs, out_shape, scratch, flops, args):
    moved = sum(a.size * a.dtype.itemsize for a in args)
    moved += sum(o.size * o.dtype.itemsize for o in jax.tree.leaves(out_shape))
    return pl.pallas_call(
        kernel,
        out_shape=out_shape,
        grid_spec=pltpu.PrefetchScalarGridSpec(
            num_scalar_prefetch=1 if scratch else 0,
            grid=grid,
            in_specs=in_specs,
            out_specs=out_specs,
            scratch_shapes=scratch,
        ),
        compiler_params=pltpu.CompilerParams(vmem_limit_bytes=VMEM_BYTES),
        cost_estimate=pl.CostEstimate(flops=flops, bytes_accessed=moved, transcendentals=0),
    )(*args)


def still(shape):
    return pl.BlockSpec(shape, lambda z, *_: (0,) * len(shape))


def lead(shape):
    return pl.BlockSpec((1,) + shape, lambda z, *_: (z,) + (0,) * len(shape))


def column(tokens, width):
    return pl.BlockSpec((tokens, width), lambda z, *_: (0, z))


def sizes(pieces):
    return pieces[0].shape + (pieces[0].shape[1] * PIECES,)


def times_up(order, x, pieces):
    groups, rows, width, depth = sizes(pieces)
    tokens = x.shape[0]
    shape = (tokens, groups * width)
    return call(
        up_kernel,
        (groups,),
        [still(x.shape)] + [lead((rows, width))] * PIECES,
        [column(tokens, width)] * 2,
        [jax.ShapeDtypeStruct(shape, jnp.float32), jax.ShapeDtypeStruct(shape, jnp.bfloat16)],
        [pltpu.VMEM((depth, width), jnp.bfloat16)],
        2 * tokens * depth * width * groups,
        (order, x) + pieces,
    )


def times_slope(order, x, pre, pieces):
    groups, rows, width, depth = sizes(pieces)
    tokens = x.shape[0]
    return call(
        slope_kernel,
        (groups,),
        [still(x.shape), column(tokens, width)] + [lead((rows, width))] * PIECES,
        column(tokens, width),
        jax.ShapeDtypeStruct(pre.shape, jnp.bfloat16),
        [pltpu.VMEM((depth, width), jnp.bfloat16)],
        2 * tokens * depth * width * groups,
        (order, x, pre) + pieces,
    )


def times_turned(order, x, pieces, low, high):
    groups, rows, width, depth = sizes(pieces)
    tokens = x.shape[0]
    return call(
        functools.partial(turned_kernel, low, high),
        (groups,),
        [still(x.shape)] + [lead((rows, width))] * PIECES,
        lead((high - low, tokens)),
        jax.ShapeDtypeStruct((groups, high - low, tokens), jnp.bfloat16),
        [pltpu.VMEM((depth, width), jnp.bfloat16)],
        2 * tokens * depth * width * groups,
        (order, x) + pieces,
    )


def collect(order, y, pieces, low, high, turned):
    groups, rows, width, depth = sizes(pieces)
    tokens = y.shape[2] if turned else y.shape[0]
    return call(
        functools.partial(collect_kernel, low, high, turned),
        (groups,),
        [lead(y.shape[1:]) if turned else column(tokens, width)]
        + [lead((rows, width))] * PIECES,
        still((tokens, depth)),
        jax.ShapeDtypeStruct((tokens, depth), jnp.float32),
        [pltpu.VMEM((depth, width), jnp.bfloat16)],
        2 * tokens * depth * (high - low) * groups,
        (order, y) + pieces,
    )


def grad_call(kernel, args, specs, groups, depth, width):
    rows = depth // PIECES
    half = PIECES // 2
    tokens = args[1].shape[0]
    return call(
        kernel,
        (groups,),
        specs,
        [pl.BlockSpec((half, 1, rows, width), lambda z, *_: (0, z, 0, 0))] * 2,
        [jax.ShapeDtypeStruct((half, groups, rows, width), jnp.bfloat16)] * 2,
        [pltpu.VMEM((depth, width), jnp.bfloat16)],
        2 * tokens * depth * width * groups,
        args,
    )


def grad_of(order, x, y, groups):
    tokens, width = x.shape[0], y.shape[1] // groups
    specs = [still(x.shape), column(tokens, width)]
    return grad_call(grad_kernel, (order, x, y), specs, groups, x.shape[1], width)


def attn_grad_of(order, x, y, b, a):
    groups, wide, tokens = y.shape
    part = a.shape[1]
    specs = [still(x.shape), lead((wide, tokens)), still(b.shape), lead((part, tokens))]
    args = (order, x, y, b, a)
    return grad_call(attn_grad_kernel, args, specs, groups, x.shape[1], wide + part)


def attend_call(projected, group):
    groups, wide, tokens = projected.shape
    part = wide // 3
    return call(
        functools.partial(attend_kernel, group),
        (groups,),
        [lead((wide, tokens))],
        lead((part, tokens)),
        jax.ShapeDtypeStruct((groups, part, tokens), jnp.bfloat16),
        [],
        4 * tokens * tokens * part * groups,
        (projected,),
    )


def attend_back_call(projected, upstream, group):
    groups, wide, tokens = projected.shape
    part = wide // 3
    return call(
        functools.partial(attend_back_kernel, group),
        (groups,),
        [lead((wide, tokens)), lead((part, tokens))],
        lead((wide, tokens)),
        jax.ShapeDtypeStruct((groups, wide, tokens), jnp.bfloat16),
        [],
        10 * tokens * tokens * part * groups,
        (projected, upstream),
    )


def own_forward(stream, modulation, order, weights, group):
    attn, up, down = weights
    width = attn[0].shape[2]
    part = width // 4
    normed, inv_scale = layer_norm(stream)
    modulated = (normed * (1.0 + modulation[1]) + modulation[0]).astype(jnp.bfloat16)
    projected = times_turned(order, modulated, attn, 0, 3 * part)
    attended = attend_call(projected, group)
    branch_attn = collect(order, attended, attn, 3 * part, width, True)
    middle = stream + modulation[2] * branch_attn
    normed_mlp, inv_mlp = layer_norm(middle)
    modulated_mlp = (normed_mlp * (1.0 + modulation[4]) + modulation[3]).astype(jnp.bfloat16)
    hidden_pre, hidden_act = times_up(order, modulated_mlp, up)
    branch_mlp = collect(order, hidden_act, down, 0, width, False)
    result = middle + modulation[5] * branch_mlp
    stored = (
        normed,
        inv_scale,
        modulated,
        projected,
        attended,
        branch_attn,
        normed_mlp,
        inv_mlp,
        modulated_mlp,
        hidden_pre,
        hidden_act,
        branch_mlp,
    )
    return result, stored


def own_backward(upstream, modulation, order, weights, stored, group):
    attn, up, down = weights
    width = attn[0].shape[2]
    part = width // 4
    groups = attn[0].shape[0]
    (
        normed,
        inv_scale,
        modulated,
        projected,
        attended,
        branch_attn,
        normed_mlp,
        inv_mlp,
        modulated_mlp,
        hidden_pre,
        hidden_act,
        branch_mlp,
    ) = stored
    d_branch_mlp = (upstream * modulation[5]).astype(jnp.bfloat16)
    d_gate_mlp = jnp.sum(upstream * branch_mlp, axis=0)
    grad_down = grad_of(order, d_branch_mlp, hidden_act, groups)
    d_pre = times_slope(order, d_branch_mlp, hidden_pre, down)
    grad_up = grad_of(order, modulated_mlp, d_pre, groups)
    d_mod_mlp = collect(order, d_pre, up, 0, width, False)
    d_shift_mlp = jnp.sum(d_mod_mlp, axis=0)
    d_scale_mlp = jnp.sum(d_mod_mlp * normed_mlp, axis=0)
    d_middle = upstream + norm_back(normed_mlp, inv_mlp, d_mod_mlp * (1.0 + modulation[4]))
    d_branch_attn = (d_middle * modulation[2]).astype(jnp.bfloat16)
    d_gate_attn = jnp.sum(d_middle * branch_attn, axis=0)
    d_attended = times_turned(order, d_branch_attn, attn, 3 * part, width)
    d_projected = attend_back_call(projected, d_attended, group)
    grad_attn = attn_grad_of(order, modulated, d_projected, d_branch_attn, attended)
    d_modulated = collect(order, d_projected, attn, 0, 3 * part, True)
    d_shift_attn = jnp.sum(d_modulated, axis=0)
    d_scale_attn = jnp.sum(d_modulated * normed, axis=0)
    d_stream = d_middle + norm_back(normed, inv_scale, d_modulated * (1.0 + modulation[1]))
    d_modulation = jnp.stack(
        [d_shift_attn, d_scale_attn, d_gate_attn, d_shift_mlp, d_scale_mlp, d_gate_mlp]
    )
    return d_stream, d_modulation, (grad_attn, grad_up, grad_down)


def finish_grads(attn_piece, up_piece, down_piece):
    rows, width = attn_piece.shape
    part = width // 4
    qkv = attn_piece[:, : 3 * part].reshape(rows, 3, part).astype(jnp.float32)
    attn = attn_piece[:, 3 * part :].T.astype(jnp.float32)
    return qkv, attn, up_piece.astype(jnp.float32), down_piece.T.astype(jnp.float32)


def places_out(stream):
    clips, frames, places, width = stream.shape
    devices, tensors = lax.axis_size(FRAME), lax.axis_size(TENSOR)
    part = places // (devices * tensors)
    blocks = stream.reshape(clips, frames, tensors, devices, part, width).transpose(
        0, 1, 3, 2, 4, 5
    )
    return lax.all_to_all(
        blocks.reshape(clips, frames, places, width),
        (FRAME, TENSOR),
        split_axis=2,
        concat_axis=1,
        tiled=True,
    )


def places_back(stream):
    devices, tensors = lax.axis_size(FRAME), lax.axis_size(TENSOR)
    moved = lax.all_to_all(stream, (FRAME, TENSOR), split_axis=1, concat_axis=2, tiled=True)
    clips, frames, places, width = moved.shape
    part = places // (devices * tensors)
    blocks = moved.reshape(clips, frames, devices, tensors, part, width).transpose(
        0, 1, 3, 2, 4, 5
    )
    return blocks.reshape(clips, frames, places, width)


def local_whole(
    x_in,
    cond,
    mod_weight_one,
    qkv_weight_one,
    attn_out_one,
    mlp_up_one,
    mlp_down_one,
    mod_weight_two,
    qkv_weight_two,
    attn_out_two,
    mlp_up_two,
    mlp_down_two,
    out_cotangent,
):
    rows, _, part = qkv_weight_one.shape
    width = x_in.shape[-1]
    packed = [
        pack_layer((qkv_weight_one, attn_out_one, mlp_up_one, mlp_down_one)),
        pack_layer((qkv_weight_two, attn_out_two, mlp_up_two, mlp_down_two)),
    ]
    cond_every = lax.all_gather(cond, CLIP, axis=0, tiled=True).astype(jnp.float32)
    clip_count = cond_every.shape[0]
    silu_every = jax.nn.silu(cond_every).astype(jnp.bfloat16)
    silu_rows = lax.dynamic_slice_in_dim(silu_every, shard_index() * rows, rows, axis=1)
    mod_weights = (mod_weight_one.astype(jnp.bfloat16), mod_weight_two.astype(jnp.bfloat16))
    partial_value = jnp.stack(
        [
            jnp.einsum("cd,dkz->ckz", silu_rows, weight, preferred_element_type=jnp.float32)
            for weight in mod_weights
        ],
        axis=1,
    )
    summed = exchange_sum(exchange_sum(partial_value, FRAME), CLIP)
    summed = lax.dynamic_index_in_dim(summed, lax.axis_index(CLIP), 0, keepdims=False)
    placed = place_along(summed, TENSOR)
    modulations = placed.transpose(1, 2, 0, 3).reshape(summed.shape[:2] + (-1,))

    order = piece_order()
    whole_weights = [[gather_piece(piece) for piece in pieces] for pieces in packed]

    frames_in = lax.all_to_all(x_in, TENSOR, split_axis=1, concat_axis=2, tiled=True)
    cotangent = lax.all_to_all(out_cotangent, FRAME, split_axis=2, concat_axis=1, tiled=True)
    frame_shape, place_shape = frames_in.shape, cotangent.shape
    group = place_shape[2]
    wide = lambda array: array.reshape(-1, width).astype(jnp.float32)
    low = lambda array, shape: array.astype(jnp.bfloat16).reshape(shape)
    middle_stream, stored_first = own_forward(
        wide(frames_in), modulations[0], order, whole_weights[0], 0
    )
    second_in = wide(places_out(low(middle_stream, frame_shape)))
    result, stored_second = own_forward(
        second_in, modulations[1], order, whole_weights[1], group
    )
    layer_out = lax.all_to_all(
        low(result, place_shape), FRAME, split_axis=1, concat_axis=2, tiled=True
    )
    d_second, d_mod_second, grads_second = own_backward(
        wide(cotangent), modulations[1], order, whole_weights[1], stored_second, group
    )
    d_first_out = wide(places_back(low(d_second, place_shape)))
    d_first, d_mod_first, grads_first = own_backward(
        d_first_out, modulations[0], order, whole_weights[0], stored_first, 0
    )
    input_grad = lax.all_to_all(
        low(d_first, frame_shape), TENSOR, split_axis=2, concat_axis=1, tiled=True
    ).astype(jnp.float32)

    second_out = finish_grads(*(scatter_piece(grad) for grad in grads_second))
    first_out = finish_grads(*(scatter_piece(grad) for grad in grads_first))

    d_mods = jnp.stack([d_mod_first, d_mod_second])
    d_mods = exchange_sum(exchange_sum(d_mods, FRAME), TENSOR)
    d_mods = lax.dynamic_slice_in_dim(d_mods, lax.axis_index(TENSOR) * part, part, axis=2)
    d_every = place_along(d_mods, CLIP)
    silu_float = silu_rows.astype(jnp.float32)
    grad_mods = [
        sum(
            silu_float[c][:, None, None] * d_every[c, layer][None] for c in range(clip_count)
        )
        for layer in range(2)
    ]
    d_silu = jnp.stack(
        [
            sum(
                jnp.sum(
                    d_every[c, layer][None] * mod_weights[layer].astype(jnp.float32), axis=(1, 2)
                )
                for layer in range(2)
            )
            for c in range(clip_count)
        ]
    )
    d_silu = place_along(place_along(exchange_sum(d_silu, TENSOR), FRAME), CLIP)
    d_silu = d_silu.transpose(2, 0, 1, 3).reshape(clip_count, -1)
    d_silu = lax.dynamic_slice_in_dim(d_silu, lax.axis_index(CLIP), 1, axis=0)
    cond_float = cond.astype(jnp.float32)
    sigmoid_cond = jax.nn.sigmoid(cond_float)
    cond_grad = d_silu * (sigmoid_cond * (1.0 + cond_float * (1.0 - sigmoid_cond)))
    return (
        layer_out,
        input_grad,
        cond_grad,
        grad_mods[0],
        *first_out,
        grad_mods[1],
        *second_out,
    )


def holds_whole(mesh):
    tensors = mesh.shape[TENSOR]
    return (
        mesh.shape[CLIP] == 2
        and mesh.shape[FRAME] == 4
        and FRAMES % (4 * tensors) == 0
        and tensors & (tensors - 1) == 0
    )


def solution(mesh):
    return jax.shard_map(
        local_whole if holds_whole(mesh) else local,
        mesh=mesh,
        in_specs=(
            P(CLIP, FRAME, TENSOR, None),
            P(CLIP, None),
            P(SHARDS, None, TENSOR),
            P(SHARDS, None, TENSOR),
            P(TENSOR, SHARDS),
            P(SHARDS, TENSOR),
            P(TENSOR, SHARDS),
            P(SHARDS, None, TENSOR),
            P(SHARDS, None, TENSOR),
            P(TENSOR, SHARDS),
            P(SHARDS, TENSOR),
            P(TENSOR, SHARDS),
            P(CLIP, FRAME, TENSOR, None),
        ),
        out_specs=(
            P(CLIP, FRAME, TENSOR, None),
            P(CLIP, FRAME, TENSOR, None),
            P(CLIP, None),
            P(SHARDS, None, TENSOR),
            P(SHARDS, None, TENSOR),
            P(TENSOR, SHARDS),
            P(SHARDS, TENSOR),
            P(TENSOR, SHARDS),
            P(SHARDS, None, TENSOR),
            P(SHARDS, None, TENSOR),
            P(TENSOR, SHARDS),
            P(SHARDS, TENSOR),
            P(TENSOR, SHARDS),
        ),
        check_vma=False,
    )
```

```python
import functools

import jax
import jax.numpy as jnp
from jax import lax
from jax.experimental import pallas as pl
from jax.experimental.pallas import tpu as pltpu
from jax.sharding import PartitionSpec as P

HD = 72
FRAMES = 16
CLIP, FRAME, TENSOR = "clip", "frame", "tensor"
SHARDS = (CLIP, FRAME)


HIGHEST_PRECISION = lax.Precision.HIGHEST
SCORE_FORMS = {True: "cfphe,cfqhe->cfhpq", False: "cfphe,cgphe->cphfg"}
APPLY_FORMS = {True: "cfhpq,cfqhe->cfphe", False: "cphfg,cgphe->cfphe"}
BACK_FORMS = {True: "cfhpq,cfphe->cfqhe", False: "cphfg,cfphe->cgphe"}
GELU_COEFF = 0.7978845608028654
CUBIC_COEFF = 0.044715


def layer_norm(stream):
    centre = stream - jnp.mean(stream, axis=-1, keepdims=True)
    inv_scale = lax.rsqrt(jnp.mean(centre * centre, axis=-1, keepdims=True) + 1e-06)
    return (centre * inv_scale, inv_scale)


def norm_back(normed, inv_scale, upstream):
    return inv_scale * (
        upstream
        - jnp.mean(upstream, axis=-1, keepdims=True)
        - normed * jnp.mean(upstream * normed, axis=-1, keepdims=True)
    )


def gelu_tanh(inputs):
    return (
        0.5
        * inputs
        * (1.0 + jnp.tanh(GELU_COEFF * (inputs + CUBIC_COEFF * inputs * inputs * inputs)))
    )


def gelu_slope(inputs):
    tangent = jnp.tanh(GELU_COEFF * (inputs + CUBIC_COEFF * inputs * inputs * inputs))
    return 0.5 * (1.0 + tangent) + 0.5 * inputs * (1.0 - tangent * tangent) * GELU_COEFF * (
        1.0 + 3.0 * CUBIC_COEFF * inputs * inputs
    )


def choose(modulation, column):
    return modulation[:, column][:, None, None, :]


def split_heads(projected):
    leading = projected.shape[:3]
    row_width = projected.shape[-1]
    head_count = row_width // HD
    queries = projected[:, :, :, 0].reshape(leading + (head_count, HD))
    key_rows = projected[:, :, :, 1].reshape(leading + (head_count, HD))
    values = projected[:, :, :, 2].reshape(leading + (head_count, HD))
    return (queries, key_rows, values, leading, row_width)


def attend(projected, spatial):
    queries, key_rows, values, leading, row_width = split_heads(projected)
    scores = jnp.einsum(
        SCORE_FORMS[spatial], queries, key_rows, preferred_element_type=jnp.float32
    ) * HD ** (-0.5)
    highest = jnp.max(scores, axis=-1, keepdims=True)
    expo = jnp.exp(scores - highest)
    denominator = jnp.sum(expo, axis=-1, keepdims=True)
    probs = (expo / denominator).astype(jnp.bfloat16)
    log_total = highest + jnp.log(denominator)
    attended = jnp.einsum(APPLY_FORMS[spatial], probs, values, preferred_element_type=jnp.float32)
    return (attended.reshape(leading + (row_width,)).astype(jnp.bfloat16), log_total)


def attend_back(projected, log_total, d_attended, spatial):
    queries, key_rows, values, leading, row_width = split_heads(projected)
    scale_factor = HD ** (-0.5)
    scores = (
        jnp.einsum(SCORE_FORMS[spatial], queries, key_rows, preferred_element_type=jnp.float32)
        * scale_factor
    )
    probs = jnp.exp(scores - log_total)
    upstream = d_attended.reshape(leading + (row_width // HD, HD))
    d_probs = jnp.einsum(SCORE_FORMS[spatial], upstream, values, preferred_element_type=jnp.float32)
    d_values = jnp.einsum(
        BACK_FORMS[spatial],
        probs.astype(jnp.bfloat16),
        upstream,
        preferred_element_type=jnp.float32,
    )
    row_inner = jnp.sum(probs * d_probs, axis=-1, keepdims=True)
    d_scores = (probs * (d_probs - row_inner)).astype(jnp.bfloat16)
    d_queries = (
        jnp.einsum(APPLY_FORMS[spatial], d_scores, key_rows, preferred_element_type=jnp.float32)
        * scale_factor
    )
    d_keys = (
        jnp.einsum(BACK_FORMS[spatial], d_scores, queries, preferred_element_type=jnp.float32)
        * scale_factor
    )
    stacked = jnp.stack([d_queries, d_keys, d_values], axis=3)
    return stacked.reshape(leading + (3, row_width)).astype(jnp.bfloat16)


def fetch_weights(weights):
    cast = tuple((weight.astype(jnp.bfloat16) for weight in weights))
    return (
        lax.all_gather(cast[0], SHARDS, axis=0, tiled=True),
        lax.all_gather(cast[1], SHARDS, axis=0, tiled=True),
        lax.all_gather(cast[2], SHARDS, axis=1, tiled=True),
        lax.all_gather(cast[3], SHARDS, axis=0, tiled=True),
        lax.all_gather(cast[4], SHARDS, axis=1, tiled=True),
    )


def backward_weights(weights):
    cast = tuple((weight.astype(jnp.bfloat16) for weight in weights))
    return (
        lax.all_gather(cast[0], SHARDS, axis=0, tiled=True),
        lax.all_gather(cast[1], SHARDS, axis=0, tiled=True),
        lax.all_gather(cast[2], SHARDS, axis=1, tiled=True),
        lax.all_gather(cast[3], SHARDS, axis=0, tiled=True),
        lax.all_gather(cast[4], SHARDS, axis=1, tiled=True),
    )


def spread_rows(rows):
    return lax.all_gather(rows, TENSOR, axis=2, tiled=True)


def collect_rows(term):
    return lax.psum_scatter(term, TENSOR, scatter_dimension=2, tiled=True)


def attention_output(attended, attn_weight):
    return collect_rows(
        jnp.einsum("cfpz,zd->cfpd", attended, attn_weight, preferred_element_type=jnp.float32)
    )


def layer_forward(stream, silu_cond, gathered, spatial):
    mod_weight, qkv_weight, attn_weight, up_weight, down_weight = gathered
    partial_value = jnp.einsum(
        "cd,dkz->ckz", silu_cond, mod_weight, preferred_element_type=jnp.float32
    )
    modulation = lax.all_gather(partial_value, TENSOR, axis=2, tiled=True)
    normed, inv_scale = layer_norm(stream)
    modulated = (normed * (1.0 + choose(modulation, 1)) + choose(modulation, 0)).astype(
        jnp.bfloat16
    )
    gathered_rows = spread_rows(modulated)
    projected = jnp.einsum(
        "cfpd,dkz->cfpkz", gathered_rows, qkv_weight, preferred_element_type=jnp.float32
    ).astype(jnp.bfloat16)
    if spatial:
        project_held = projected
        attended, log_total = attend(project_held, True)
    else:
        project_held = lax.all_to_all(projected, FRAME, split_axis=2, concat_axis=1, tiled=True)
        placed, log_total = attend(project_held, False)
        attended = lax.all_to_all(placed, FRAME, split_axis=1, concat_axis=2, tiled=True)
    branch_attn = attention_output(attended, attn_weight)
    middle = stream + choose(modulation, 2) * branch_attn
    normed_mlp, inv_mlp = layer_norm(middle)
    modulated_mlp = (normed_mlp * (1.0 + choose(modulation, 4)) + choose(modulation, 3)).astype(
        jnp.bfloat16
    )
    gathered_mlp = spread_rows(modulated_mlp)
    hidden_pre = jnp.einsum(
        "cfpd,dz->cfpz", gathered_mlp, up_weight, preferred_element_type=jnp.float32
    )
    hidden_act = gelu_tanh(hidden_pre).astype(jnp.bfloat16)
    branch_mlp = collect_rows(
        jnp.einsum("cfpz,zd->cfpd", hidden_act, down_weight, preferred_element_type=jnp.float32)
    )
    result = middle + choose(modulation, 5) * branch_mlp
    stored = (
        modulation,
        normed,
        inv_scale,
        gathered_rows,
        project_held,
        log_total,
        attended,
        branch_attn,
        normed_mlp,
        inv_mlp,
        gathered_mlp,
        hidden_pre,
        hidden_act,
        branch_mlp,
    )
    return (result, stored)


def layer_backward(upstream, silu_cond, gathered, stored, spatial):
    mod_weight, qkv_weight, attn_weight, up_weight, down_weight = gathered
    (
        modulation,
        normed,
        inv_scale,
        gathered_rows,
        project_held,
        log_total,
        attended,
        branch_attn,
        normed_mlp,
        inv_mlp,
        gathered_mlp,
        hidden_pre,
        hidden_act,
        branch_mlp,
    ) = stored
    d_branch_mlp = (upstream * choose(modulation, 5)).astype(jnp.bfloat16)
    d_gate_mlp = jnp.sum(upstream * branch_mlp, axis=(1, 2))
    d_branch_all = spread_rows(d_branch_mlp)
    grad_down = jnp.einsum(
        "cfpz,cfpd->zd", hidden_act, d_branch_all, preferred_element_type=jnp.float32
    )
    d_act = jnp.einsum(
        "cfpd,zd->cfpz", d_branch_all, down_weight, preferred_element_type=jnp.float32
    )
    d_pre = (d_act * gelu_slope(hidden_pre)).astype(jnp.bfloat16)
    grad_up = jnp.einsum("cfpd,cfpz->dz", gathered_mlp, d_pre, preferred_element_type=jnp.float32)
    d_mod_mlp = collect_rows(
        jnp.einsum("cfpz,dz->cfpd", d_pre, up_weight, preferred_element_type=jnp.float32)
    )
    d_shift_mlp = jnp.sum(d_mod_mlp, axis=(1, 2))
    d_scale_mlp = jnp.sum(d_mod_mlp * normed_mlp, axis=(1, 2))
    d_middle = upstream + norm_back(normed_mlp, inv_mlp, d_mod_mlp * (1.0 + choose(modulation, 4)))
    d_branch_attn = (d_middle * choose(modulation, 2)).astype(jnp.bfloat16)
    d_gate_attn = jnp.sum(d_middle * branch_attn, axis=(1, 2))
    d_attn_all = spread_rows(d_branch_attn)
    grad_attn = jnp.einsum(
        "cfpz,cfpd->zd", attended, d_attn_all, preferred_element_type=jnp.float32
    )
    d_attended = jnp.einsum(
        "cfpd,zd->cfpz", d_attn_all, attn_weight, preferred_element_type=jnp.float32
    ).astype(jnp.bfloat16)
    if spatial:
        d_projected = attend_back(project_held, log_total, d_attended, True)
    else:
        d_placed = lax.all_to_all(d_attended, FRAME, split_axis=2, concat_axis=1, tiled=True)
        d_projected = lax.all_to_all(
            attend_back(project_held, log_total, d_placed, False),
            FRAME,
            split_axis=1,
            concat_axis=2,
            tiled=True,
        )
    grad_qkv = jnp.einsum(
        "cfpd,cfpkz->dkz", gathered_rows, d_projected, preferred_element_type=jnp.float32
    )
    d_modulated = collect_rows(
        jnp.einsum("cfpkz,dkz->cfpd", d_projected, qkv_weight, preferred_element_type=jnp.float32)
    )
    d_shift_attn = jnp.sum(d_modulated, axis=(1, 2))
    d_scale_attn = jnp.sum(d_modulated * normed, axis=(1, 2))
    d_stream = d_middle + norm_back(normed, inv_scale, d_modulated * (1.0 + choose(modulation, 1)))
    d_modulation = jnp.stack(
        [d_shift_attn, d_scale_attn, d_gate_attn, d_shift_mlp, d_scale_mlp, d_gate_mlp], axis=1
    )
    d_mod_own = lax.psum_scatter(d_modulation, TENSOR, scatter_dimension=2, tiled=True)
    grad_mod = jnp.einsum(
        "cd,ckz->dkz", silu_cond.astype(jnp.float32), d_mod_own, precision=HIGHEST_PRECISION
    )
    d_silu = jnp.einsum(
        "ckz,dkz->cd", d_mod_own, mod_weight.astype(jnp.float32), precision=HIGHEST_PRECISION
    )
    grads = (
        lax.psum_scatter(
            grad_mod.astype(jnp.bfloat16), SHARDS, scatter_dimension=0, tiled=True
        ).astype(jnp.float32),
        lax.psum_scatter(
            grad_qkv.astype(jnp.bfloat16), SHARDS, scatter_dimension=0, tiled=True
        ).astype(jnp.float32),
        lax.psum_scatter(
            grad_attn.astype(jnp.bfloat16), SHARDS, scatter_dimension=1, tiled=True
        ).astype(jnp.float32),
        lax.psum_scatter(
            grad_up.astype(jnp.bfloat16), SHARDS, scatter_dimension=0, tiled=True
        ).astype(jnp.float32),
        lax.psum_scatter(
            grad_down.astype(jnp.bfloat16), SHARDS, scatter_dimension=1, tiled=True
        ).astype(jnp.float32),
    )
    return (d_stream, d_silu, grads)


def local(
    x_in,
    cond,
    mod_weight_one,
    qkv_weight_one,
    attn_out_one,
    mlp_up_one,
    mlp_down_one,
    mod_weight_two,
    qkv_weight_two,
    attn_out_two,
    mlp_up_two,
    mlp_down_two,
    out_cotangent,
):
    weights_first = (mod_weight_one, qkv_weight_one, attn_out_one, mlp_up_one, mlp_down_one)
    weights_second = (mod_weight_two, qkv_weight_two, attn_out_two, mlp_up_two, mlp_down_two)
    cond_float = cond.astype(jnp.float32)
    silu_cond = jax.nn.silu(cond_float).astype(jnp.bfloat16)
    gathered_first = fetch_weights(weights_first)
    middle_stream, stored_first = layer_forward(
        x_in.astype(jnp.float32), silu_cond, gathered_first, True
    )
    gathered_second = fetch_weights(weights_second)
    result, stored_second = layer_forward(middle_stream, silu_cond, gathered_second, False)
    back_second = backward_weights(weights_second)
    d_middle_stream, d_silu_second, grads_second = layer_backward(
        out_cotangent.astype(jnp.float32), silu_cond, back_second, stored_second, False
    )
    back_first = backward_weights(weights_first)
    input_grad, d_silu_first, grads_first = layer_backward(
        d_middle_stream, silu_cond, back_first, stored_first, True
    )
    d_silu_total = lax.psum(d_silu_first + d_silu_second, (FRAME, TENSOR))
    sigmoid_cond = jax.nn.sigmoid(cond_float)
    cond_grad = d_silu_total * (sigmoid_cond * (1.0 + cond_float * (1.0 - sigmoid_cond)))
    return (
        result.astype(jnp.bfloat16),
        input_grad,
        cond_grad,
        grads_first[0],
        grads_first[1],
        grads_first[2],
        grads_first[3],
        grads_first[4],
        grads_second[0],
        grads_second[1],
        grads_second[2],
        grads_second[3],
        grads_second[4],
    )

def flip(array, axis, bit):
    count = lax.axis_size(axis)
    return lax.ppermute(array, axis, [(i, i ^ bit) for i in range(count)])


def first_flip(shard):
    return 2 if shard % 2 == 0 else 4


def hop(array, which):
    if which == 0:
        pairs = [(i, i ^ 1) for i in range(8)]
    elif which == 1:
        pairs = [(i, i ^ first_flip(i)) for i in range(8)]
    else:
        pairs = [(i, i ^ (6 - first_flip(i))) for i in range(8)]
    return lax.ppermute(array, SHARDS, pairs)


class Line:
    def __init__(self):
        self.last = ()
        self.awaited = []
        self.under_way = []

    def held(self, value):
        return lax.optimization_barrier((value, self.last, self.awaited))[0]

    def __call__(self, work, *inputs):
        self.last = work(*self.held(inputs))
        self.awaited = []
        return self.last

    def wait(self, value):
        self.awaited.append(value)
        return value

    def send(self, array, move):
        self.under_way.append(move(self.held(array)))
        return self.under_way[-1]

    def hop(self, array, which):
        return self.send(array, lambda held: hop(held, which))

    def exchange_sum(self, array, axis):
        bit = 1
        while bit < lax.axis_size(axis):
            array = self(jnp.add, array, flip(array, axis, bit))
            bit *= 2
        return array

    def place_along(self, array, axis):
        count = lax.axis_size(axis)
        own = (jnp.arange(count) == lax.axis_index(axis)).reshape((count,) + (1,) * array.ndim)
        return self.exchange_sum(jnp.where(own, array[None], 0.0), axis)

    def tick(self):
        self.awaited += self.under_way
        self.under_way = []


def shard_index():
    return lax.axis_index(CLIP) * lax.axis_size(FRAME) + lax.axis_index(FRAME)


def piece_order():
    shard = shard_index()
    first = jnp.where(shard % 2 == 0, 2, 4)
    second = 6 - first
    masks = [0, first, second, 6, 1, 1 ^ second, 1 ^ first, 7]
    return jnp.stack([shard ^ mask for mask in masks]).astype(jnp.int32)


class Gather:
    def __init__(self, line, piece):
        self.line = line
        self.whole = lax.all_gather(piece, TENSOR, axis=0, tiled=False)

    def soon(self):
        self.line.under_way.append(self.whole)

    def send(self):
        self.line.wait(self.whole)
        self.near = self.line.hop(self.whole, 1)

    def relay(self):
        self.pair = self.line(lambda *pair: jnp.stack(pair), self.whole, self.near)
        self.far = self.line.hop(self.pair, 2)
        self.other_pair = self.line.hop(self.pair, 0)

    def end(self):
        other_far = self.line.hop(self.far, 0)
        self.pieces = (self.pair, self.far, self.other_pair, other_far)


def wide(array):
    return array.astype(jnp.float32)


def low(array):
    return array.astype(jnp.bfloat16)


def total(*arrays):
    return low(sum(wide(array) for array in arrays))


class Scatter:
    def __init__(self, line, grad):
        self.line = line
        self.keep, self.away = grad

    def send(self):
        self.far = self.line.hop(self.away, 2)

    def relay(self):
        work = lambda keep, far: total(keep[1], far[1])
        self.near = self.line.hop(self.line(work, self.keep, self.far), 1)

    def finish(self):
        work = lambda keep, far, near: total(keep[0], far[0], near)
        own = self.line(work, self.keep, self.far, self.near)
        self.piece = lax.psum_scatter(own, TENSOR, scatter_dimension=0, tiled=False)


def pack_layer(weights):
    qkv, attn, up, down = (weight.astype(jnp.bfloat16) for weight in weights)
    rows = qkv.shape[0]
    attn_part = jnp.concatenate([qkv.reshape(rows, -1), attn.T], axis=1)
    return attn_part, up, down.T


PIECES = 8
PAIRS = 4
VMEM_BYTES = 48 << 20
COST_SHARE = 8


def contract(left, right, left_dim, right_dim):
    return lax.dot_general(
        left, right, (((left_dim,), (right_dim,)), ((), ())), preferred_element_type=jnp.float32
    )


def assemble(order_ref, piece_refs, whole_ref):
    rows = piece_refs[0].shape[2]
    for j in range(PIECES):
        start = pl.multiple_of(order_ref[j] * rows, 16)
        whole_ref[pl.ds(start, rows), :] = piece_refs[j // 2][j % 2, 0]


def up_kernel(order_ref, x_ref, *refs):
    pre_ref, act_ref, whole_ref = refs[PAIRS:]
    assemble(order_ref, refs[:PAIRS], whole_ref)
    pre = contract(x_ref[...], whole_ref[...], 1, 0)
    pre_ref[...] = pre
    act_ref[...] = gelu_tanh(pre).astype(jnp.bfloat16)


def slope_kernel(order_ref, x_ref, pre_ref, *refs):
    out_ref, whole_ref = refs[PAIRS:]
    assemble(order_ref, refs[:PAIRS], whole_ref)
    d_act = contract(x_ref[...], whole_ref[...], 1, 0)
    out_ref[...] = (d_act * gelu_slope(pre_ref[...])).astype(jnp.bfloat16)


def turned_kernel(low, high, order_ref, x_ref, *refs):
    out_ref, whole_ref = refs[PAIRS:]
    assemble(order_ref, refs[:PAIRS], whole_ref)
    whole = contract(x_ref[...], whole_ref[...], 1, 0)
    out_ref[0] = whole[:, low:high].astype(jnp.bfloat16).T


def collect_kernel(low, high, turned, order_ref, y_ref, *refs):
    out_ref, whole_ref = refs[PAIRS:]
    assemble(order_ref, refs[:PAIRS], whole_ref)
    rows = y_ref[0].T if turned else y_ref[...]
    term = contract(rows, whole_ref[:, low:high], 1, 1)

    @pl.when(pl.program_id(0) == 0)
    def _():
        out_ref[...] = term

    @pl.when(pl.program_id(0) > 0)
    def _():
        out_ref[...] += term


def turn(order_ref, x_refs, whole_ref, turned_ref):
    rows, tokens = turned_ref.shape[0] * 2 // PIECES, turned_ref.shape[1] // 2
    for side in range(2):
        whole_ref[...] = x_refs[side][...].T
        for j in range(PIECES // 2):
            start = pl.multiple_of(order_ref[j] * rows, 16)
            turned_ref[pl.ds(j * rows, rows), pl.ds(side * tokens, tokens)] = whole_ref[
                pl.ds(start, rows), :
            ]


def deal_out(grad, *out_refs):
    rows = out_refs[0].shape[2]
    for j in range(PIECES // 2):
        out_refs[j // 2][j % 2, 0] = grad[j * rows : (j + 1) * rows]


def grad_kernel(order_ref, x_ref, x_other, y_ref, y_other, *refs):
    whole_ref, turned_ref = refs[2:]

    @pl.when(pl.program_id(0) == 0)
    def _():
        turn(order_ref, (x_ref, x_other), whole_ref, turned_ref)

    tokens = x_ref.shape[0]
    grad = contract(turned_ref[:, :tokens], y_ref[...], 1, 0)
    grad += contract(turned_ref[:, tokens:], y_other[...], 1, 0)
    deal_out(grad.astype(jnp.bfloat16), *refs[:2])


def attn_grad_kernel(order_ref, *refs):
    x_refs, b_refs, y_refs, a_refs = (refs[2 * j : 2 * j + 2] for j in range(4))
    out_refs, (whole_ref, x_turned, b_turned, grad_ref) = refs[8:10], refs[10:]

    @pl.when(pl.program_id(0) == 0)
    def _():
        turn(order_ref, x_refs, whole_ref, x_turned)
        turn(order_ref, b_refs, whole_ref, b_turned)

    tokens, split = y_refs[0].shape[2], y_refs[0].shape[1]
    for turned, pair, lanes in (
        (x_turned, y_refs, slice(0, split)),
        (b_turned, a_refs, slice(split, grad_ref.shape[1])),
    ):
        grad = contract(turned[:, :tokens], pair[0][0], 1, 1)
        grad += contract(turned[:, tokens:], pair[1][0], 1, 1)
        grad_ref[:, lanes] = grad.astype(jnp.bfloat16)
    deal_out(grad_ref[...], *out_refs)


def masked_scores(queries, keys, group):
    scores = contract(queries, keys, 0, 0) * HD ** (-0.5)
    if group:
        place = lax.broadcasted_iota(jnp.int32, scores.shape, 0) % group
        other = lax.broadcasted_iota(jnp.int32, scores.shape, 1) % group
        scores = jnp.where(place == other, scores, -3e38)
    expo = jnp.exp(scores - jnp.max(scores, axis=-1, keepdims=True))
    return expo / jnp.sum(expo, axis=-1, keepdims=True)


def attend_kernel(group, projected_ref, out_ref):
    part = out_ref.shape[1]
    for start in range(0, part, HD):
        queries, keys, values = (
            projected_ref[0, pl.ds(j * part + start, HD), :] for j in range(3)
        )
        probs = masked_scores(queries, keys, group).astype(jnp.bfloat16)
        out_ref[0, pl.ds(start, HD), :] = contract(values, probs, 1, 1).astype(jnp.bfloat16)


def attend_back_kernel(group, projected_ref, upstream_ref, out_ref):
    part = upstream_ref.shape[1]
    scale_factor = HD ** (-0.5)
    for start in range(0, part, HD):
        queries, keys, values = (
            projected_ref[0, pl.ds(j * part + start, HD), :] for j in range(3)
        )
        upstream = upstream_ref[0, pl.ds(start, HD), :]
        probs = masked_scores(queries, keys, group)
        d_probs = contract(upstream, values, 0, 0)
        row_inner = jnp.sum(probs * d_probs, axis=-1, keepdims=True)
        d_scores = (probs * (d_probs - row_inner)).astype(jnp.bfloat16)
        grads = (
            contract(keys, d_scores, 1, 1) * scale_factor,
            contract(queries, d_scores, 1, 0) * scale_factor,
            contract(upstream, probs.astype(jnp.bfloat16), 1, 0),
        )
        for j in range(3):
            out_ref[0, pl.ds(j * part + start, HD), :] = grads[j].astype(jnp.bfloat16)


def call(kernel, grid, in_specs, out_specs, out_shape, scratch, flops, args):
    moved = sum(a.size * a.dtype.itemsize for a in args)
    moved += sum(o.size * o.dtype.itemsize for o in jax.tree.leaves(out_shape))
    return pl.pallas_call(
        kernel,
        out_shape=out_shape,
        grid_spec=pltpu.PrefetchScalarGridSpec(
            num_scalar_prefetch=1 if scratch else 0,
            grid=grid,
            in_specs=in_specs,
            out_specs=out_specs,
            scratch_shapes=scratch,
        ),
        compiler_params=pltpu.CompilerParams(vmem_limit_bytes=VMEM_BYTES),
        cost_estimate=pl.CostEstimate(
            flops=flops // COST_SHARE, bytes_accessed=moved // COST_SHARE, transcendentals=0
        ),
    )(*args)


def still(shape):
    return pl.BlockSpec(shape, lambda z, *_: (0,) * len(shape))


def lead(shape):
    return pl.BlockSpec((1,) + shape, lambda z, *_: (z,) + (0,) * len(shape))


def column(tokens, width):
    return pl.BlockSpec((tokens, width), lambda z, *_: (0, z))


def sizes(pieces):
    _, groups, rows, width = pieces[0].shape
    return groups, rows, width, rows * PIECES


def pair_specs(rows, width, count):
    return [pl.BlockSpec((2, 1, rows, width), lambda z, *_: (0, z, 0, 0))] * count


def times_up(order, x, pieces):
    groups, rows, width, depth = sizes(pieces)
    tokens = x.shape[0]
    shape = (tokens, groups * width)
    return call(
        up_kernel,
        (groups,),
        [still(x.shape)] + pair_specs(rows, width, PAIRS),
        [column(tokens, width)] * 2,
        [jax.ShapeDtypeStruct(shape, jnp.float32), jax.ShapeDtypeStruct(shape, jnp.bfloat16)],
        [pltpu.VMEM((depth, width), jnp.bfloat16)],
        2 * tokens * depth * width * groups,
        (order, x) + pieces,
    )


def times_slope(order, x, pre, pieces):
    groups, rows, width, depth = sizes(pieces)
    tokens = x.shape[0]
    return call(
        slope_kernel,
        (groups,),
        [still(x.shape), column(tokens, width)] + pair_specs(rows, width, PAIRS),
        column(tokens, width),
        jax.ShapeDtypeStruct(pre.shape, jnp.bfloat16),
        [pltpu.VMEM((depth, width), jnp.bfloat16)],
        2 * tokens * depth * width * groups,
        (order, x, pre) + pieces,
    )


def times_turned(order, x, pieces, low, high):
    groups, rows, width, depth = sizes(pieces)
    tokens = x.shape[0]
    return call(
        functools.partial(turned_kernel, low, high),
        (groups,),
        [still(x.shape)] + pair_specs(rows, width, PAIRS),
        lead((high - low, tokens)),
        jax.ShapeDtypeStruct((groups, high - low, tokens), jnp.bfloat16),
        [pltpu.VMEM((depth, width), jnp.bfloat16)],
        2 * tokens * depth * width * groups,
        (order, x) + pieces,
    )


def collect(order, y, pieces, low, high, turned):
    groups, rows, width, depth = sizes(pieces)
    tokens = y.shape[2] if turned else y.shape[0]
    return call(
        functools.partial(collect_kernel, low, high, turned),
        (groups,),
        [lead(y.shape[1:]) if turned else column(tokens, width)]
        + pair_specs(rows, width, PAIRS),
        still((tokens, depth)),
        jax.ShapeDtypeStruct((tokens, depth), jnp.float32),
        [pltpu.VMEM((depth, width), jnp.bfloat16)],
        2 * tokens * depth * (high - low) * groups,
        (order, y) + pieces,
    )


def grad_call(kernel, args, specs, groups, depth, width, scratch):
    rows = depth // PIECES
    tokens = args[1].shape[0]
    return call(
        kernel,
        (groups,),
        specs,
        pair_specs(rows, width, 2),
        [jax.ShapeDtypeStruct((2, groups, rows, width), jnp.bfloat16)] * 2,
        [pltpu.VMEM((depth, tokens), jnp.bfloat16)]
        + [pltpu.VMEM(shape, jnp.bfloat16) for shape in scratch],
        2 * tokens * depth * width * groups,
        args,
    )


def grad_of(order, x, x_other, y, y_other, groups):
    tokens, width = x.shape[0], y.shape[1] // groups
    depth = x.shape[1]
    specs = [still(x.shape)] * 2 + [column(tokens, width)] * 2
    args = (order, x, x_other, y, y_other)
    scratch = [(depth // 2, 2 * tokens)]
    return grad_call(grad_kernel, args, specs, groups, depth, width, scratch)


def attn_grad_of(order, *args):
    x, y, a = args[0], args[4], args[6]
    groups, wide_part, tokens = y.shape
    part, depth = a.shape[1], x.shape[1]
    specs = [still(x.shape)] * 4 + [lead((wide_part, tokens))] * 2 + [lead((part, tokens))] * 2
    scratch = [(depth // 2, 2 * tokens)] * 2 + [(depth // 2, wide_part + part)]
    return grad_call(
        attn_grad_kernel, (order, *args), specs, groups, depth, wide_part + part, scratch
    )


def attend_call(projected, group):
    groups, wide, tokens = projected.shape
    part = wide // 3
    return call(
        functools.partial(attend_kernel, group),
        (groups,),
        [lead((wide, tokens))],
        lead((part, tokens)),
        jax.ShapeDtypeStruct((groups, part, tokens), jnp.bfloat16),
        [],
        4 * tokens * tokens * part * groups,
        (projected,),
    )


def attend_back_call(projected, upstream, group):
    groups, wide, tokens = projected.shape
    part = wide // 3
    return call(
        functools.partial(attend_back_kernel, group),
        (groups,),
        [lead((wide, tokens)), lead((part, tokens))],
        lead((wide, tokens)),
        jax.ShapeDtypeStruct((groups, wide, tokens), jnp.bfloat16),
        [],
        10 * tokens * tokens * part * groups,
        (projected, upstream),
    )


class Layer:
    def __init__(self, line, order, modulation, group):
        self.line = line
        self.order = order
        self.modulation = modulation
        self.group = group
        self.others = {}

    def share(self, *arrays):
        for array in arrays:
            self.others[id(array)] = self.line.hop(array, 0)

    def both(self, array):
        return array, self.others[id(array)]

    def project(self, stream, attn):
        self.stream = stream
        self.attn = attn
        self.width = attn[0].shape[-1]
        self.part = self.width // 4
        rows = self.modulation

        def work(stream, attn):
            normed, inv_scale = layer_norm(stream)
            modulated = low(normed * (1.0 + rows[1]) + rows[0])
            projected = times_turned(self.order, modulated, attn, 0, 3 * self.part)
            return normed, inv_scale, modulated, projected

        made = self.line(work, stream, attn)
        self.normed, self.inv_scale, self.modulated, self.projected = made

    def attend(self):
        self.attended = self.line(
            lambda projected: attend_call(projected, self.group), self.projected
        )

    def attention_out(self):
        rows = self.modulation

        def work(attended, stream, attn):
            branch_attn = collect(self.order, attended, attn, 3 * self.part, self.width, True)
            middle = stream + rows[2] * branch_attn
            normed_mlp, inv_mlp = layer_norm(middle)
            modulated_mlp = low(normed_mlp * (1.0 + rows[4]) + rows[3])
            return branch_attn, middle, normed_mlp, inv_mlp, modulated_mlp

        made = self.line(work, self.attended, self.stream, self.attn)
        self.branch_attn, self.middle, self.normed_mlp, self.inv_mlp, self.modulated_mlp = made

    def mlp_up(self, up):
        self.up = up
        work = lambda rows, up: times_up(self.order, rows, up)
        self.hidden_pre, self.hidden_act = self.line(work, self.modulated_mlp, up)

    def mlp_down(self, down, last):
        rows = self.modulation

        def work(act, middle, down):
            branch_mlp = collect(self.order, act, down, 0, self.width, False)
            return branch_mlp, last(middle + rows[5] * branch_mlp)

        self.branch_mlp, result = self.line(work, self.hidden_act, self.middle, down)
        return result

    def turn_back(self, upstream):
        rows = self.modulation
        self.upstream = upstream
        self.d_branch_mlp = self.line(lambda rows_in: low(rows_in * rows[5]), upstream)

    def gradient(self, *args):
        groups = self.attn[0].shape[1]
        work = lambda *rows: grad_of(self.order, *rows, groups)
        return Scatter(self.line, self.line(work, *args))

    def grad_down(self):
        return self.gradient(*self.both(self.d_branch_mlp), *self.both(self.hidden_act))

    def slope(self, down):
        work = lambda rows, pre, down: times_slope(self.order, rows, pre, down)
        self.d_pre = self.line(work, self.d_branch_mlp, self.hidden_pre, down)

    def grad_up(self):
        return self.gradient(*self.both(self.modulated_mlp), *self.both(self.d_pre))

    def back_up(self):
        rows = self.modulation

        def work(d_pre, upstream, normed, inv_mlp, up):
            d_mod_mlp = collect(self.order, d_pre, up, 0, self.width, False)
            d_middle = upstream + norm_back(normed, inv_mlp, d_mod_mlp * (1.0 + rows[4]))
            return d_mod_mlp, d_middle, low(d_middle * rows[2])

        made = self.line(
            work, self.d_pre, self.upstream, self.normed_mlp, self.inv_mlp, self.up
        )
        self.d_mod_mlp, self.d_middle, self.d_branch_attn = made

    def back_out(self):
        work = lambda rows, attn: times_turned(
            self.order, rows, attn, 3 * self.part, self.width
        )
        self.d_attended = self.line(work, self.d_branch_attn, self.attn)

    def back_attend(self):
        work = lambda projected, upstream: attend_back_call(projected, upstream, self.group)
        self.d_projected = self.line(work, self.projected, self.d_attended)

    def grad_attn(self):
        work = lambda *rows: attn_grad_of(self.order, *rows)
        rows = (self.modulated, self.d_branch_attn, self.d_projected, self.attended)
        grad = self.line(work, *(one for array in rows for one in self.both(array)))
        return Scatter(self.line, grad)

    def back_project(self, last):
        rows = self.modulation

        def work(d_projected, d_middle, normed, inv_scale, attn):
            d_modulated = collect(self.order, d_projected, attn, 0, 3 * self.part, True)
            back = norm_back(normed, inv_scale, d_modulated * (1.0 + rows[1]))
            return d_modulated, last(d_middle + back)

        self.d_modulated, result = self.line(
            work, self.d_projected, self.d_middle, self.normed, self.inv_scale, self.attn
        )
        return result

    def d_modulation(self):
        terms = (
            self.d_modulated,
            self.d_modulated * self.normed,
            self.d_middle * self.branch_attn,
            self.d_mod_mlp,
            self.d_mod_mlp * self.normed_mlp,
            self.upstream * self.branch_mlp,
        )
        return jnp.stack([jnp.sum(term, axis=0) for term in terms])


def finish_grads(attn_piece, up_piece, down_piece):
    rows, width = attn_piece.shape
    part = width // 4
    qkv = attn_piece[:, : 3 * part].reshape(rows, 3, part).astype(jnp.float32)
    attn = attn_piece[:, 3 * part :].T.astype(jnp.float32)
    return qkv, attn, up_piece.astype(jnp.float32), down_piece.T.astype(jnp.float32)


def deal_rows(rows, axes):
    return lax.all_to_all(rows, axes, split_axis=0, concat_axis=0, tiled=True)


def swap_blocks(rows, outer, inner):
    return rows.reshape(outer, inner, -1, rows.shape[1]).swapaxes(0, 1).reshape(rows.shape)


def local_whole(
    x_in,
    cond,
    mod_weight_one,
    qkv_weight_one,
    attn_out_one,
    mlp_up_one,
    mlp_down_one,
    mod_weight_two,
    qkv_weight_two,
    attn_out_two,
    mlp_up_two,
    mlp_down_two,
    out_cotangent,
):
    rows, _, part = qkv_weight_one.shape
    width = x_in.shape[-1]
    packed = [
        pack_layer((qkv_weight_one, attn_out_one, mlp_up_one, mlp_down_one)),
        pack_layer((qkv_weight_two, attn_out_two, mlp_up_two, mlp_down_two)),
    ]
    cond_every = lax.all_gather(cond, CLIP, axis=0, tiled=True).astype(jnp.float32)
    clip_count = cond_every.shape[0]
    silu_every = jax.nn.silu(cond_every).astype(jnp.bfloat16)
    silu_rows = lax.dynamic_slice_in_dim(silu_every, shard_index() * rows, rows, axis=1)
    mod_weights = (mod_weight_one.astype(jnp.bfloat16), mod_weight_two.astype(jnp.bfloat16))
    partial_value = jnp.stack(
        [
            jnp.einsum("cd,dkz->ckz", silu_rows, weight, preferred_element_type=jnp.float32)
            for weight in mod_weights
        ],
        axis=1,
    )
    devices, tensors = lax.axis_size(FRAME), lax.axis_size(TENSOR)
    own_frames = x_in.shape[1]
    own_places = x_in.shape[2] // devices
    cotangent = deal_rows(swap_blocks(out_cotangent.reshape(-1, width), own_frames, devices), FRAME)
    cotangent = swap_blocks(cotangent, devices, own_frames)
    line = Line()
    summed = line.exchange_sum(line.exchange_sum(partial_value, FRAME), CLIP)
    line.wait(cotangent)
    summed = lax.dynamic_index_in_dim(summed, lax.axis_index(CLIP), 0, keepdims=False)
    placed = line.place_along(summed, TENSOR)
    modulations = placed.transpose(1, 2, 0, 3).reshape(summed.shape[:2] + (-1,))

    order = piece_order()
    attn_one, up_one, down_one = (Gather(line, piece) for piece in packed[0])
    attn_two, up_two, down_two = (Gather(line, piece) for piece in packed[1])
    one = Layer(line, order, modulations[0], 0)
    two = Layer(line, order, modulations[1], own_places)

    attn_one.send()
    line.tick()
    attn_one.relay()
    frames_in = line.send(x_in.reshape(-1, width), lambda held: deal_rows(held, TENSOR))
    up_one.send()
    down_one.soon()
    line.tick()
    attn_one.end()
    up_one.relay()
    down_one.send()
    one.project(line(wide, frames_in), attn_one.pieces)
    one.attend()
    one.attention_out()
    attn_two.soon()
    line.tick()
    up_one.end()
    down_one.relay()
    attn_two.send()
    one.mlp_up(up_one.pieces)
    cotangent = line(wide, cotangent)
    up_two.soon()
    line.tick()
    down_one.end()
    attn_two.relay()
    up_two.send()
    down_two.soon()
    between = one.mlp_down(down_one.pieces, low)
    two.turn_back(cotangent)
    line.tick()
    attn_two.end()
    up_two.relay()
    down_two.send()
    two.share(two.d_branch_mlp)
    between = line(wide, line.send(between, lambda held: deal_rows(held, (TENSOR, FRAME))))
    two.project(between, attn_two.pieces)
    two.attend()
    two.attention_out()
    line.tick()
    up_two.end()
    down_two.relay()
    two.mlp_up(up_two.pieces)
    two.share(two.hidden_act)
    down_grad = two.grad_down()
    line.tick()
    down_two.end()
    down_grad.send()
    two.share(two.modulated_mlp, two.modulated)
    two.slope(down_two.pieces)
    two.share(two.d_pre)
    two.back_up()
    up_grad = two.grad_up()
    line.tick()
    down_grad.relay()
    up_grad.send()
    two.share(two.d_branch_attn, two.attended)
    two.back_out()
    two.back_attend()
    two.share(two.d_projected)
    d_second = two.back_project(low)
    attn_grad = two.grad_attn()
    line.tick()
    up_grad.relay()
    attn_grad.send()
    one.share(one.hidden_act, one.attended)
    d_second = line(wide, deal_rows(d_second, (TENSOR, FRAME)))
    down_grad.finish()
    one.turn_back(d_second)
    one.share(one.d_branch_mlp)
    one.slope(down_one.pieces)
    down_last = one.grad_down()
    line.tick()
    attn_grad.relay()
    down_last.send()
    one.share(one.d_pre, one.modulated_mlp, one.modulated)
    up_grad.finish()
    one.back_up()
    up_last = one.grad_up()
    one.back_out()
    one.back_attend()
    line.tick()
    down_last.relay()
    up_last.send()
    one.share(one.d_branch_attn, one.d_projected)
    attn_grad.finish()
    d_first = one.back_project(low)
    result = two.mlp_down(
        down_two.pieces, lambda rows: swap_blocks(low(rows), own_frames, devices)
    )
    d_mods = line(lambda: jnp.stack([one.d_modulation(), two.d_modulation()]))
    d_mods = line(jnp.add, d_mods, flip(d_mods, FRAME, 1))
    attn_last = one.grad_attn()
    d_mods = line(jnp.add, d_mods, flip(d_mods, TENSOR, 1))
    near_mods = flip(d_mods, TENSOR, 2)
    line.tick()
    up_last.relay()
    attn_last.send()
    down_last.finish()
    input_grad = deal_rows(d_first, TENSOR)
    line.under_way.append(input_grad)
    d_mods = line(jnp.add, d_mods, near_mods)
    near_mods = line.send(d_mods, lambda held: flip(held, FRAME, 2))
    line.tick()
    attn_last.relay()
    up_last.finish()
    input_grad = line(wide, input_grad).reshape(x_in.shape)
    layer_out = swap_blocks(deal_rows(result, FRAME), devices, own_frames).reshape(x_in.shape)
    d_mods = line(jnp.add, d_mods, near_mods)
    d_mods = lax.dynamic_slice_in_dim(d_mods, lax.axis_index(TENSOR) * part, part, axis=2)
    d_every = line.place_along(d_mods, CLIP)
    line.tick()
    attn_last.finish()
    silu_float = silu_rows.astype(jnp.float32)
    grad_mods = [
        sum(
            silu_float[c][:, None, None] * d_every[c, layer][None] for c in range(clip_count)
        )
        for layer in range(2)
    ]
    d_silu = jnp.stack(
        [
            sum(
                jnp.sum(
                    d_every[c, layer][None] * mod_weights[layer].astype(jnp.float32), axis=(1, 2)
                )
                for layer in range(2)
            )
            for c in range(clip_count)
        ]
    )
    d_silu = line.exchange_sum(d_silu, TENSOR)
    d_silu = line.place_along(line.place_along(d_silu, FRAME), CLIP)
    d_silu = d_silu.transpose(2, 0, 1, 3).reshape(clip_count, -1)
    d_silu = lax.dynamic_slice_in_dim(d_silu, lax.axis_index(CLIP), 1, axis=0)
    cond_float = cond.astype(jnp.float32)
    sigmoid_cond = jax.nn.sigmoid(cond_float)
    cond_grad = d_silu * (sigmoid_cond * (1.0 + cond_float * (1.0 - sigmoid_cond)))
    first_out = finish_grads(attn_last.piece, up_last.piece, down_last.piece)
    second_out = finish_grads(attn_grad.piece, up_grad.piece, down_grad.piece)
    return (
        layer_out,
        input_grad,
        cond_grad,
        grad_mods[0],
        *first_out,
        grad_mods[1],
        *second_out,
    )


def holds_whole(mesh):
    tensors = mesh.shape[TENSOR]
    return (
        mesh.shape[CLIP] == 2
        and mesh.shape[FRAME] == 4
        and FRAMES % (4 * tensors) == 0
        and tensors & (tensors - 1) == 0
    )


def solution(mesh):
    return jax.shard_map(
        local_whole if holds_whole(mesh) else local,
        mesh=mesh,
        in_specs=(
            P(CLIP, FRAME, TENSOR, None),
            P(CLIP, None),
            P(SHARDS, None, TENSOR),
            P(SHARDS, None, TENSOR),
            P(TENSOR, SHARDS),
            P(SHARDS, TENSOR),
            P(TENSOR, SHARDS),
            P(SHARDS, None, TENSOR),
            P(SHARDS, None, TENSOR),
            P(TENSOR, SHARDS),
            P(SHARDS, TENSOR),
            P(TENSOR, SHARDS),
            P(CLIP, FRAME, TENSOR, None),
        ),
        out_specs=(
            P(CLIP, FRAME, TENSOR, None),
            P(CLIP, FRAME, TENSOR, None),
            P(CLIP, None),
            P(SHARDS, None, TENSOR),
            P(SHARDS, None, TENSOR),
            P(TENSOR, SHARDS),
            P(SHARDS, TENSOR),
            P(TENSOR, SHARDS),
            P(SHARDS, None, TENSOR),
            P(SHARDS, None, TENSOR),
            P(TENSOR, SHARDS),
            P(SHARDS, TENSOR),
            P(TENSOR, SHARDS),
        ),
        check_vma=False,
    )
```

```python
import functools

import jax
import jax.numpy as jnp
from jax import lax
from jax.experimental import pallas as pl
from jax.experimental.pallas import tpu as pltpu
from jax.sharding import PartitionSpec as P

HD = 72
FRAMES = 16
CLIP, FRAME, TENSOR = "clip", "frame", "tensor"
SHARDS = (CLIP, FRAME)


HIGHEST_PRECISION = lax.Precision.HIGHEST
SCORE_FORMS = {True: "cfphe,cfqhe->cfhpq", False: "cfphe,cgphe->cphfg"}
APPLY_FORMS = {True: "cfhpq,cfqhe->cfphe", False: "cphfg,cgphe->cfphe"}
BACK_FORMS = {True: "cfhpq,cfphe->cfqhe", False: "cphfg,cfphe->cgphe"}
GELU_COEFF = 0.7978845608028654
CUBIC_COEFF = 0.044715


def layer_norm(stream):
    centre = stream - jnp.mean(stream, axis=-1, keepdims=True)
    inv_scale = lax.rsqrt(jnp.mean(centre * centre, axis=-1, keepdims=True) + 1e-06)
    return (centre * inv_scale, inv_scale)


def norm_back(normed, inv_scale, upstream):
    return inv_scale * (
        upstream
        - jnp.mean(upstream, axis=-1, keepdims=True)
        - normed * jnp.mean(upstream * normed, axis=-1, keepdims=True)
    )


def gelu_tanh(inputs):
    return (
        0.5
        * inputs
        * (1.0 + jnp.tanh(GELU_COEFF * (inputs + CUBIC_COEFF * inputs * inputs * inputs)))
    )


def gelu_slope(inputs):
    tangent = jnp.tanh(GELU_COEFF * (inputs + CUBIC_COEFF * inputs * inputs * inputs))
    return 0.5 * (1.0 + tangent) + 0.5 * inputs * (1.0 - tangent * tangent) * GELU_COEFF * (
        1.0 + 3.0 * CUBIC_COEFF * inputs * inputs
    )


def choose(modulation, column):
    return modulation[:, column][:, None, None, :]


def split_heads(projected):
    leading = projected.shape[:3]
    row_width = projected.shape[-1]
    head_count = row_width // HD
    queries = projected[:, :, :, 0].reshape(leading + (head_count, HD))
    key_rows = projected[:, :, :, 1].reshape(leading + (head_count, HD))
    values = projected[:, :, :, 2].reshape(leading + (head_count, HD))
    return (queries, key_rows, values, leading, row_width)


def attend(projected, spatial):
    queries, key_rows, values, leading, row_width = split_heads(projected)
    scores = jnp.einsum(
        SCORE_FORMS[spatial], queries, key_rows, preferred_element_type=jnp.float32
    ) * HD ** (-0.5)
    highest = jnp.max(scores, axis=-1, keepdims=True)
    expo = jnp.exp(scores - highest)
    denominator = jnp.sum(expo, axis=-1, keepdims=True)
    probs = (expo / denominator).astype(jnp.bfloat16)
    log_total = highest + jnp.log(denominator)
    attended = jnp.einsum(APPLY_FORMS[spatial], probs, values, preferred_element_type=jnp.float32)
    return (attended.reshape(leading + (row_width,)).astype(jnp.bfloat16), log_total)


def attend_back(projected, log_total, d_attended, spatial):
    queries, key_rows, values, leading, row_width = split_heads(projected)
    scale_factor = HD ** (-0.5)
    scores = (
        jnp.einsum(SCORE_FORMS[spatial], queries, key_rows, preferred_element_type=jnp.float32)
        * scale_factor
    )
    probs = jnp.exp(scores - log_total)
    upstream = d_attended.reshape(leading + (row_width // HD, HD))
    d_probs = jnp.einsum(SCORE_FORMS[spatial], upstream, values, preferred_element_type=jnp.float32)
    d_values = jnp.einsum(
        BACK_FORMS[spatial],
        probs.astype(jnp.bfloat16),
        upstream,
        preferred_element_type=jnp.float32,
    )
    row_inner = jnp.sum(probs * d_probs, axis=-1, keepdims=True)
    d_scores = (probs * (d_probs - row_inner)).astype(jnp.bfloat16)
    d_queries = (
        jnp.einsum(APPLY_FORMS[spatial], d_scores, key_rows, preferred_element_type=jnp.float32)
        * scale_factor
    )
    d_keys = (
        jnp.einsum(BACK_FORMS[spatial], d_scores, queries, preferred_element_type=jnp.float32)
        * scale_factor
    )
    stacked = jnp.stack([d_queries, d_keys, d_values], axis=3)
    return stacked.reshape(leading + (3, row_width)).astype(jnp.bfloat16)


def fetch_weights(weights):
    cast = tuple((weight.astype(jnp.bfloat16) for weight in weights))
    return (
        lax.all_gather(cast[0], SHARDS, axis=0, tiled=True),
        lax.all_gather(cast[1], SHARDS, axis=0, tiled=True),
        lax.all_gather(cast[2], SHARDS, axis=1, tiled=True),
        lax.all_gather(cast[3], SHARDS, axis=0, tiled=True),
        lax.all_gather(cast[4], SHARDS, axis=1, tiled=True),
    )


def backward_weights(weights):
    cast = tuple((weight.astype(jnp.bfloat16) for weight in weights))
    return (
        lax.all_gather(cast[0], SHARDS, axis=0, tiled=True),
        lax.all_gather(cast[1], SHARDS, axis=0, tiled=True),
        lax.all_gather(cast[2], SHARDS, axis=1, tiled=True),
        lax.all_gather(cast[3], SHARDS, axis=0, tiled=True),
        lax.all_gather(cast[4], SHARDS, axis=1, tiled=True),
    )


def spread_rows(rows):
    return lax.all_gather(rows, TENSOR, axis=2, tiled=True)


def collect_rows(term):
    return lax.psum_scatter(term, TENSOR, scatter_dimension=2, tiled=True)


def attention_output(attended, attn_weight):
    return collect_rows(
        jnp.einsum("cfpz,zd->cfpd", attended, attn_weight, preferred_element_type=jnp.float32)
    )


def layer_forward(stream, silu_cond, gathered, spatial):
    mod_weight, qkv_weight, attn_weight, up_weight, down_weight = gathered
    partial_value = jnp.einsum(
        "cd,dkz->ckz", silu_cond, mod_weight, preferred_element_type=jnp.float32
    )
    modulation = lax.all_gather(partial_value, TENSOR, axis=2, tiled=True)
    normed, inv_scale = layer_norm(stream)
    modulated = (normed * (1.0 + choose(modulation, 1)) + choose(modulation, 0)).astype(
        jnp.bfloat16
    )
    gathered_rows = spread_rows(modulated)
    projected = jnp.einsum(
        "cfpd,dkz->cfpkz", gathered_rows, qkv_weight, preferred_element_type=jnp.float32
    ).astype(jnp.bfloat16)
    if spatial:
        project_held = projected
        attended, log_total = attend(project_held, True)
    else:
        project_held = lax.all_to_all(projected, FRAME, split_axis=2, concat_axis=1, tiled=True)
        placed, log_total = attend(project_held, False)
        attended = lax.all_to_all(placed, FRAME, split_axis=1, concat_axis=2, tiled=True)
    branch_attn = attention_output(attended, attn_weight)
    middle = stream + choose(modulation, 2) * branch_attn
    normed_mlp, inv_mlp = layer_norm(middle)
    modulated_mlp = (normed_mlp * (1.0 + choose(modulation, 4)) + choose(modulation, 3)).astype(
        jnp.bfloat16
    )
    gathered_mlp = spread_rows(modulated_mlp)
    hidden_pre = jnp.einsum(
        "cfpd,dz->cfpz", gathered_mlp, up_weight, preferred_element_type=jnp.float32
    )
    hidden_act = gelu_tanh(hidden_pre).astype(jnp.bfloat16)
    branch_mlp = collect_rows(
        jnp.einsum("cfpz,zd->cfpd", hidden_act, down_weight, preferred_element_type=jnp.float32)
    )
    result = middle + choose(modulation, 5) * branch_mlp
    stored = (
        modulation,
        normed,
        inv_scale,
        gathered_rows,
        project_held,
        log_total,
        attended,
        branch_attn,
        normed_mlp,
        inv_mlp,
        gathered_mlp,
        hidden_pre,
        hidden_act,
        branch_mlp,
    )
    return (result, stored)


def layer_backward(upstream, silu_cond, gathered, stored, spatial):
    mod_weight, qkv_weight, attn_weight, up_weight, down_weight = gathered
    (
        modulation,
        normed,
        inv_scale,
        gathered_rows,
        project_held,
        log_total,
        attended,
        branch_attn,
        normed_mlp,
        inv_mlp,
        gathered_mlp,
        hidden_pre,
        hidden_act,
        branch_mlp,
    ) = stored
    d_branch_mlp = (upstream * choose(modulation, 5)).astype(jnp.bfloat16)
    d_gate_mlp = jnp.sum(upstream * branch_mlp, axis=(1, 2))
    d_branch_all = spread_rows(d_branch_mlp)
    grad_down = jnp.einsum(
        "cfpz,cfpd->zd", hidden_act, d_branch_all, preferred_element_type=jnp.float32
    )
    d_act = jnp.einsum(
        "cfpd,zd->cfpz", d_branch_all, down_weight, preferred_element_type=jnp.float32
    )
    d_pre = (d_act * gelu_slope(hidden_pre)).astype(jnp.bfloat16)
    grad_up = jnp.einsum("cfpd,cfpz->dz", gathered_mlp, d_pre, preferred_element_type=jnp.float32)
    d_mod_mlp = collect_rows(
        jnp.einsum("cfpz,dz->cfpd", d_pre, up_weight, preferred_element_type=jnp.float32)
    )
    d_shift_mlp = jnp.sum(d_mod_mlp, axis=(1, 2))
    d_scale_mlp = jnp.sum(d_mod_mlp * normed_mlp, axis=(1, 2))
    d_middle = upstream + norm_back(normed_mlp, inv_mlp, d_mod_mlp * (1.0 + choose(modulation, 4)))
    d_branch_attn = (d_middle * choose(modulation, 2)).astype(jnp.bfloat16)
    d_gate_attn = jnp.sum(d_middle * branch_attn, axis=(1, 2))
    d_attn_all = spread_rows(d_branch_attn)
    grad_attn = jnp.einsum(
        "cfpz,cfpd->zd", attended, d_attn_all, preferred_element_type=jnp.float32
    )
    d_attended = jnp.einsum(
        "cfpd,zd->cfpz", d_attn_all, attn_weight, preferred_element_type=jnp.float32
    ).astype(jnp.bfloat16)
    if spatial:
        d_projected = attend_back(project_held, log_total, d_attended, True)
    else:
        d_placed = lax.all_to_all(d_attended, FRAME, split_axis=2, concat_axis=1, tiled=True)
        d_projected = lax.all_to_all(
            attend_back(project_held, log_total, d_placed, False),
            FRAME,
            split_axis=1,
            concat_axis=2,
            tiled=True,
        )
    grad_qkv = jnp.einsum(
        "cfpd,cfpkz->dkz", gathered_rows, d_projected, preferred_element_type=jnp.float32
    )
    d_modulated = collect_rows(
        jnp.einsum("cfpkz,dkz->cfpd", d_projected, qkv_weight, preferred_element_type=jnp.float32)
    )
    d_shift_attn = jnp.sum(d_modulated, axis=(1, 2))
    d_scale_attn = jnp.sum(d_modulated * normed, axis=(1, 2))
    d_stream = d_middle + norm_back(normed, inv_scale, d_modulated * (1.0 + choose(modulation, 1)))
    d_modulation = jnp.stack(
        [d_shift_attn, d_scale_attn, d_gate_attn, d_shift_mlp, d_scale_mlp, d_gate_mlp], axis=1
    )
    d_mod_own = lax.psum_scatter(d_modulation, TENSOR, scatter_dimension=2, tiled=True)
    grad_mod = jnp.einsum(
        "cd,ckz->dkz", silu_cond.astype(jnp.float32), d_mod_own, precision=HIGHEST_PRECISION
    )
    d_silu = jnp.einsum(
        "ckz,dkz->cd", d_mod_own, mod_weight.astype(jnp.float32), precision=HIGHEST_PRECISION
    )
    grads = (
        lax.psum_scatter(
            grad_mod.astype(jnp.bfloat16), SHARDS, scatter_dimension=0, tiled=True
        ).astype(jnp.float32),
        lax.psum_scatter(
            grad_qkv.astype(jnp.bfloat16), SHARDS, scatter_dimension=0, tiled=True
        ).astype(jnp.float32),
        lax.psum_scatter(
            grad_attn.astype(jnp.bfloat16), SHARDS, scatter_dimension=1, tiled=True
        ).astype(jnp.float32),
        lax.psum_scatter(
            grad_up.astype(jnp.bfloat16), SHARDS, scatter_dimension=0, tiled=True
        ).astype(jnp.float32),
        lax.psum_scatter(
            grad_down.astype(jnp.bfloat16), SHARDS, scatter_dimension=1, tiled=True
        ).astype(jnp.float32),
    )
    return (d_stream, d_silu, grads)


def local(
    x_in,
    cond,
    mod_weight_one,
    qkv_weight_one,
    attn_out_one,
    mlp_up_one,
    mlp_down_one,
    mod_weight_two,
    qkv_weight_two,
    attn_out_two,
    mlp_up_two,
    mlp_down_two,
    out_cotangent,
):
    weights_first = (mod_weight_one, qkv_weight_one, attn_out_one, mlp_up_one, mlp_down_one)
    weights_second = (mod_weight_two, qkv_weight_two, attn_out_two, mlp_up_two, mlp_down_two)
    cond_float = cond.astype(jnp.float32)
    silu_cond = jax.nn.silu(cond_float).astype(jnp.bfloat16)
    gathered_first = fetch_weights(weights_first)
    middle_stream, stored_first = layer_forward(
        x_in.astype(jnp.float32), silu_cond, gathered_first, True
    )
    gathered_second = fetch_weights(weights_second)
    result, stored_second = layer_forward(middle_stream, silu_cond, gathered_second, False)
    back_second = backward_weights(weights_second)
    d_middle_stream, d_silu_second, grads_second = layer_backward(
        out_cotangent.astype(jnp.float32), silu_cond, back_second, stored_second, False
    )
    back_first = backward_weights(weights_first)
    input_grad, d_silu_first, grads_first = layer_backward(
        d_middle_stream, silu_cond, back_first, stored_first, True
    )
    d_silu_total = lax.psum(d_silu_first + d_silu_second, (FRAME, TENSOR))
    sigmoid_cond = jax.nn.sigmoid(cond_float)
    cond_grad = d_silu_total * (sigmoid_cond * (1.0 + cond_float * (1.0 - sigmoid_cond)))
    return (
        result.astype(jnp.bfloat16),
        input_grad,
        cond_grad,
        grads_first[0],
        grads_first[1],
        grads_first[2],
        grads_first[3],
        grads_first[4],
        grads_second[0],
        grads_second[1],
        grads_second[2],
        grads_second[3],
        grads_second[4],
    )

def flip(array, axis, bit):
    count = lax.axis_size(axis)
    return lax.ppermute(array, axis, [(i, i ^ bit) for i in range(count)])


def first_flip(shard):
    return 2 if shard % 2 == 0 else 4


def hop(array, which):
    if which == 0:
        pairs = [(i, i ^ 1) for i in range(8)]
    elif which == 1:
        pairs = [(i, i ^ first_flip(i)) for i in range(8)]
    else:
        pairs = [(i, i ^ (6 - first_flip(i))) for i in range(8)]
    return lax.ppermute(array, SHARDS, pairs)


class Line:
    def __init__(self):
        self.last = ()
        self.awaited = []
        self.under_way = []
        self.under_way_next = []

    def held(self, value):
        return lax.optimization_barrier((value, self.last, self.awaited))[0]

    def __call__(self, work, *inputs):
        self.last = work(*self.held(inputs))
        self.awaited = []
        return self.last

    def wait(self, value):
        self.awaited.append(value)
        return value

    def send(self, array, move):
        self.under_way.append(move(self.held(array)))
        return self.under_way[-1]

    def hop(self, array, which):
        return self.send(array, lambda held: hop(held, which))

    def exchange_sum(self, array, axis):
        bit = 1
        while bit < lax.axis_size(axis):
            array = self(jnp.add, array, flip(array, axis, bit))
            bit *= 2
        return array

    def place_along(self, array, axis):
        count = lax.axis_size(axis)
        own = (jnp.arange(count) == lax.axis_index(axis)).reshape((count,) + (1,) * array.ndim)
        return self.exchange_sum(jnp.where(own, array[None], 0.0), axis)

    def send_ahead(self, array, move):
        self.under_way_next.append(move(self.held(array)))
        return self.under_way_next[-1]

    def tick(self):
        self.awaited += self.under_way
        self.under_way = self.under_way_next
        self.under_way_next = []


def shard_index():
    return lax.axis_index(CLIP) * lax.axis_size(FRAME) + lax.axis_index(FRAME)


def piece_order():
    shard = shard_index()
    first = jnp.where(shard % 2 == 0, 2, 4)
    second = 6 - first
    masks = [0, first, second, 6, 1, 1 ^ second, 1 ^ first, 7]
    return jnp.stack([shard ^ mask for mask in masks]).astype(jnp.int32)


class Gather:
    def __init__(self, line, piece):
        self.line = line
        self.whole = lax.all_gather(piece, TENSOR, axis=0, tiled=False)

    def soon(self):
        self.line.under_way.append(self.whole)

    def send(self):
        self.line.wait(self.whole)
        self.near = self.line.hop(self.whole, 1)

    def relay(self):
        self.pair = self.line(lambda *pair: jnp.stack(pair), self.whole, self.near)
        self.far = self.line.hop(self.pair, 2)
        self.other_pair = self.line.hop(self.pair, 0)

    def end(self):
        other_far = self.line.hop(self.far, 0)
        self.pieces = (self.pair, self.far, self.other_pair, other_far)


def wide(array):
    return array.astype(jnp.float32)


def low(array):
    return array.astype(jnp.bfloat16)


def total(*arrays):
    return low(sum(wide(array) for array in arrays))


class Scatter:
    def __init__(self, line, grad):
        self.line = line
        self.keep, away = grad
        self.far = line.send_ahead(away, lambda held: hop(held, 2))

    def relay(self):
        work = lambda keep, far: total(keep[1], far[1])
        self.near = self.line.hop(self.line(work, self.keep, self.far), 1)

    def finish(self):
        work = lambda keep, far, near: total(keep[0], far[0], near)
        own = self.line(work, self.keep, self.far, self.near)
        self.piece = lax.psum_scatter(own, TENSOR, scatter_dimension=0, tiled=False)


def pack_layer(weights):
    qkv, attn, up, down = (weight.astype(jnp.bfloat16) for weight in weights)
    rows = qkv.shape[0]
    attn_part = jnp.concatenate([qkv.reshape(rows, -1), attn.T], axis=1)
    return attn_part, up, down.T


PIECES = 8
PAIRS = 4
VMEM_BYTES = 48 << 20
COST_SHARE = 8


def contract(left, right, left_dim, right_dim):
    return lax.dot_general(
        left, right, (((left_dim,), (right_dim,)), ((), ())), preferred_element_type=jnp.float32
    )


def assemble(order_ref, piece_refs, whole_ref):
    rows = piece_refs[0].shape[2]
    for j in range(PIECES):
        start = pl.multiple_of(order_ref[j] * rows, 16)
        whole_ref[pl.ds(start, rows), :] = piece_refs[j // 2][j % 2, 0]


def up_kernel(order_ref, x_ref, *refs):
    pre_ref, act_ref, whole_ref = refs[PAIRS:]
    assemble(order_ref, refs[:PAIRS], whole_ref)
    pre = contract(x_ref[...], whole_ref[...], 1, 0)
    pre_ref[...] = pre
    act_ref[...] = gelu_tanh(pre).astype(jnp.bfloat16)


def slope_kernel(order_ref, x_ref, pre_ref, *refs):
    out_ref, whole_ref = refs[PAIRS:]
    assemble(order_ref, refs[:PAIRS], whole_ref)
    d_act = contract(x_ref[...], whole_ref[...], 1, 0)
    out_ref[...] = (d_act * gelu_slope(pre_ref[...])).astype(jnp.bfloat16)


def turned_kernel(low, high, order_ref, x_ref, *refs):
    out_ref, whole_ref = refs[PAIRS:]
    assemble(order_ref, refs[:PAIRS], whole_ref)
    whole = contract(x_ref[...], whole_ref[...], 1, 0)
    out_ref[0] = whole[:, low:high].astype(jnp.bfloat16).T


def collect_kernel(low, high, turned, order_ref, y_ref, *refs):
    out_ref, whole_ref = refs[PAIRS:]
    assemble(order_ref, refs[:PAIRS], whole_ref)
    rows = y_ref[0].T if turned else y_ref[...]
    term = contract(rows, whole_ref[:, low:high], 1, 1)

    @pl.when(pl.program_id(0) == 0)
    def _():
        out_ref[...] = term

    @pl.when(pl.program_id(0) > 0)
    def _():
        out_ref[...] += term


def turn(order_ref, x_refs, whole_ref, turned_ref):
    rows, tokens = turned_ref.shape[0] * 2 // PIECES, turned_ref.shape[1] // 2
    for side in range(2):
        whole_ref[...] = x_refs[side][...].T
        for j in range(PIECES // 2):
            start = pl.multiple_of(order_ref[j] * rows, 16)
            turned_ref[pl.ds(j * rows, rows), pl.ds(side * tokens, tokens)] = whole_ref[
                pl.ds(start, rows), :
            ]


def deal_out(grad, *out_refs):
    rows = out_refs[0].shape[2]
    for j in range(PIECES // 2):
        out_refs[j // 2][j % 2, 0] = grad[j * rows : (j + 1) * rows]


def grad_kernel(order_ref, x_ref, x_other, y_ref, y_other, *refs):
    whole_ref, turned_ref = refs[2:]

    @pl.when(pl.program_id(0) == 0)
    def _():
        turn(order_ref, (x_ref, x_other), whole_ref, turned_ref)

    tokens = x_ref.shape[0]
    grad = contract(turned_ref[:, :tokens], y_ref[...], 1, 0)
    grad += contract(turned_ref[:, tokens:], y_other[...], 1, 0)
    deal_out(grad.astype(jnp.bfloat16), *refs[:2])


def attn_grad_kernel(order_ref, *refs):
    x_refs, b_refs, y_refs, a_refs = (refs[2 * j : 2 * j + 2] for j in range(4))
    out_refs, (whole_ref, x_turned, b_turned, grad_ref) = refs[8:10], refs[10:]

    @pl.when(pl.program_id(0) == 0)
    def _():
        turn(order_ref, x_refs, whole_ref, x_turned)
        turn(order_ref, b_refs, whole_ref, b_turned)

    tokens, split = y_refs[0].shape[2], y_refs[0].shape[1]
    for turned, pair, lanes in (
        (x_turned, y_refs, slice(0, split)),
        (b_turned, a_refs, slice(split, grad_ref.shape[1])),
    ):
        grad = contract(turned[:, :tokens], pair[0][0], 1, 1)
        grad += contract(turned[:, tokens:], pair[1][0], 1, 1)
        grad_ref[:, lanes] = grad.astype(jnp.bfloat16)
    deal_out(grad_ref[...], *out_refs)


def masked_scores(queries, keys, group):
    scores = contract(queries, keys, 0, 0) * HD ** (-0.5)
    if group:
        place = lax.broadcasted_iota(jnp.int32, scores.shape, 0) % group
        other = lax.broadcasted_iota(jnp.int32, scores.shape, 1) % group
        scores = jnp.where(place == other, scores, -3e38)
    expo = jnp.exp(scores - jnp.max(scores, axis=-1, keepdims=True))
    return expo / jnp.sum(expo, axis=-1, keepdims=True)


def attend_kernel(group, projected_ref, out_ref):
    part = out_ref.shape[1]
    for start in range(0, part, HD):
        queries, keys, values = (
            projected_ref[0, pl.ds(j * part + start, HD), :] for j in range(3)
        )
        probs = masked_scores(queries, keys, group).astype(jnp.bfloat16)
        out_ref[0, pl.ds(start, HD), :] = contract(values, probs, 1, 1).astype(jnp.bfloat16)


def attend_back_kernel(group, projected_ref, upstream_ref, out_ref):
    part = upstream_ref.shape[1]
    scale_factor = HD ** (-0.5)
    for start in range(0, part, HD):
        queries, keys, values = (
            projected_ref[0, pl.ds(j * part + start, HD), :] for j in range(3)
        )
        upstream = upstream_ref[0, pl.ds(start, HD), :]
        probs = masked_scores(queries, keys, group)
        d_probs = contract(upstream, values, 0, 0)
        row_inner = jnp.sum(probs * d_probs, axis=-1, keepdims=True)
        d_scores = (probs * (d_probs - row_inner)).astype(jnp.bfloat16)
        grads = (
            contract(keys, d_scores, 1, 1) * scale_factor,
            contract(queries, d_scores, 1, 0) * scale_factor,
            contract(upstream, probs.astype(jnp.bfloat16), 1, 0),
        )
        for j in range(3):
            out_ref[0, pl.ds(j * part + start, HD), :] = grads[j].astype(jnp.bfloat16)


def call(kernel, grid, in_specs, out_specs, out_shape, scratch, flops, args):
    moved = sum(a.size * a.dtype.itemsize for a in args)
    moved += sum(o.size * o.dtype.itemsize for o in jax.tree.leaves(out_shape))
    return pl.pallas_call(
        kernel,
        out_shape=out_shape,
        grid_spec=pltpu.PrefetchScalarGridSpec(
            num_scalar_prefetch=1 if scratch else 0,
            grid=grid,
            in_specs=in_specs,
            out_specs=out_specs,
            scratch_shapes=scratch,
        ),
        compiler_params=pltpu.CompilerParams(vmem_limit_bytes=VMEM_BYTES),
        cost_estimate=pl.CostEstimate(
            flops=flops // COST_SHARE, bytes_accessed=moved // COST_SHARE, transcendentals=0
        ),
    )(*args)


def still(shape):
    return pl.BlockSpec(shape, lambda z, *_: (0,) * len(shape))


def lead(shape):
    return pl.BlockSpec((1,) + shape, lambda z, *_: (z,) + (0,) * len(shape))


def column(tokens, width):
    return pl.BlockSpec((tokens, width), lambda z, *_: (0, z))


def sizes(pieces):
    _, groups, rows, width = pieces[0].shape
    return groups, rows, width, rows * PIECES


def pair_specs(rows, width, count):
    return [pl.BlockSpec((2, 1, rows, width), lambda z, *_: (0, z, 0, 0))] * count


def times_up(order, x, pieces):
    groups, rows, width, depth = sizes(pieces)
    tokens = x.shape[0]
    shape = (tokens, groups * width)
    return call(
        up_kernel,
        (groups,),
        [still(x.shape)] + pair_specs(rows, width, PAIRS),
        [column(tokens, width)] * 2,
        [jax.ShapeDtypeStruct(shape, jnp.float32), jax.ShapeDtypeStruct(shape, jnp.bfloat16)],
        [pltpu.VMEM((depth, width), jnp.bfloat16)],
        2 * tokens * depth * width * groups,
        (order, x) + pieces,
    )


def times_slope(order, x, pre, pieces):
    groups, rows, width, depth = sizes(pieces)
    tokens = x.shape[0]
    return call(
        slope_kernel,
        (groups,),
        [still(x.shape), column(tokens, width)] + pair_specs(rows, width, PAIRS),
        column(tokens, width),
        jax.ShapeDtypeStruct(pre.shape, jnp.bfloat16),
        [pltpu.VMEM((depth, width), jnp.bfloat16)],
        2 * tokens * depth * width * groups,
        (order, x, pre) + pieces,
    )


def times_turned(order, x, pieces, low, high):
    groups, rows, width, depth = sizes(pieces)
    tokens = x.shape[0]
    return call(
        functools.partial(turned_kernel, low, high),
        (groups,),
        [still(x.shape)] + pair_specs(rows, width, PAIRS),
        lead((high - low, tokens)),
        jax.ShapeDtypeStruct((groups, high - low, tokens), jnp.bfloat16),
        [pltpu.VMEM((depth, width), jnp.bfloat16)],
        2 * tokens * depth * width * groups,
        (order, x) + pieces,
    )


def collect(order, y, pieces, low, high, turned):
    groups, rows, width, depth = sizes(pieces)
    tokens = y.shape[2] if turned else y.shape[0]
    return call(
        functools.partial(collect_kernel, low, high, turned),
        (groups,),
        [lead(y.shape[1:]) if turned else column(tokens, width)]
        + pair_specs(rows, width, PAIRS),
        still((tokens, depth)),
        jax.ShapeDtypeStruct((tokens, depth), jnp.float32),
        [pltpu.VMEM((depth, width), jnp.bfloat16)],
        2 * tokens * depth * (high - low) * groups,
        (order, y) + pieces,
    )


def grad_call(kernel, args, specs, groups, depth, width, scratch):
    rows = depth // PIECES
    tokens = args[1].shape[0]
    return call(
        kernel,
        (groups,),
        specs,
        pair_specs(rows, width, 2),
        [jax.ShapeDtypeStruct((2, groups, rows, width), jnp.bfloat16)] * 2,
        [pltpu.VMEM((depth, tokens), jnp.bfloat16)]
        + [pltpu.VMEM(shape, jnp.bfloat16) for shape in scratch],
        2 * tokens * depth * width * groups,
        args,
    )


def grad_of(order, x, x_other, y, y_other, groups):
    tokens, width = x.shape[0], y.shape[1] // groups
    depth = x.shape[1]
    specs = [still(x.shape)] * 2 + [column(tokens, width)] * 2
    args = (order, x, x_other, y, y_other)
    scratch = [(depth // 2, 2 * tokens)]
    return grad_call(grad_kernel, args, specs, groups, depth, width, scratch)


def attn_grad_of(order, *args):
    x, y, a = args[0], args[4], args[6]
    groups, wide_part, tokens = y.shape
    part, depth = a.shape[1], x.shape[1]
    specs = [still(x.shape)] * 4 + [lead((wide_part, tokens))] * 2 + [lead((part, tokens))] * 2
    scratch = [(depth // 2, 2 * tokens)] * 2 + [(depth // 2, wide_part + part)]
    return grad_call(
        attn_grad_kernel, (order, *args), specs, groups, depth, wide_part + part, scratch
    )


def attend_call(projected, group):
    groups, wide, tokens = projected.shape
    part = wide // 3
    return call(
        functools.partial(attend_kernel, group),
        (groups,),
        [lead((wide, tokens))],
        lead((part, tokens)),
        jax.ShapeDtypeStruct((groups, part, tokens), jnp.bfloat16),
        [],
        4 * tokens * tokens * part * groups,
        (projected,),
    )


def attend_back_call(projected, upstream, group):
    groups, wide, tokens = projected.shape
    part = wide // 3
    return call(
        functools.partial(attend_back_kernel, group),
        (groups,),
        [lead((wide, tokens)), lead((part, tokens))],
        lead((wide, tokens)),
        jax.ShapeDtypeStruct((groups, wide, tokens), jnp.bfloat16),
        [],
        10 * tokens * tokens * part * groups,
        (projected, upstream),
    )


class Layer:
    def __init__(self, line, order, modulation, group):
        self.line = line
        self.order = order
        self.modulation = modulation
        self.group = group
        self.others = {}

    def share(self, *arrays):
        for array in arrays:
            self.others[id(array)] = self.line.hop(array, 0)

    def both(self, array):
        return array, self.others[id(array)]

    def project(self, stream, attn):
        self.stream = stream
        self.attn = attn
        self.width = attn[0].shape[-1]
        self.part = self.width // 4
        rows = self.modulation

        def work(stream, attn):
            normed, inv_scale = layer_norm(stream)
            modulated = low(normed * (1.0 + rows[1]) + rows[0])
            projected = times_turned(self.order, modulated, attn, 0, 3 * self.part)
            return normed, inv_scale, modulated, projected

        made = self.line(work, stream, attn)
        self.normed, self.inv_scale, self.modulated, self.projected = made

    def attend(self):
        self.attended = self.line(
            lambda projected: attend_call(projected, self.group), self.projected
        )

    def attention_out(self):
        rows = self.modulation

        def work(attended, stream, attn):
            branch_attn = collect(self.order, attended, attn, 3 * self.part, self.width, True)
            middle = stream + rows[2] * branch_attn
            normed_mlp, inv_mlp = layer_norm(middle)
            modulated_mlp = low(normed_mlp * (1.0 + rows[4]) + rows[3])
            return branch_attn, middle, normed_mlp, inv_mlp, modulated_mlp

        made = self.line(work, self.attended, self.stream, self.attn)
        self.branch_attn, self.middle, self.normed_mlp, self.inv_mlp, self.modulated_mlp = made

    def mlp_up(self, up):
        self.up = up
        work = lambda rows, up: times_up(self.order, rows, up)
        self.hidden_pre, self.hidden_act = self.line(work, self.modulated_mlp, up)

    def mlp_down(self, down, last):
        rows = self.modulation

        def work(act, middle, down):
            branch_mlp = collect(self.order, act, down, 0, self.width, False)
            return branch_mlp, last(middle + rows[5] * branch_mlp)

        self.branch_mlp, result = self.line(work, self.hidden_act, self.middle, down)
        return result

    def turn_back(self, upstream):
        rows = self.modulation
        self.upstream = upstream
        self.d_branch_mlp = self.line(lambda rows_in: low(rows_in * rows[5]), upstream)

    def gradient(self, *args):
        groups = self.attn[0].shape[1]
        work = lambda *rows: grad_of(self.order, *rows, groups)
        return Scatter(self.line, self.line(work, *args))

    def grad_down(self):
        return self.gradient(*self.both(self.d_branch_mlp), *self.both(self.hidden_act))

    def slope(self, down):
        work = lambda rows, pre, down: times_slope(self.order, rows, pre, down)
        self.d_pre = self.line(work, self.d_branch_mlp, self.hidden_pre, down)

    def grad_up(self):
        return self.gradient(*self.both(self.modulated_mlp), *self.both(self.d_pre))

    def back_up(self):
        rows = self.modulation

        def work(d_pre, upstream, normed, inv_mlp, up):
            d_mod_mlp = collect(self.order, d_pre, up, 0, self.width, False)
            d_middle = upstream + norm_back(normed, inv_mlp, d_mod_mlp * (1.0 + rows[4]))
            return d_mod_mlp, d_middle, low(d_middle * rows[2])

        made = self.line(
            work, self.d_pre, self.upstream, self.normed_mlp, self.inv_mlp, self.up
        )
        self.d_mod_mlp, self.d_middle, self.d_branch_attn = made

    def back_out(self):
        work = lambda rows, attn: times_turned(
            self.order, rows, attn, 3 * self.part, self.width
        )
        self.d_attended = self.line(work, self.d_branch_attn, self.attn)

    def back_attend(self):
        work = lambda projected, upstream: attend_back_call(projected, upstream, self.group)
        self.d_projected = self.line(work, self.projected, self.d_attended)

    def grad_attn(self):
        work = lambda *rows: attn_grad_of(self.order, *rows)
        rows = (self.modulated, self.d_branch_attn, self.d_projected, self.attended)
        grad = self.line(work, *(one for array in rows for one in self.both(array)))
        return Scatter(self.line, grad)

    def back_project(self, last):
        rows = self.modulation

        def work(d_projected, d_middle, normed, inv_scale, attn):
            d_modulated = collect(self.order, d_projected, attn, 0, 3 * self.part, True)
            back = norm_back(normed, inv_scale, d_modulated * (1.0 + rows[1]))
            return d_modulated, last(d_middle + back)

        self.d_modulated, result = self.line(
            work, self.d_projected, self.d_middle, self.normed, self.inv_scale, self.attn
        )
        return result

    def d_modulation(self):
        terms = (
            self.d_modulated,
            self.d_modulated * self.normed,
            self.d_middle * self.branch_attn,
            self.d_mod_mlp,
            self.d_mod_mlp * self.normed_mlp,
            self.upstream * self.branch_mlp,
        )
        return jnp.stack([jnp.sum(term, axis=0) for term in terms])


def finish_grads(attn_piece, up_piece, down_piece):
    rows, width = attn_piece.shape
    part = width // 4
    qkv = attn_piece[:, : 3 * part].reshape(rows, 3, part).astype(jnp.float32)
    attn = attn_piece[:, 3 * part :].T.astype(jnp.float32)
    return qkv, attn, up_piece.astype(jnp.float32), down_piece.T.astype(jnp.float32)


def deal_rows(rows, axes):
    return lax.all_to_all(rows, axes, split_axis=0, concat_axis=0, tiled=True)


def swap_blocks(rows, outer, inner):
    return rows.reshape(outer, inner, -1, rows.shape[1]).swapaxes(0, 1).reshape(rows.shape)


def local_whole(
    x_in,
    cond,
    mod_weight_one,
    qkv_weight_one,
    attn_out_one,
    mlp_up_one,
    mlp_down_one,
    mod_weight_two,
    qkv_weight_two,
    attn_out_two,
    mlp_up_two,
    mlp_down_two,
    out_cotangent,
):
    rows, _, part = qkv_weight_one.shape
    width = x_in.shape[-1]
    packed = [
        pack_layer((qkv_weight_one, attn_out_one, mlp_up_one, mlp_down_one)),
        pack_layer((qkv_weight_two, attn_out_two, mlp_up_two, mlp_down_two)),
    ]
    cond_every = lax.all_gather(cond, CLIP, axis=0, tiled=True).astype(jnp.float32)
    clip_count = cond_every.shape[0]
    silu_every = jax.nn.silu(cond_every).astype(jnp.bfloat16)
    silu_rows = lax.dynamic_slice_in_dim(silu_every, shard_index() * rows, rows, axis=1)
    mod_weights = (mod_weight_one.astype(jnp.bfloat16), mod_weight_two.astype(jnp.bfloat16))
    partial_value = jnp.stack(
        [
            jnp.einsum("cd,dkz->ckz", silu_rows, weight, preferred_element_type=jnp.float32)
            for weight in mod_weights
        ],
        axis=1,
    )
    devices, tensors = lax.axis_size(FRAME), lax.axis_size(TENSOR)
    own_frames = x_in.shape[1]
    own_places = x_in.shape[2] // devices
    cotangent = deal_rows(swap_blocks(out_cotangent.reshape(-1, width), own_frames, devices), FRAME)
    cotangent = swap_blocks(cotangent, devices, own_frames)
    line = Line()
    summed = line.exchange_sum(line.exchange_sum(partial_value, FRAME), CLIP)
    line.wait(cotangent)
    summed = lax.dynamic_index_in_dim(summed, lax.axis_index(CLIP), 0, keepdims=False)
    placed = line.place_along(summed, TENSOR)
    modulations = placed.transpose(1, 2, 0, 3).reshape(summed.shape[:2] + (-1,))

    order = piece_order()
    attn_one, up_one, down_one = (Gather(line, piece) for piece in packed[0])
    attn_two, up_two, down_two = (Gather(line, piece) for piece in packed[1])
    one = Layer(line, order, modulations[0], 0)
    two = Layer(line, order, modulations[1], own_places)

    attn_one.send()
    line.tick()
    attn_one.relay()
    frames_in = line.send(x_in.reshape(-1, width), lambda held: deal_rows(held, TENSOR))
    up_one.send()
    down_one.soon()
    line.tick()
    attn_one.end()
    up_one.relay()
    down_one.send()
    one.project(line(wide, frames_in), attn_one.pieces)
    one.attend()
    one.attention_out()
    attn_two.soon()
    line.tick()
    up_one.end()
    down_one.relay()
    attn_two.send()
    one.mlp_up(up_one.pieces)
    cotangent = line(wide, cotangent)
    up_two.soon()
    line.tick()
    down_one.end()
    attn_two.relay()
    up_two.send()
    down_two.soon()
    between = one.mlp_down(down_one.pieces, low)
    between = line.send_ahead(between, lambda held: deal_rows(held, (TENSOR, FRAME)))
    two.turn_back(cotangent)
    line.tick()
    attn_two.end()
    up_two.relay()
    down_two.send()
    two.share(two.d_branch_mlp)
    between = line(wide, between)
    two.project(between, attn_two.pieces)
    two.attend()
    two.attention_out()
    line.tick()
    up_two.end()
    down_two.relay()
    two.mlp_up(up_two.pieces)
    two.share(two.hidden_act)
    down_grad = two.grad_down()
    line.tick()
    down_two.end()
    two.share(two.modulated_mlp, two.modulated)
    two.slope(down_two.pieces)
    two.share(two.d_pre)
    two.back_up()
    up_grad = two.grad_up()
    line.tick()
    down_grad.relay()
    two.share(two.d_branch_attn, two.attended)
    two.back_out()
    two.back_attend()
    two.share(two.d_projected)
    d_second = two.back_project(low)
    d_second = line.send_ahead(d_second, lambda held: deal_rows(held, (TENSOR, FRAME)))
    attn_grad = two.grad_attn()
    line.tick()
    up_grad.relay()
    one.share(one.hidden_act, one.attended)
    d_second = line(wide, d_second)
    down_grad.finish()
    one.turn_back(d_second)
    one.share(one.d_branch_mlp)
    one.slope(down_one.pieces)
    down_last = one.grad_down()
    line.tick()
    attn_grad.relay()
    one.share(one.d_pre, one.modulated_mlp, one.modulated)
    up_grad.finish()
    one.back_up()
    up_last = one.grad_up()
    one.back_out()
    one.back_attend()
    line.tick()
    down_last.relay()
    one.share(one.d_branch_attn, one.d_projected)
    attn_grad.finish()
    d_first = one.back_project(low)
    result = two.mlp_down(
        down_two.pieces, lambda rows: swap_blocks(low(rows), own_frames, devices)
    )
    d_mods = line(lambda: jnp.stack([one.d_modulation(), two.d_modulation()]))
    d_mods = line(jnp.add, d_mods, flip(d_mods, FRAME, 1))
    attn_last = one.grad_attn()
    d_mods = line(jnp.add, d_mods, flip(d_mods, TENSOR, 1))
    near_mods = flip(d_mods, TENSOR, 2)
    line.tick()
    up_last.relay()
    down_last.finish()
    input_grad = deal_rows(d_first, TENSOR)
    line.under_way.append(input_grad)
    d_mods = line(jnp.add, d_mods, near_mods)
    near_mods = line.send(d_mods, lambda held: flip(held, FRAME, 2))
    line.tick()
    attn_last.relay()
    up_last.finish()
    input_grad = line(wide, input_grad).reshape(x_in.shape)
    line.tick()
    attn_last.finish()
    layer_out = swap_blocks(deal_rows(result, FRAME), devices, own_frames).reshape(x_in.shape)
    d_mods = line(jnp.add, d_mods, near_mods)
    d_mods = lax.dynamic_slice_in_dim(d_mods, lax.axis_index(TENSOR) * part, part, axis=2)
    d_every = line.place_along(d_mods, CLIP)
    silu_float = silu_rows.astype(jnp.float32)
    grad_mods = [
        sum(
            silu_float[c][:, None, None] * d_every[c, layer][None] for c in range(clip_count)
        )
        for layer in range(2)
    ]
    d_silu = jnp.stack(
        [
            sum(
                jnp.sum(
                    d_every[c, layer][None] * mod_weights[layer].astype(jnp.float32), axis=(1, 2)
                )
                for layer in range(2)
            )
            for c in range(clip_count)
        ]
    )
    d_silu = line.exchange_sum(d_silu, TENSOR)
    d_silu = line.place_along(line.place_along(d_silu, FRAME), CLIP)
    d_silu = d_silu.transpose(2, 0, 1, 3).reshape(clip_count, -1)
    d_silu = lax.dynamic_slice_in_dim(d_silu, lax.axis_index(CLIP), 1, axis=0)
    cond_float = cond.astype(jnp.float32)
    sigmoid_cond = jax.nn.sigmoid(cond_float)
    cond_grad = d_silu * (sigmoid_cond * (1.0 + cond_float * (1.0 - sigmoid_cond)))
    first_out = finish_grads(attn_last.piece, up_last.piece, down_last.piece)
    second_out = finish_grads(attn_grad.piece, up_grad.piece, down_grad.piece)
    return (
        layer_out,
        input_grad,
        cond_grad,
        grad_mods[0],
        *first_out,
        grad_mods[1],
        *second_out,
    )


def holds_whole(mesh):
    tensors = mesh.shape[TENSOR]
    return (
        mesh.shape[CLIP] == 2
        and mesh.shape[FRAME] == 4
        and FRAMES % (4 * tensors) == 0
        and tensors & (tensors - 1) == 0
    )


def solution(mesh):
    return jax.shard_map(
        local_whole if holds_whole(mesh) else local,
        mesh=mesh,
        in_specs=(
            P(CLIP, FRAME, TENSOR, None),
            P(CLIP, None),
            P(SHARDS, None, TENSOR),
            P(SHARDS, None, TENSOR),
            P(TENSOR, SHARDS),
            P(SHARDS, TENSOR),
            P(TENSOR, SHARDS),
            P(SHARDS, None, TENSOR),
            P(SHARDS, None, TENSOR),
            P(TENSOR, SHARDS),
            P(SHARDS, TENSOR),
            P(TENSOR, SHARDS),
            P(CLIP, FRAME, TENSOR, None),
        ),
        out_specs=(
            P(CLIP, FRAME, TENSOR, None),
            P(CLIP, FRAME, TENSOR, None),
            P(CLIP, None),
            P(SHARDS, None, TENSOR),
            P(SHARDS, None, TENSOR),
            P(TENSOR, SHARDS),
            P(SHARDS, TENSOR),
            P(TENSOR, SHARDS),
            P(SHARDS, None, TENSOR),
            P(SHARDS, None, TENSOR),
            P(TENSOR, SHARDS),
            P(SHARDS, TENSOR),
            P(TENSOR, SHARDS),
        ),
        check_vma=False,
    )
```

```python
import functools

import jax
import jax.numpy as jnp
from jax import lax
from jax.experimental import pallas as pl
from jax.experimental.pallas import tpu as pltpu
from jax.sharding import PartitionSpec as P

HD = 72
FRAMES = 16
CLIP, FRAME, TENSOR = "clip", "frame", "tensor"
SHARDS = (CLIP, FRAME)


HIGHEST_PRECISION = lax.Precision.HIGHEST
SCORE_FORMS = {True: "cfphe,cfqhe->cfhpq", False: "cfphe,cgphe->cphfg"}
APPLY_FORMS = {True: "cfhpq,cfqhe->cfphe", False: "cphfg,cgphe->cfphe"}
BACK_FORMS = {True: "cfhpq,cfphe->cfqhe", False: "cphfg,cfphe->cgphe"}
GELU_COEFF = 0.7978845608028654
CUBIC_COEFF = 0.044715


def layer_norm(stream):
    centre = stream - jnp.mean(stream, axis=-1, keepdims=True)
    inv_scale = lax.rsqrt(jnp.mean(centre * centre, axis=-1, keepdims=True) + 1e-06)
    return (centre * inv_scale, inv_scale)


def norm_back(normed, inv_scale, upstream):
    return inv_scale * (
        upstream
        - jnp.mean(upstream, axis=-1, keepdims=True)
        - normed * jnp.mean(upstream * normed, axis=-1, keepdims=True)
    )


def gelu_tanh(inputs):
    return (
        0.5
        * inputs
        * (1.0 + jnp.tanh(GELU_COEFF * (inputs + CUBIC_COEFF * inputs * inputs * inputs)))
    )


def gelu_slope(inputs):
    tangent = jnp.tanh(GELU_COEFF * (inputs + CUBIC_COEFF * inputs * inputs * inputs))
    return 0.5 * (1.0 + tangent) + 0.5 * inputs * (1.0 - tangent * tangent) * GELU_COEFF * (
        1.0 + 3.0 * CUBIC_COEFF * inputs * inputs
    )


def choose(modulation, column):
    return modulation[:, column][:, None, None, :]


def split_heads(projected):
    leading = projected.shape[:3]
    row_width = projected.shape[-1]
    head_count = row_width // HD
    queries = projected[:, :, :, 0].reshape(leading + (head_count, HD))
    key_rows = projected[:, :, :, 1].reshape(leading + (head_count, HD))
    values = projected[:, :, :, 2].reshape(leading + (head_count, HD))
    return (queries, key_rows, values, leading, row_width)


def attend(projected, spatial):
    queries, key_rows, values, leading, row_width = split_heads(projected)
    scores = jnp.einsum(
        SCORE_FORMS[spatial], queries, key_rows, preferred_element_type=jnp.float32
    ) * HD ** (-0.5)
    highest = jnp.max(scores, axis=-1, keepdims=True)
    expo = jnp.exp(scores - highest)
    denominator = jnp.sum(expo, axis=-1, keepdims=True)
    probs = (expo / denominator).astype(jnp.bfloat16)
    log_total = highest + jnp.log(denominator)
    attended = jnp.einsum(APPLY_FORMS[spatial], probs, values, preferred_element_type=jnp.float32)
    return (attended.reshape(leading + (row_width,)).astype(jnp.bfloat16), log_total)


def attend_back(projected, log_total, d_attended, spatial):
    queries, key_rows, values, leading, row_width = split_heads(projected)
    scale_factor = HD ** (-0.5)
    scores = (
        jnp.einsum(SCORE_FORMS[spatial], queries, key_rows, preferred_element_type=jnp.float32)
        * scale_factor
    )
    probs = jnp.exp(scores - log_total)
    upstream = d_attended.reshape(leading + (row_width // HD, HD))
    d_probs = jnp.einsum(SCORE_FORMS[spatial], upstream, values, preferred_element_type=jnp.float32)
    d_values = jnp.einsum(
        BACK_FORMS[spatial],
        probs.astype(jnp.bfloat16),
        upstream,
        preferred_element_type=jnp.float32,
    )
    row_inner = jnp.sum(probs * d_probs, axis=-1, keepdims=True)
    d_scores = (probs * (d_probs - row_inner)).astype(jnp.bfloat16)
    d_queries = (
        jnp.einsum(APPLY_FORMS[spatial], d_scores, key_rows, preferred_element_type=jnp.float32)
        * scale_factor
    )
    d_keys = (
        jnp.einsum(BACK_FORMS[spatial], d_scores, queries, preferred_element_type=jnp.float32)
        * scale_factor
    )
    stacked = jnp.stack([d_queries, d_keys, d_values], axis=3)
    return stacked.reshape(leading + (3, row_width)).astype(jnp.bfloat16)


def fetch_weights(weights):
    cast = tuple((weight.astype(jnp.bfloat16) for weight in weights))
    return (
        lax.all_gather(cast[0], SHARDS, axis=0, tiled=True),
        lax.all_gather(cast[1], SHARDS, axis=0, tiled=True),
        lax.all_gather(cast[2], SHARDS, axis=1, tiled=True),
        lax.all_gather(cast[3], SHARDS, axis=0, tiled=True),
        lax.all_gather(cast[4], SHARDS, axis=1, tiled=True),
    )


def backward_weights(weights):
    cast = tuple((weight.astype(jnp.bfloat16) for weight in weights))
    return (
        lax.all_gather(cast[0], SHARDS, axis=0, tiled=True),
        lax.all_gather(cast[1], SHARDS, axis=0, tiled=True),
        lax.all_gather(cast[2], SHARDS, axis=1, tiled=True),
        lax.all_gather(cast[3], SHARDS, axis=0, tiled=True),
        lax.all_gather(cast[4], SHARDS, axis=1, tiled=True),
    )


def spread_rows(rows):
    return lax.all_gather(rows, TENSOR, axis=2, tiled=True)


def collect_rows(term):
    return lax.psum_scatter(term, TENSOR, scatter_dimension=2, tiled=True)


def attention_output(attended, attn_weight):
    return collect_rows(
        jnp.einsum("cfpz,zd->cfpd", attended, attn_weight, preferred_element_type=jnp.float32)
    )


def layer_forward(stream, silu_cond, gathered, spatial):
    mod_weight, qkv_weight, attn_weight, up_weight, down_weight = gathered
    partial_value = jnp.einsum(
        "cd,dkz->ckz", silu_cond, mod_weight, preferred_element_type=jnp.float32
    )
    modulation = lax.all_gather(partial_value, TENSOR, axis=2, tiled=True)
    normed, inv_scale = layer_norm(stream)
    modulated = (normed * (1.0 + choose(modulation, 1)) + choose(modulation, 0)).astype(
        jnp.bfloat16
    )
    gathered_rows = spread_rows(modulated)
    projected = jnp.einsum(
        "cfpd,dkz->cfpkz", gathered_rows, qkv_weight, preferred_element_type=jnp.float32
    ).astype(jnp.bfloat16)
    if spatial:
        project_held = projected
        attended, log_total = attend(project_held, True)
    else:
        project_held = lax.all_to_all(projected, FRAME, split_axis=2, concat_axis=1, tiled=True)
        placed, log_total = attend(project_held, False)
        attended = lax.all_to_all(placed, FRAME, split_axis=1, concat_axis=2, tiled=True)
    branch_attn = attention_output(attended, attn_weight)
    middle = stream + choose(modulation, 2) * branch_attn
    normed_mlp, inv_mlp = layer_norm(middle)
    modulated_mlp = (normed_mlp * (1.0 + choose(modulation, 4)) + choose(modulation, 3)).astype(
        jnp.bfloat16
    )
    gathered_mlp = spread_rows(modulated_mlp)
    hidden_pre = jnp.einsum(
        "cfpd,dz->cfpz", gathered_mlp, up_weight, preferred_element_type=jnp.float32
    )
    hidden_act = gelu_tanh(hidden_pre).astype(jnp.bfloat16)
    branch_mlp = collect_rows(
        jnp.einsum("cfpz,zd->cfpd", hidden_act, down_weight, preferred_element_type=jnp.float32)
    )
    result = middle + choose(modulation, 5) * branch_mlp
    stored = (
        modulation,
        normed,
        inv_scale,
        gathered_rows,
        project_held,
        log_total,
        attended,
        branch_attn,
        normed_mlp,
        inv_mlp,
        gathered_mlp,
        hidden_pre,
        hidden_act,
        branch_mlp,
    )
    return (result, stored)


def layer_backward(upstream, silu_cond, gathered, stored, spatial):
    mod_weight, qkv_weight, attn_weight, up_weight, down_weight = gathered
    (
        modulation,
        normed,
        inv_scale,
        gathered_rows,
        project_held,
        log_total,
        attended,
        branch_attn,
        normed_mlp,
        inv_mlp,
        gathered_mlp,
        hidden_pre,
        hidden_act,
        branch_mlp,
    ) = stored
    d_branch_mlp = (upstream * choose(modulation, 5)).astype(jnp.bfloat16)
    d_gate_mlp = jnp.sum(upstream * branch_mlp, axis=(1, 2))
    d_branch_all = spread_rows(d_branch_mlp)
    grad_down = jnp.einsum(
        "cfpz,cfpd->zd", hidden_act, d_branch_all, preferred_element_type=jnp.float32
    )
    d_act = jnp.einsum(
        "cfpd,zd->cfpz", d_branch_all, down_weight, preferred_element_type=jnp.float32
    )
    d_pre = (d_act * gelu_slope(hidden_pre)).astype(jnp.bfloat16)
    grad_up = jnp.einsum("cfpd,cfpz->dz", gathered_mlp, d_pre, preferred_element_type=jnp.float32)
    d_mod_mlp = collect_rows(
        jnp.einsum("cfpz,dz->cfpd", d_pre, up_weight, preferred_element_type=jnp.float32)
    )
    d_shift_mlp = jnp.sum(d_mod_mlp, axis=(1, 2))
    d_scale_mlp = jnp.sum(d_mod_mlp * normed_mlp, axis=(1, 2))
    d_middle = upstream + norm_back(normed_mlp, inv_mlp, d_mod_mlp * (1.0 + choose(modulation, 4)))
    d_branch_attn = (d_middle * choose(modulation, 2)).astype(jnp.bfloat16)
    d_gate_attn = jnp.sum(d_middle * branch_attn, axis=(1, 2))
    d_attn_all = spread_rows(d_branch_attn)
    grad_attn = jnp.einsum(
        "cfpz,cfpd->zd", attended, d_attn_all, preferred_element_type=jnp.float32
    )
    d_attended = jnp.einsum(
        "cfpd,zd->cfpz", d_attn_all, attn_weight, preferred_element_type=jnp.float32
    ).astype(jnp.bfloat16)
    if spatial:
        d_projected = attend_back(project_held, log_total, d_attended, True)
    else:
        d_placed = lax.all_to_all(d_attended, FRAME, split_axis=2, concat_axis=1, tiled=True)
        d_projected = lax.all_to_all(
            attend_back(project_held, log_total, d_placed, False),
            FRAME,
            split_axis=1,
            concat_axis=2,
            tiled=True,
        )
    grad_qkv = jnp.einsum(
        "cfpd,cfpkz->dkz", gathered_rows, d_projected, preferred_element_type=jnp.float32
    )
    d_modulated = collect_rows(
        jnp.einsum("cfpkz,dkz->cfpd", d_projected, qkv_weight, preferred_element_type=jnp.float32)
    )
    d_shift_attn = jnp.sum(d_modulated, axis=(1, 2))
    d_scale_attn = jnp.sum(d_modulated * normed, axis=(1, 2))
    d_stream = d_middle + norm_back(normed, inv_scale, d_modulated * (1.0 + choose(modulation, 1)))
    d_modulation = jnp.stack(
        [d_shift_attn, d_scale_attn, d_gate_attn, d_shift_mlp, d_scale_mlp, d_gate_mlp], axis=1
    )
    d_mod_own = lax.psum_scatter(d_modulation, TENSOR, scatter_dimension=2, tiled=True)
    grad_mod = jnp.einsum(
        "cd,ckz->dkz", silu_cond.astype(jnp.float32), d_mod_own, precision=HIGHEST_PRECISION
    )
    d_silu = jnp.einsum(
        "ckz,dkz->cd", d_mod_own, mod_weight.astype(jnp.float32), precision=HIGHEST_PRECISION
    )
    grads = (
        lax.psum_scatter(
            grad_mod.astype(jnp.bfloat16), SHARDS, scatter_dimension=0, tiled=True
        ).astype(jnp.float32),
        lax.psum_scatter(
            grad_qkv.astype(jnp.bfloat16), SHARDS, scatter_dimension=0, tiled=True
        ).astype(jnp.float32),
        lax.psum_scatter(
            grad_attn.astype(jnp.bfloat16), SHARDS, scatter_dimension=1, tiled=True
        ).astype(jnp.float32),
        lax.psum_scatter(
            grad_up.astype(jnp.bfloat16), SHARDS, scatter_dimension=0, tiled=True
        ).astype(jnp.float32),
        lax.psum_scatter(
            grad_down.astype(jnp.bfloat16), SHARDS, scatter_dimension=1, tiled=True
        ).astype(jnp.float32),
    )
    return (d_stream, d_silu, grads)


def local(
    x_in,
    cond,
    mod_weight_one,
    qkv_weight_one,
    attn_out_one,
    mlp_up_one,
    mlp_down_one,
    mod_weight_two,
    qkv_weight_two,
    attn_out_two,
    mlp_up_two,
    mlp_down_two,
    out_cotangent,
):
    weights_first = (mod_weight_one, qkv_weight_one, attn_out_one, mlp_up_one, mlp_down_one)
    weights_second = (mod_weight_two, qkv_weight_two, attn_out_two, mlp_up_two, mlp_down_two)
    cond_float = cond.astype(jnp.float32)
    silu_cond = jax.nn.silu(cond_float).astype(jnp.bfloat16)
    gathered_first = fetch_weights(weights_first)
    middle_stream, stored_first = layer_forward(
        x_in.astype(jnp.float32), silu_cond, gathered_first, True
    )
    gathered_second = fetch_weights(weights_second)
    result, stored_second = layer_forward(middle_stream, silu_cond, gathered_second, False)
    back_second = backward_weights(weights_second)
    d_middle_stream, d_silu_second, grads_second = layer_backward(
        out_cotangent.astype(jnp.float32), silu_cond, back_second, stored_second, False
    )
    back_first = backward_weights(weights_first)
    input_grad, d_silu_first, grads_first = layer_backward(
        d_middle_stream, silu_cond, back_first, stored_first, True
    )
    d_silu_total = lax.psum(d_silu_first + d_silu_second, (FRAME, TENSOR))
    sigmoid_cond = jax.nn.sigmoid(cond_float)
    cond_grad = d_silu_total * (sigmoid_cond * (1.0 + cond_float * (1.0 - sigmoid_cond)))
    return (
        result.astype(jnp.bfloat16),
        input_grad,
        cond_grad,
        grads_first[0],
        grads_first[1],
        grads_first[2],
        grads_first[3],
        grads_first[4],
        grads_second[0],
        grads_second[1],
        grads_second[2],
        grads_second[3],
        grads_second[4],
    )

def flip(array, axis, bit):
    count = lax.axis_size(axis)
    return lax.ppermute(array, axis, [(i, i ^ bit) for i in range(count)])


def first_flip(shard):
    return 2 if shard % 2 == 0 else 4


def hop(array, which):
    if which == 0:
        pairs = [(i, i ^ 1) for i in range(8)]
    elif which == 1:
        pairs = [(i, i ^ first_flip(i)) for i in range(8)]
    else:
        pairs = [(i, i ^ (6 - first_flip(i))) for i in range(8)]
    return lax.ppermute(array, SHARDS, pairs)


class Line:
    def __init__(self):
        self.last = ()
        self.awaited = []
        self.under_way = []
        self.under_way_next = []

    def held(self, value):
        return lax.optimization_barrier((value, self.last, self.awaited))[0]

    def __call__(self, work, *inputs):
        self.last = work(*self.held(inputs))
        self.awaited = []
        return self.last

    def wait(self, value):
        self.awaited.append(value)
        return value

    def send(self, array, move):
        self.under_way.append(move(self.held(array)))
        return self.under_way[-1]

    def hop(self, array, which):
        return self.send(array, lambda held: hop(held, which))

    def exchange_sum(self, array, axis):
        bit = 1
        while bit < lax.axis_size(axis):
            array = self(jnp.add, array, flip(array, axis, bit))
            bit *= 2
        return array

    def place_along(self, array, axis):
        count = lax.axis_size(axis)
        own = (jnp.arange(count) == lax.axis_index(axis)).reshape((count,) + (1,) * array.ndim)
        return self.exchange_sum(jnp.where(own, array[None], 0.0), axis)

    def send_ahead(self, array, move):
        self.under_way_next.append(move(self.held(array)))
        return self.under_way_next[-1]

    def tick(self):
        self.awaited += self.under_way
        self.under_way = self.under_way_next
        self.under_way_next = []


def shard_index():
    return lax.axis_index(CLIP) * lax.axis_size(FRAME) + lax.axis_index(FRAME)


def piece_order():
    shard = shard_index()
    first = jnp.where(shard % 2 == 0, 2, 4)
    second = 6 - first
    masks = [0, first, second, 6, 1, 1 ^ second, 1 ^ first, 7]
    return jnp.stack([shard ^ mask for mask in masks]).astype(jnp.int32)


class Gather:
    def __init__(self, line, piece):
        self.line = line
        self.whole = lax.all_gather(piece, TENSOR, axis=0, tiled=False)

    def soon(self):
        self.line.under_way.append(self.whole)

    def send(self):
        self.line.wait(self.whole)
        self.near = self.line.hop(self.whole, 1)

    def relay(self):
        self.pair = self.line(lambda *pair: jnp.stack(pair), self.whole, self.near)
        self.far = self.line.hop(self.pair, 2)
        self.other_pair = self.line.hop(self.pair, 0)

    def end(self):
        other_far = self.line.hop(self.far, 0)
        self.pieces = (self.pair, self.far, self.other_pair, other_far)


def wide(array):
    return array.astype(jnp.float32)


def low(array):
    return array.astype(jnp.bfloat16)


def total(*arrays):
    return low(sum(wide(array) for array in arrays))


class Scatter:
    def __init__(self, line, grad):
        self.line = line
        self.keep, away = grad
        self.far = line.send_ahead(away, lambda held: hop(held, 2))

    def relay(self):
        work = lambda keep, far: total(keep[1], far[1])
        self.near = self.line.hop(self.line(work, self.keep, self.far), 1)

    def finish(self):
        work = lambda keep, far, near: total(keep[0], far[0], near)
        own = self.line(work, self.keep, self.far, self.near)
        self.piece = lax.psum_scatter(own, TENSOR, scatter_dimension=0, tiled=False)


def pack_layer(weights):
    qkv, attn, up, down = (weight.astype(jnp.bfloat16) for weight in weights)
    rows = qkv.shape[0]
    attn_part = jnp.concatenate([qkv.reshape(rows, -1), attn.T], axis=1)
    return attn_part, up, down.T


PIECES = 8
PAIRS = 4
VMEM_BYTES = 48 << 20
COST_SHARE = 8


def contract(left, right, left_dim, right_dim):
    return lax.dot_general(
        left, right, (((left_dim,), (right_dim,)), ((), ())), preferred_element_type=jnp.float32
    )


def assemble(order_ref, piece_refs, whole_ref):
    rows = piece_refs[0].shape[2]
    for j in range(PIECES):
        start = pl.multiple_of(order_ref[j] * rows, 16)
        whole_ref[pl.ds(start, rows), :] = piece_refs[j // 2][j % 2, 0]


def up_kernel(order_ref, x_ref, *refs):
    pre_ref, act_ref, whole_ref = refs[PAIRS:]
    assemble(order_ref, refs[:PAIRS], whole_ref)
    pre = contract(x_ref[...], whole_ref[...], 1, 0)
    pre_ref[...] = pre
    act_ref[...] = gelu_tanh(pre).astype(jnp.bfloat16)


def slope_kernel(order_ref, x_ref, pre_ref, *refs):
    out_ref, whole_ref = refs[PAIRS:]
    assemble(order_ref, refs[:PAIRS], whole_ref)
    d_act = contract(x_ref[...], whole_ref[...], 1, 0)
    out_ref[...] = (d_act * gelu_slope(pre_ref[...])).astype(jnp.bfloat16)


def turned_kernel(low, high, order_ref, x_ref, *refs):
    out_ref, whole_ref = refs[PAIRS:]
    assemble(order_ref, refs[:PAIRS], whole_ref)
    whole = contract(x_ref[...], whole_ref[...], 1, 0)
    out_ref[0] = whole[:, low:high].astype(jnp.bfloat16).T


def collect_kernel(low, high, turned, order_ref, y_ref, *refs):
    out_ref, whole_ref = refs[PAIRS:]
    assemble(order_ref, refs[:PAIRS], whole_ref)
    rows = y_ref[0].T if turned else y_ref[...]
    term = contract(rows, whole_ref[:, low:high], 1, 1)

    @pl.when(pl.program_id(0) == 0)
    def _():
        out_ref[...] = term

    @pl.when(pl.program_id(0) > 0)
    def _():
        out_ref[...] += term


def turn(order_ref, x_refs, whole_ref, turned_ref):
    rows, tokens = turned_ref.shape[0] * 2 // PIECES, turned_ref.shape[1] // 2
    for side in range(2):
        whole_ref[...] = x_refs[side][...].T
        for j in range(PIECES // 2):
            start = pl.multiple_of(order_ref[j] * rows, 16)
            turned_ref[pl.ds(j * rows, rows), pl.ds(side * tokens, tokens)] = whole_ref[
                pl.ds(start, rows), :
            ]


def deal_out(grad, *out_refs):
    rows = out_refs[0].shape[2]
    for j in range(PIECES // 2):
        out_refs[j // 2][j % 2, 0] = grad[j * rows : (j + 1) * rows]


def grad_kernel(order_ref, x_ref, x_other, y_ref, y_other, *refs):
    whole_ref, turned_ref = refs[2:]

    @pl.when(pl.program_id(0) == 0)
    def _():
        turn(order_ref, (x_ref, x_other), whole_ref, turned_ref)

    tokens = x_ref.shape[0]
    grad = contract(turned_ref[:, :tokens], y_ref[...], 1, 0)
    grad += contract(turned_ref[:, tokens:], y_other[...], 1, 0)
    deal_out(grad.astype(jnp.bfloat16), *refs[:2])


def attn_grad_kernel(order_ref, *refs):
    x_refs, b_refs, y_refs, a_refs = (refs[2 * j : 2 * j + 2] for j in range(4))
    out_refs, (whole_ref, x_turned, b_turned, grad_ref) = refs[8:10], refs[10:]

    @pl.when(pl.program_id(0) == 0)
    def _():
        turn(order_ref, x_refs, whole_ref, x_turned)
        turn(order_ref, b_refs, whole_ref, b_turned)

    tokens, split = y_refs[0].shape[2], y_refs[0].shape[1]
    for turned, pair, lanes in (
        (x_turned, y_refs, slice(0, split)),
        (b_turned, a_refs, slice(split, grad_ref.shape[1])),
    ):
        grad = contract(turned[:, :tokens], pair[0][0], 1, 1)
        grad += contract(turned[:, tokens:], pair[1][0], 1, 1)
        grad_ref[:, lanes] = grad.astype(jnp.bfloat16)
    deal_out(grad_ref[...], *out_refs)


def masked_scores(queries, keys, group):
    scores = contract(queries, keys, 0, 0) * HD ** (-0.5)
    if group:
        place = lax.broadcasted_iota(jnp.int32, scores.shape, 0) % group
        other = lax.broadcasted_iota(jnp.int32, scores.shape, 1) % group
        scores = jnp.where(place == other, scores, -3e38)
    expo = jnp.exp(scores - jnp.max(scores, axis=-1, keepdims=True))
    return expo / jnp.sum(expo, axis=-1, keepdims=True)


def attend_kernel(group, projected_ref, out_ref):
    part = out_ref.shape[1]
    for start in range(0, part, HD):
        queries, keys, values = (
            projected_ref[0, pl.ds(j * part + start, HD), :] for j in range(3)
        )
        probs = masked_scores(queries, keys, group).astype(jnp.bfloat16)
        out_ref[0, pl.ds(start, HD), :] = contract(values, probs, 1, 1).astype(jnp.bfloat16)


def attend_back_kernel(group, projected_ref, upstream_ref, out_ref):
    part = upstream_ref.shape[1]
    scale_factor = HD ** (-0.5)
    for start in range(0, part, HD):
        queries, keys, values = (
            projected_ref[0, pl.ds(j * part + start, HD), :] for j in range(3)
        )
        upstream = upstream_ref[0, pl.ds(start, HD), :]
        probs = masked_scores(queries, keys, group)
        d_probs = contract(upstream, values, 0, 0)
        row_inner = jnp.sum(probs * d_probs, axis=-1, keepdims=True)
        d_scores = (probs * (d_probs - row_inner)).astype(jnp.bfloat16)
        grads = (
            contract(keys, d_scores, 1, 1) * scale_factor,
            contract(queries, d_scores, 1, 0) * scale_factor,
            contract(upstream, probs.astype(jnp.bfloat16), 1, 0),
        )
        for j in range(3):
            out_ref[0, pl.ds(j * part + start, HD), :] = grads[j].astype(jnp.bfloat16)


def call(kernel, grid, in_specs, out_specs, out_shape, scratch, flops, args):
    moved = sum(a.size * a.dtype.itemsize for a in args)
    moved += sum(o.size * o.dtype.itemsize for o in jax.tree.leaves(out_shape))
    return pl.pallas_call(
        kernel,
        out_shape=out_shape,
        grid_spec=pltpu.PrefetchScalarGridSpec(
            num_scalar_prefetch=1 if scratch else 0,
            grid=grid,
            in_specs=in_specs,
            out_specs=out_specs,
            scratch_shapes=scratch,
        ),
        compiler_params=pltpu.CompilerParams(vmem_limit_bytes=VMEM_BYTES),
        cost_estimate=pl.CostEstimate(
            flops=flops // COST_SHARE, bytes_accessed=moved // COST_SHARE, transcendentals=0
        ),
    )(*args)


def still(shape):
    return pl.BlockSpec(shape, lambda z, *_: (0,) * len(shape))


def lead(shape):
    return pl.BlockSpec((1,) + shape, lambda z, *_: (z,) + (0,) * len(shape))


def column(tokens, width):
    return pl.BlockSpec((tokens, width), lambda z, *_: (0, z))


def sizes(pieces):
    _, groups, rows, width = pieces[0].shape
    return groups, rows, width, rows * PIECES


def pair_specs(rows, width, count):
    return [pl.BlockSpec((2, 1, rows, width), lambda z, *_: (0, z, 0, 0))] * count


def times_up(order, x, pieces):
    groups, rows, width, depth = sizes(pieces)
    tokens = x.shape[0]
    shape = (tokens, groups * width)
    return call(
        up_kernel,
        (groups,),
        [still(x.shape)] + pair_specs(rows, width, PAIRS),
        [column(tokens, width)] * 2,
        [jax.ShapeDtypeStruct(shape, jnp.float32), jax.ShapeDtypeStruct(shape, jnp.bfloat16)],
        [pltpu.VMEM((depth, width), jnp.bfloat16)],
        2 * tokens * depth * width * groups,
        (order, x) + pieces,
    )


def times_slope(order, x, pre, pieces):
    groups, rows, width, depth = sizes(pieces)
    tokens = x.shape[0]
    return call(
        slope_kernel,
        (groups,),
        [still(x.shape), column(tokens, width)] + pair_specs(rows, width, PAIRS),
        column(tokens, width),
        jax.ShapeDtypeStruct(pre.shape, jnp.bfloat16),
        [pltpu.VMEM((depth, width), jnp.bfloat16)],
        2 * tokens * depth * width * groups,
        (order, x, pre) + pieces,
    )


def times_turned(order, x, pieces, low, high):
    groups, rows, width, depth = sizes(pieces)
    tokens = x.shape[0]
    return call(
        functools.partial(turned_kernel, low, high),
        (groups,),
        [still(x.shape)] + pair_specs(rows, width, PAIRS),
        lead((high - low, tokens)),
        jax.ShapeDtypeStruct((groups, high - low, tokens), jnp.bfloat16),
        [pltpu.VMEM((depth, width), jnp.bfloat16)],
        2 * tokens * depth * width * groups,
        (order, x) + pieces,
    )


def collect(order, y, pieces, low, high, turned):
    groups, rows, width, depth = sizes(pieces)
    tokens = y.shape[2] if turned else y.shape[0]
    return call(
        functools.partial(collect_kernel, low, high, turned),
        (groups,),
        [lead(y.shape[1:]) if turned else column(tokens, width)]
        + pair_specs(rows, width, PAIRS),
        still((tokens, depth)),
        jax.ShapeDtypeStruct((tokens, depth), jnp.float32),
        [pltpu.VMEM((depth, width), jnp.bfloat16)],
        2 * tokens * depth * (high - low) * groups,
        (order, y) + pieces,
    )


def grad_call(kernel, args, specs, groups, depth, width, scratch):
    rows = depth // PIECES
    tokens = args[1].shape[0]
    return call(
        kernel,
        (groups,),
        specs,
        pair_specs(rows, width, 2),
        [jax.ShapeDtypeStruct((2, groups, rows, width), jnp.bfloat16)] * 2,
        [pltpu.VMEM((depth, tokens), jnp.bfloat16)]
        + [pltpu.VMEM(shape, jnp.bfloat16) for shape in scratch],
        2 * tokens * depth * width * groups,
        args,
    )


def grad_of(order, x, x_other, y, y_other, groups):
    tokens, width = x.shape[0], y.shape[1] // groups
    depth = x.shape[1]
    specs = [still(x.shape)] * 2 + [column(tokens, width)] * 2
    args = (order, x, x_other, y, y_other)
    scratch = [(depth // 2, 2 * tokens)]
    return grad_call(grad_kernel, args, specs, groups, depth, width, scratch)


def attn_grad_of(order, *args):
    x, y, a = args[0], args[4], args[6]
    groups, wide_part, tokens = y.shape
    part, depth = a.shape[1], x.shape[1]
    specs = [still(x.shape)] * 4 + [lead((wide_part, tokens))] * 2 + [lead((part, tokens))] * 2
    scratch = [(depth // 2, 2 * tokens)] * 2 + [(depth // 2, wide_part + part)]
    return grad_call(
        attn_grad_kernel, (order, *args), specs, groups, depth, wide_part + part, scratch
    )


def attend_call(projected, group):
    groups, wide, tokens = projected.shape
    part = wide // 3
    return call(
        functools.partial(attend_kernel, group),
        (groups,),
        [lead((wide, tokens))],
        lead((part, tokens)),
        jax.ShapeDtypeStruct((groups, part, tokens), jnp.bfloat16),
        [],
        4 * tokens * tokens * part * groups,
        (projected,),
    )


def attend_back_call(projected, upstream, group):
    groups, wide, tokens = projected.shape
    part = wide // 3
    return call(
        functools.partial(attend_back_kernel, group),
        (groups,),
        [lead((wide, tokens)), lead((part, tokens))],
        lead((wide, tokens)),
        jax.ShapeDtypeStruct((groups, wide, tokens), jnp.bfloat16),
        [],
        10 * tokens * tokens * part * groups,
        (projected, upstream),
    )


class Layer:
    def __init__(self, line, order, modulation, group):
        self.line = line
        self.order = order
        self.modulation = modulation
        self.group = group
        self.others = {}

    def share(self, *arrays):
        for array in arrays:
            self.others[id(array)] = self.line.hop(array, 0)

    def both(self, array):
        return array, self.others[id(array)]

    def project(self, stream, attn):
        self.stream = stream
        self.attn = attn
        self.width = attn[0].shape[-1]
        self.part = self.width // 4
        rows = self.modulation

        def work(stream, attn):
            normed, inv_scale = layer_norm(stream)
            modulated = low(normed * (1.0 + rows[1]) + rows[0])
            projected = times_turned(self.order, modulated, attn, 0, 3 * self.part)
            return normed, inv_scale, modulated, projected

        made = self.line(work, stream, attn)
        self.normed, self.inv_scale, self.modulated, self.projected = made

    def attend(self):
        self.attended = self.line(
            lambda projected: attend_call(projected, self.group), self.projected
        )

    def attention_out(self):
        rows = self.modulation

        def work(attended, stream, attn):
            branch_attn = collect(self.order, attended, attn, 3 * self.part, self.width, True)
            middle = stream + rows[2] * branch_attn
            normed_mlp, inv_mlp = layer_norm(middle)
            modulated_mlp = low(normed_mlp * (1.0 + rows[4]) + rows[3])
            return branch_attn, middle, normed_mlp, inv_mlp, modulated_mlp

        made = self.line(work, self.attended, self.stream, self.attn)
        self.branch_attn, self.middle, self.normed_mlp, self.inv_mlp, self.modulated_mlp = made

    def mlp_up(self, up):
        self.up = up
        work = lambda rows, up: times_up(self.order, rows, up)
        self.hidden_pre, self.hidden_act = self.line(work, self.modulated_mlp, up)

    def mlp_down(self, down, last):
        rows = self.modulation

        def work(act, middle, down):
            branch_mlp = collect(self.order, act, down, 0, self.width, False)
            return branch_mlp, last(middle + rows[5] * branch_mlp)

        self.branch_mlp, result = self.line(work, self.hidden_act, self.middle, down)
        return result

    def turn_back(self, upstream):
        rows = self.modulation
        self.upstream = upstream
        self.d_branch_mlp = self.line(lambda rows_in: low(rows_in * rows[5]), upstream)

    def gradient(self, *args):
        groups = self.attn[0].shape[1]
        work = lambda *rows: grad_of(self.order, *rows, groups)
        return Scatter(self.line, self.line(work, *args))

    def grad_down(self):
        return self.gradient(*self.both(self.d_branch_mlp), *self.both(self.hidden_act))

    def slope(self, down):
        work = lambda rows, pre, down: times_slope(self.order, rows, pre, down)
        self.d_pre = self.line(work, self.d_branch_mlp, self.hidden_pre, down)

    def grad_up(self):
        return self.gradient(*self.both(self.modulated_mlp), *self.both(self.d_pre))

    def back_up(self):
        rows = self.modulation

        def work(d_pre, upstream, normed, inv_mlp, up):
            d_mod_mlp = collect(self.order, d_pre, up, 0, self.width, False)
            d_middle = upstream + norm_back(normed, inv_mlp, d_mod_mlp * (1.0 + rows[4]))
            return d_mod_mlp, d_middle, low(d_middle * rows[2])

        made = self.line(
            work, self.d_pre, self.upstream, self.normed_mlp, self.inv_mlp, self.up
        )
        self.d_mod_mlp, self.d_middle, self.d_branch_attn = made

    def back_out(self):
        work = lambda rows, attn: times_turned(
            self.order, rows, attn, 3 * self.part, self.width
        )
        self.d_attended = self.line(work, self.d_branch_attn, self.attn)

    def back_attend(self):
        work = lambda projected, upstream: attend_back_call(projected, upstream, self.group)
        self.d_projected = self.line(work, self.projected, self.d_attended)

    def grad_attn(self):
        work = lambda *rows: attn_grad_of(self.order, *rows)
        rows = (self.modulated, self.d_branch_attn, self.d_projected, self.attended)
        grad = self.line(work, *(one for array in rows for one in self.both(array)))
        return Scatter(self.line, grad)

    def back_project(self, last):
        rows = self.modulation

        def work(d_projected, d_middle, normed, inv_scale, attn):
            d_modulated = collect(self.order, d_projected, attn, 0, 3 * self.part, True)
            back = norm_back(normed, inv_scale, d_modulated * (1.0 + rows[1]))
            return d_modulated, last(d_middle + back)

        self.d_modulated, result = self.line(
            work, self.d_projected, self.d_middle, self.normed, self.inv_scale, self.attn
        )
        return result

    def d_modulation(self):
        terms = (
            self.d_modulated,
            self.d_modulated * self.normed,
            self.d_middle * self.branch_attn,
            self.d_mod_mlp,
            self.d_mod_mlp * self.normed_mlp,
            self.upstream * self.branch_mlp,
        )
        return jnp.stack([jnp.sum(term, axis=0) for term in terms])


def finish_grads(attn_piece, up_piece, down_piece):
    rows, width = attn_piece.shape
    part = width // 4
    qkv = attn_piece[:, : 3 * part].reshape(rows, 3, part).astype(jnp.float32)
    attn = attn_piece[:, 3 * part :].T.astype(jnp.float32)
    return qkv, attn, up_piece.astype(jnp.float32), down_piece.T.astype(jnp.float32)


def deal_rows(rows, axes):
    return lax.all_to_all(rows, axes, split_axis=0, concat_axis=0, tiled=True)


def swap_blocks(rows, outer, inner):
    return rows.reshape(outer, inner, -1, rows.shape[1]).swapaxes(0, 1).reshape(rows.shape)


def local_whole(
    x_in,
    cond,
    mod_weight_one,
    qkv_weight_one,
    attn_out_one,
    mlp_up_one,
    mlp_down_one,
    mod_weight_two,
    qkv_weight_two,
    attn_out_two,
    mlp_up_two,
    mlp_down_two,
    out_cotangent,
):
    rows, _, part = qkv_weight_one.shape
    width = x_in.shape[-1]
    packed = [
        pack_layer((qkv_weight_one, attn_out_one, mlp_up_one, mlp_down_one)),
        pack_layer((qkv_weight_two, attn_out_two, mlp_up_two, mlp_down_two)),
    ]
    cond_every = lax.all_gather(cond, CLIP, axis=0, tiled=True).astype(jnp.float32)
    clip_count = cond_every.shape[0]
    silu_every = jax.nn.silu(cond_every).astype(jnp.bfloat16)
    silu_rows = lax.dynamic_slice_in_dim(silu_every, shard_index() * rows, rows, axis=1)
    mod_weights = (mod_weight_one.astype(jnp.bfloat16), mod_weight_two.astype(jnp.bfloat16))
    partial_value = jnp.stack(
        [
            jnp.einsum("cd,dkz->ckz", silu_rows, weight, preferred_element_type=jnp.float32)
            for weight in mod_weights
        ],
        axis=1,
    )
    devices, tensors = lax.axis_size(FRAME), lax.axis_size(TENSOR)
    own_frames = x_in.shape[1]
    own_places = x_in.shape[2] // devices
    cotangent = deal_rows(swap_blocks(out_cotangent.reshape(-1, width), own_frames, devices), FRAME)
    cotangent = swap_blocks(cotangent, devices, own_frames)
    line = Line()
    summed = line.exchange_sum(line.exchange_sum(partial_value, FRAME), CLIP)
    line.wait(cotangent)
    summed = lax.dynamic_index_in_dim(summed, lax.axis_index(CLIP), 0, keepdims=False)
    placed = line.place_along(summed, TENSOR)
    modulations = placed.transpose(1, 2, 0, 3).reshape(summed.shape[:2] + (-1,))

    order = piece_order()
    attn_one, up_one, down_one = (Gather(line, piece) for piece in packed[0])
    attn_two, up_two, down_two = (Gather(line, piece) for piece in packed[1])
    one = Layer(line, order, modulations[0], 0)
    two = Layer(line, order, modulations[1], own_places)

    line.wait(packed)
    attn_one.send()
    line.tick()
    attn_one.relay()
    up_one.send()
    down_one.soon()
    line.tick()
    attn_one.end()
    up_one.relay()
    down_one.send()
    frames_in = line.send(x_in.reshape(-1, width), lambda held: deal_rows(held, TENSOR))
    one.project(line(wide, frames_in), attn_one.pieces)
    one.attend()
    one.attention_out()
    attn_two.soon()
    line.tick()
    up_one.end()
    down_one.relay()
    attn_two.send()
    one.mlp_up(up_one.pieces)
    cotangent = line(wide, cotangent)
    up_two.soon()
    line.tick()
    down_one.end()
    attn_two.relay()
    up_two.send()
    down_two.soon()
    between = one.mlp_down(down_one.pieces, low)
    between = line.send(between, lambda held: deal_rows(held, (TENSOR, FRAME)))
    two.turn_back(cotangent)
    line.tick()
    attn_two.end()
    up_two.relay()
    down_two.send()
    two.share(two.d_branch_mlp)
    between = line(wide, between)
    two.project(between, attn_two.pieces)
    two.attend()
    two.attention_out()
    line.tick()
    up_two.end()
    down_two.relay()
    two.mlp_up(up_two.pieces)
    two.share(two.hidden_act)
    down_grad = two.grad_down()
    line.tick()
    down_two.end()
    two.share(two.modulated_mlp, two.modulated)
    two.slope(down_two.pieces)
    two.share(two.d_pre)
    two.back_up()
    up_grad = two.grad_up()
    line.tick()
    down_grad.relay()
    two.share(two.d_branch_attn, two.attended)
    two.back_out()
    two.back_attend()
    two.share(two.d_projected)
    d_second = two.back_project(low)
    d_second = line.send_ahead(d_second, lambda held: deal_rows(held, (TENSOR, FRAME)))
    attn_grad = two.grad_attn()
    line.tick()
    up_grad.relay()
    one.share(one.hidden_act, one.attended)
    d_second = line(wide, d_second)
    down_grad.finish()
    one.turn_back(d_second)
    one.share(one.d_branch_mlp)
    one.slope(down_one.pieces)
    down_last = one.grad_down()
    line.tick()
    attn_grad.relay()
    one.share(one.d_pre, one.modulated_mlp, one.modulated)
    up_grad.finish()
    one.back_up()
    up_last = one.grad_up()
    one.back_out()
    one.back_attend()
    line.tick()
    down_last.relay()
    one.share(one.d_branch_attn, one.d_projected)
    attn_grad.finish()
    d_first = one.back_project(low)
    result = two.mlp_down(
        down_two.pieces, lambda rows: swap_blocks(low(rows), own_frames, devices)
    )
    d_mods = line(lambda: jnp.stack([one.d_modulation(), two.d_modulation()]))
    d_mods = line(jnp.add, d_mods, flip(d_mods, FRAME, 1))
    attn_last = one.grad_attn()
    d_mods = line(jnp.add, d_mods, flip(d_mods, TENSOR, 1))
    near_mods = flip(d_mods, TENSOR, 2)
    line.tick()
    up_last.relay()
    down_last.finish()
    input_grad = deal_rows(d_first, TENSOR)
    line.under_way.append(input_grad)
    d_mods = line(jnp.add, d_mods, near_mods)
    near_mods = line.send(d_mods, lambda held: flip(held, FRAME, 2))
    line.tick()
    attn_last.relay()
    up_last.finish()
    input_grad = line(wide, input_grad).reshape(x_in.shape)
    line.tick()
    attn_last.finish()
    layer_out = swap_blocks(deal_rows(result, FRAME), devices, own_frames).reshape(x_in.shape)
    d_mods = line(jnp.add, d_mods, near_mods)
    d_mods = lax.dynamic_slice_in_dim(d_mods, lax.axis_index(TENSOR) * part, part, axis=2)
    d_every = line.place_along(d_mods, CLIP)
    silu_float = silu_rows.astype(jnp.float32)
    grad_mods = [
        sum(
            silu_float[c][:, None, None] * d_every[c, layer][None] for c in range(clip_count)
        )
        for layer in range(2)
    ]
    d_silu = jnp.stack(
        [
            sum(
                jnp.sum(
                    d_every[c, layer][None] * mod_weights[layer].astype(jnp.float32), axis=(1, 2)
                )
                for layer in range(2)
            )
            for c in range(clip_count)
        ]
    )
    d_silu = line.exchange_sum(d_silu, TENSOR)
    d_silu = line.place_along(line.place_along(d_silu, FRAME), CLIP)
    d_silu = d_silu.transpose(2, 0, 1, 3).reshape(clip_count, -1)
    d_silu = lax.dynamic_slice_in_dim(d_silu, lax.axis_index(CLIP), 1, axis=0)
    cond_float = cond.astype(jnp.float32)
    sigmoid_cond = jax.nn.sigmoid(cond_float)
    cond_grad = d_silu * (sigmoid_cond * (1.0 + cond_float * (1.0 - sigmoid_cond)))
    first_out = finish_grads(attn_last.piece, up_last.piece, down_last.piece)
    second_out = finish_grads(attn_grad.piece, up_grad.piece, down_grad.piece)
    return (
        layer_out,
        input_grad,
        cond_grad,
        grad_mods[0],
        *first_out,
        grad_mods[1],
        *second_out,
    )


def holds_whole(mesh):
    tensors = mesh.shape[TENSOR]
    return (
        mesh.shape[CLIP] == 2
        and mesh.shape[FRAME] == 4
        and FRAMES % (4 * tensors) == 0
        and tensors & (tensors - 1) == 0
    )


def solution(mesh):
    return jax.shard_map(
        local_whole if holds_whole(mesh) else local,
        mesh=mesh,
        in_specs=(
            P(CLIP, FRAME, TENSOR, None),
            P(CLIP, None),
            P(SHARDS, None, TENSOR),
            P(SHARDS, None, TENSOR),
            P(TENSOR, SHARDS),
            P(SHARDS, TENSOR),
            P(TENSOR, SHARDS),
            P(SHARDS, None, TENSOR),
            P(SHARDS, None, TENSOR),
            P(TENSOR, SHARDS),
            P(SHARDS, TENSOR),
            P(TENSOR, SHARDS),
            P(CLIP, FRAME, TENSOR, None),
        ),
        out_specs=(
            P(CLIP, FRAME, TENSOR, None),
            P(CLIP, FRAME, TENSOR, None),
            P(CLIP, None),
            P(SHARDS, None, TENSOR),
            P(SHARDS, None, TENSOR),
            P(TENSOR, SHARDS),
            P(SHARDS, TENSOR),
            P(TENSOR, SHARDS),
            P(SHARDS, None, TENSOR),
            P(SHARDS, None, TENSOR),
            P(TENSOR, SHARDS),
            P(SHARDS, TENSOR),
            P(TENSOR, SHARDS),
        ),
        check_vma=False,
    )
```

```python
import functools

import jax
import jax.numpy as jnp
from jax import lax
from jax.experimental import pallas as pl
from jax.experimental.pallas import tpu as pltpu
from jax.sharding import PartitionSpec as P

HD = 72
FRAMES = 16
CLIP, FRAME, TENSOR = "clip", "frame", "tensor"
SHARDS = (CLIP, FRAME)


HIGHEST_PRECISION = lax.Precision.HIGHEST
SCORE_FORMS = {True: "cfphe,cfqhe->cfhpq", False: "cfphe,cgphe->cphfg"}
APPLY_FORMS = {True: "cfhpq,cfqhe->cfphe", False: "cphfg,cgphe->cfphe"}
BACK_FORMS = {True: "cfhpq,cfphe->cfqhe", False: "cphfg,cfphe->cgphe"}
GELU_COEFF = 0.7978845608028654
CUBIC_COEFF = 0.044715


def layer_norm(stream):
    centre = stream - jnp.mean(stream, axis=-1, keepdims=True)
    inv_scale = lax.rsqrt(jnp.mean(centre * centre, axis=-1, keepdims=True) + 1e-06)
    return (centre * inv_scale, inv_scale)


def norm_back(normed, inv_scale, upstream):
    return inv_scale * (
        upstream
        - jnp.mean(upstream, axis=-1, keepdims=True)
        - normed * jnp.mean(upstream * normed, axis=-1, keepdims=True)
    )


def gelu_tanh(inputs):
    return (
        0.5
        * inputs
        * (1.0 + jnp.tanh(GELU_COEFF * (inputs + CUBIC_COEFF * inputs * inputs * inputs)))
    )


def gelu_slope(inputs):
    tangent = jnp.tanh(GELU_COEFF * (inputs + CUBIC_COEFF * inputs * inputs * inputs))
    return 0.5 * (1.0 + tangent) + 0.5 * inputs * (1.0 - tangent * tangent) * GELU_COEFF * (
        1.0 + 3.0 * CUBIC_COEFF * inputs * inputs
    )


def choose(modulation, column):
    return modulation[:, column][:, None, None, :]


def split_heads(projected):
    leading = projected.shape[:3]
    row_width = projected.shape[-1]
    head_count = row_width // HD
    queries = projected[:, :, :, 0].reshape(leading + (head_count, HD))
    key_rows = projected[:, :, :, 1].reshape(leading + (head_count, HD))
    values = projected[:, :, :, 2].reshape(leading + (head_count, HD))
    return (queries, key_rows, values, leading, row_width)


def attend(projected, spatial):
    queries, key_rows, values, leading, row_width = split_heads(projected)
    scores = jnp.einsum(
        SCORE_FORMS[spatial], queries, key_rows, preferred_element_type=jnp.float32
    ) * HD ** (-0.5)
    highest = jnp.max(scores, axis=-1, keepdims=True)
    expo = jnp.exp(scores - highest)
    denominator = jnp.sum(expo, axis=-1, keepdims=True)
    probs = (expo / denominator).astype(jnp.bfloat16)
    log_total = highest + jnp.log(denominator)
    attended = jnp.einsum(APPLY_FORMS[spatial], probs, values, preferred_element_type=jnp.float32)
    return (attended.reshape(leading + (row_width,)).astype(jnp.bfloat16), log_total)


def attend_back(projected, log_total, d_attended, spatial):
    queries, key_rows, values, leading, row_width = split_heads(projected)
    scale_factor = HD ** (-0.5)
    scores = (
        jnp.einsum(SCORE_FORMS[spatial], queries, key_rows, preferred_element_type=jnp.float32)
        * scale_factor
    )
    probs = jnp.exp(scores - log_total)
    upstream = d_attended.reshape(leading + (row_width // HD, HD))
    d_probs = jnp.einsum(SCORE_FORMS[spatial], upstream, values, preferred_element_type=jnp.float32)
    d_values = jnp.einsum(
        BACK_FORMS[spatial],
        probs.astype(jnp.bfloat16),
        upstream,
        preferred_element_type=jnp.float32,
    )
    row_inner = jnp.sum(probs * d_probs, axis=-1, keepdims=True)
    d_scores = (probs * (d_probs - row_inner)).astype(jnp.bfloat16)
    d_queries = (
        jnp.einsum(APPLY_FORMS[spatial], d_scores, key_rows, preferred_element_type=jnp.float32)
        * scale_factor
    )
    d_keys = (
        jnp.einsum(BACK_FORMS[spatial], d_scores, queries, preferred_element_type=jnp.float32)
        * scale_factor
    )
    stacked = jnp.stack([d_queries, d_keys, d_values], axis=3)
    return stacked.reshape(leading + (3, row_width)).astype(jnp.bfloat16)


def fetch_weights(weights):
    cast = tuple((weight.astype(jnp.bfloat16) for weight in weights))
    return (
        lax.all_gather(cast[0], SHARDS, axis=0, tiled=True),
        lax.all_gather(cast[1], SHARDS, axis=0, tiled=True),
        lax.all_gather(cast[2], SHARDS, axis=1, tiled=True),
        lax.all_gather(cast[3], SHARDS, axis=0, tiled=True),
        lax.all_gather(cast[4], SHARDS, axis=1, tiled=True),
    )


def backward_weights(weights):
    cast = tuple((weight.astype(jnp.bfloat16) for weight in weights))
    return (
        lax.all_gather(cast[0], SHARDS, axis=0, tiled=True),
        lax.all_gather(cast[1], SHARDS, axis=0, tiled=True),
        lax.all_gather(cast[2], SHARDS, axis=1, tiled=True),
        lax.all_gather(cast[3], SHARDS, axis=0, tiled=True),
        lax.all_gather(cast[4], SHARDS, axis=1, tiled=True),
    )


def spread_rows(rows):
    return lax.all_gather(rows, TENSOR, axis=2, tiled=True)


def collect_rows(term):
    return lax.psum_scatter(term, TENSOR, scatter_dimension=2, tiled=True)


def attention_output(attended, attn_weight):
    return collect_rows(
        jnp.einsum("cfpz,zd->cfpd", attended, attn_weight, preferred_element_type=jnp.float32)
    )


def layer_forward(stream, silu_cond, gathered, spatial):
    mod_weight, qkv_weight, attn_weight, up_weight, down_weight = gathered
    partial_value = jnp.einsum(
        "cd,dkz->ckz", silu_cond, mod_weight, preferred_element_type=jnp.float32
    )
    modulation = lax.all_gather(partial_value, TENSOR, axis=2, tiled=True)
    normed, inv_scale = layer_norm(stream)
    modulated = (normed * (1.0 + choose(modulation, 1)) + choose(modulation, 0)).astype(
        jnp.bfloat16
    )
    gathered_rows = spread_rows(modulated)
    projected = jnp.einsum(
        "cfpd,dkz->cfpkz", gathered_rows, qkv_weight, preferred_element_type=jnp.float32
    ).astype(jnp.bfloat16)
    if spatial:
        project_held = projected
        attended, log_total = attend(project_held, True)
    else:
        project_held = lax.all_to_all(projected, FRAME, split_axis=2, concat_axis=1, tiled=True)
        placed, log_total = attend(project_held, False)
        attended = lax.all_to_all(placed, FRAME, split_axis=1, concat_axis=2, tiled=True)
    branch_attn = attention_output(attended, attn_weight)
    middle = stream + choose(modulation, 2) * branch_attn
    normed_mlp, inv_mlp = layer_norm(middle)
    modulated_mlp = (normed_mlp * (1.0 + choose(modulation, 4)) + choose(modulation, 3)).astype(
        jnp.bfloat16
    )
    gathered_mlp = spread_rows(modulated_mlp)
    hidden_pre = jnp.einsum(
        "cfpd,dz->cfpz", gathered_mlp, up_weight, preferred_element_type=jnp.float32
    )
    hidden_act = gelu_tanh(hidden_pre).astype(jnp.bfloat16)
    branch_mlp = collect_rows(
        jnp.einsum("cfpz,zd->cfpd", hidden_act, down_weight, preferred_element_type=jnp.float32)
    )
    result = middle + choose(modulation, 5) * branch_mlp
    stored = (
        modulation,
        normed,
        inv_scale,
        gathered_rows,
        project_held,
        log_total,
        attended,
        branch_attn,
        normed_mlp,
        inv_mlp,
        gathered_mlp,
        hidden_pre,
        hidden_act,
        branch_mlp,
    )
    return (result, stored)


def layer_backward(upstream, silu_cond, gathered, stored, spatial):
    mod_weight, qkv_weight, attn_weight, up_weight, down_weight = gathered
    (
        modulation,
        normed,
        inv_scale,
        gathered_rows,
        project_held,
        log_total,
        attended,
        branch_attn,
        normed_mlp,
        inv_mlp,
        gathered_mlp,
        hidden_pre,
        hidden_act,
        branch_mlp,
    ) = stored
    d_branch_mlp = (upstream * choose(modulation, 5)).astype(jnp.bfloat16)
    d_gate_mlp = jnp.sum(upstream * branch_mlp, axis=(1, 2))
    d_branch_all = spread_rows(d_branch_mlp)
    grad_down = jnp.einsum(
        "cfpz,cfpd->zd", hidden_act, d_branch_all, preferred_element_type=jnp.float32
    )
    d_act = jnp.einsum(
        "cfpd,zd->cfpz", d_branch_all, down_weight, preferred_element_type=jnp.float32
    )
    d_pre = (d_act * gelu_slope(hidden_pre)).astype(jnp.bfloat16)
    grad_up = jnp.einsum("cfpd,cfpz->dz", gathered_mlp, d_pre, preferred_element_type=jnp.float32)
    d_mod_mlp = collect_rows(
        jnp.einsum("cfpz,dz->cfpd", d_pre, up_weight, preferred_element_type=jnp.float32)
    )
    d_shift_mlp = jnp.sum(d_mod_mlp, axis=(1, 2))
    d_scale_mlp = jnp.sum(d_mod_mlp * normed_mlp, axis=(1, 2))
    d_middle = upstream + norm_back(normed_mlp, inv_mlp, d_mod_mlp * (1.0 + choose(modulation, 4)))
    d_branch_attn = (d_middle * choose(modulation, 2)).astype(jnp.bfloat16)
    d_gate_attn = jnp.sum(d_middle * branch_attn, axis=(1, 2))
    d_attn_all = spread_rows(d_branch_attn)
    grad_attn = jnp.einsum(
        "cfpz,cfpd->zd", attended, d_attn_all, preferred_element_type=jnp.float32
    )
    d_attended = jnp.einsum(
        "cfpd,zd->cfpz", d_attn_all, attn_weight, preferred_element_type=jnp.float32
    ).astype(jnp.bfloat16)
    if spatial:
        d_projected = attend_back(project_held, log_total, d_attended, True)
    else:
        d_placed = lax.all_to_all(d_attended, FRAME, split_axis=2, concat_axis=1, tiled=True)
        d_projected = lax.all_to_all(
            attend_back(project_held, log_total, d_placed, False),
            FRAME,
            split_axis=1,
            concat_axis=2,
            tiled=True,
        )
    grad_qkv = jnp.einsum(
        "cfpd,cfpkz->dkz", gathered_rows, d_projected, preferred_element_type=jnp.float32
    )
    d_modulated = collect_rows(
        jnp.einsum("cfpkz,dkz->cfpd", d_projected, qkv_weight, preferred_element_type=jnp.float32)
    )
    d_shift_attn = jnp.sum(d_modulated, axis=(1, 2))
    d_scale_attn = jnp.sum(d_modulated * normed, axis=(1, 2))
    d_stream = d_middle + norm_back(normed, inv_scale, d_modulated * (1.0 + choose(modulation, 1)))
    d_modulation = jnp.stack(
        [d_shift_attn, d_scale_attn, d_gate_attn, d_shift_mlp, d_scale_mlp, d_gate_mlp], axis=1
    )
    d_mod_own = lax.psum_scatter(d_modulation, TENSOR, scatter_dimension=2, tiled=True)
    grad_mod = jnp.einsum(
        "cd,ckz->dkz", silu_cond.astype(jnp.float32), d_mod_own, precision=HIGHEST_PRECISION
    )
    d_silu = jnp.einsum(
        "ckz,dkz->cd", d_mod_own, mod_weight.astype(jnp.float32), precision=HIGHEST_PRECISION
    )
    grads = (
        lax.psum_scatter(
            grad_mod.astype(jnp.bfloat16), SHARDS, scatter_dimension=0, tiled=True
        ).astype(jnp.float32),
        lax.psum_scatter(
            grad_qkv.astype(jnp.bfloat16), SHARDS, scatter_dimension=0, tiled=True
        ).astype(jnp.float32),
        lax.psum_scatter(
            grad_attn.astype(jnp.bfloat16), SHARDS, scatter_dimension=1, tiled=True
        ).astype(jnp.float32),
        lax.psum_scatter(
            grad_up.astype(jnp.bfloat16), SHARDS, scatter_dimension=0, tiled=True
        ).astype(jnp.float32),
        lax.psum_scatter(
            grad_down.astype(jnp.bfloat16), SHARDS, scatter_dimension=1, tiled=True
        ).astype(jnp.float32),
    )
    return (d_stream, d_silu, grads)


def local(
    x_in,
    cond,
    mod_weight_one,
    qkv_weight_one,
    attn_out_one,
    mlp_up_one,
    mlp_down_one,
    mod_weight_two,
    qkv_weight_two,
    attn_out_two,
    mlp_up_two,
    mlp_down_two,
    out_cotangent,
):
    weights_first = (mod_weight_one, qkv_weight_one, attn_out_one, mlp_up_one, mlp_down_one)
    weights_second = (mod_weight_two, qkv_weight_two, attn_out_two, mlp_up_two, mlp_down_two)
    cond_float = cond.astype(jnp.float32)
    silu_cond = jax.nn.silu(cond_float).astype(jnp.bfloat16)
    gathered_first = fetch_weights(weights_first)
    middle_stream, stored_first = layer_forward(
        x_in.astype(jnp.float32), silu_cond, gathered_first, True
    )
    gathered_second = fetch_weights(weights_second)
    result, stored_second = layer_forward(middle_stream, silu_cond, gathered_second, False)
    back_second = backward_weights(weights_second)
    d_middle_stream, d_silu_second, grads_second = layer_backward(
        out_cotangent.astype(jnp.float32), silu_cond, back_second, stored_second, False
    )
    back_first = backward_weights(weights_first)
    input_grad, d_silu_first, grads_first = layer_backward(
        d_middle_stream, silu_cond, back_first, stored_first, True
    )
    d_silu_total = lax.psum(d_silu_first + d_silu_second, (FRAME, TENSOR))
    sigmoid_cond = jax.nn.sigmoid(cond_float)
    cond_grad = d_silu_total * (sigmoid_cond * (1.0 + cond_float * (1.0 - sigmoid_cond)))
    return (
        result.astype(jnp.bfloat16),
        input_grad,
        cond_grad,
        grads_first[0],
        grads_first[1],
        grads_first[2],
        grads_first[3],
        grads_first[4],
        grads_second[0],
        grads_second[1],
        grads_second[2],
        grads_second[3],
        grads_second[4],
    )

def flip(array, axis, bit):
    count = lax.axis_size(axis)
    return lax.ppermute(array, axis, [(i, i ^ bit) for i in range(count)])


def first_flip(shard):
    return 2 if shard % 2 == 0 else 4


def hop(array, which):
    if which == 0:
        pairs = [(i, i ^ 1) for i in range(8)]
    elif which == 1:
        pairs = [(i, i ^ first_flip(i)) for i in range(8)]
    else:
        pairs = [(i, i ^ (6 - first_flip(i))) for i in range(8)]
    return lax.ppermute(array, SHARDS, pairs)


class Line:
    def __init__(self):
        self.last = ()
        self.awaited = []
        self.under_way = []
        self.under_way_next = []

    def held(self, value):
        return lax.optimization_barrier((value, self.last, self.awaited))[0]

    def __call__(self, work, *inputs):
        self.last = work(*self.held(inputs))
        self.awaited = []
        return self.last

    def wait(self, value):
        self.awaited.append(value)
        return value

    def send(self, array, move):
        self.under_way.append(move(self.held(array)))
        return self.under_way[-1]

    def hop(self, array, which):
        return self.send(array, lambda held: hop(held, which))

    def exchange_sum(self, array, axis):
        bit = 1
        while bit < lax.axis_size(axis):
            array = self(jnp.add, array, flip(array, axis, bit))
            bit *= 2
        return array

    def place_along(self, array, axis):
        count = lax.axis_size(axis)
        own = (jnp.arange(count) == lax.axis_index(axis)).reshape((count,) + (1,) * array.ndim)
        return self.exchange_sum(jnp.where(own, array[None], 0.0), axis)

    def send_ahead(self, array, move):
        self.under_way_next.append(move(self.held(array)))
        return self.under_way_next[-1]

    def tick(self):
        self.awaited += self.under_way
        self.under_way = self.under_way_next
        self.under_way_next = []


def shard_index():
    return lax.axis_index(CLIP) * lax.axis_size(FRAME) + lax.axis_index(FRAME)


def piece_order():
    shard = shard_index()
    first = jnp.where(shard % 2 == 0, 2, 4)
    second = 6 - first
    masks = [0, first, second, 6, 1, 1 ^ second, 1 ^ first, 7]
    return jnp.stack([shard ^ mask for mask in masks]).astype(jnp.int32)


class Gather:
    def __init__(self, line, piece):
        self.line = line
        self.whole = lax.all_gather(piece, TENSOR, axis=0, tiled=False)

    def send(self):
        self.line.wait(self.whole)
        self.near = self.line.hop(self.whole, 1)

    def relay(self):
        self.pair = self.line(lambda *pair: jnp.stack(pair), self.whole, self.near)
        self.far = self.line.hop(self.pair, 2)
        self.other_pair = self.line.hop(self.pair, 0)

    def end(self):
        other_far = self.line.hop(self.far, 0)
        self.pieces = (self.pair, self.far, self.other_pair, other_far)


class MidGather:
    def __init__(self, line, piece):
        self.line = line
        self.piece = piece

    def send(self):
        self.near = self.line.hop(self.piece, 1)

    def join(self):
        pair = self.line(lambda *pair: jnp.stack(pair), self.piece, self.near)
        self.pair = lax.all_gather(pair, TENSOR, axis=0, tiled=False)

    def relay(self):
        self.far = self.line.hop(self.pair, 2)
        self.other_pair = self.line.hop(self.pair, 0)

    def end(self):
        other_far = self.line.hop(self.far, 0)
        self.pieces = (self.pair, self.far, self.other_pair, other_far)


def wide(array):
    return array.astype(jnp.float32)


def low(array):
    return array.astype(jnp.bfloat16)


def total(*arrays):
    return low(sum(wide(array) for array in arrays))


class Scatter:
    def __init__(self, line, grad):
        self.line = line
        self.keep, away = grad
        self.far = line.send_ahead(away, lambda held: hop(held, 2))

    def relay(self):
        work = lambda keep, far: total(keep[1], far[1])
        self.near = self.line.hop(self.line(work, self.keep, self.far), 1)

    def finish(self):
        work = lambda keep, far, near: total(keep[0], far[0], near)
        own = self.line(work, self.keep, self.far, self.near)
        self.piece = lax.psum_scatter(own, TENSOR, scatter_dimension=0, tiled=False)


def pack_layer(weights):
    qkv, attn, up, down = (weight.astype(jnp.bfloat16) for weight in weights)
    rows = qkv.shape[0]
    attn_part = jnp.concatenate([qkv.reshape(rows, -1), attn.T], axis=1)
    return attn_part, up, down.T


PIECES = 8
PAIRS = 4
VMEM_BYTES = 48 << 20
COST_SHARE = 8


def contract(left, right, left_dim, right_dim):
    return lax.dot_general(
        left, right, (((left_dim,), (right_dim,)), ((), ())), preferred_element_type=jnp.float32
    )


def assemble(order_ref, piece_refs, whole_ref):
    for j in range(PIECES):
        ref = piece_refs[j // 2]
        rows = ref.shape[2]
        start = pl.multiple_of(order_ref[j] * rows, 16)
        whole_ref[pl.ds(start, rows), :] = ref[(0, j % 2) if ref.shape[0] == 1 else (j % 2, 0)]


def up_kernel(order_ref, x_ref, *refs):
    pre_ref, act_ref, whole_ref = refs[PAIRS:]
    assemble(order_ref, refs[:PAIRS], whole_ref)
    pre = contract(x_ref[...], whole_ref[...], 1, 0)
    pre_ref[...] = pre
    act_ref[...] = gelu_tanh(pre).astype(jnp.bfloat16)


def slope_kernel(order_ref, x_ref, pre_ref, *refs):
    out_ref, whole_ref = refs[PAIRS:]
    assemble(order_ref, refs[:PAIRS], whole_ref)
    d_act = contract(x_ref[...], whole_ref[...], 1, 0)
    out_ref[...] = (d_act * gelu_slope(pre_ref[...])).astype(jnp.bfloat16)


def turned_kernel(low, high, order_ref, x_ref, *refs):
    out_ref, whole_ref = refs[PAIRS:]
    assemble(order_ref, refs[:PAIRS], whole_ref)
    whole = contract(x_ref[...], whole_ref[...], 1, 0)
    out_ref[0] = whole[:, low:high].astype(jnp.bfloat16).T


def collect_kernel(low, high, turned, order_ref, y_ref, *refs):
    out_ref, whole_ref = refs[PAIRS:]
    assemble(order_ref, refs[:PAIRS], whole_ref)
    rows = y_ref[0].T if turned else y_ref[...]
    term = contract(rows, whole_ref[:, low:high], 1, 1)

    @pl.when(pl.program_id(0) == 0)
    def _():
        out_ref[...] = term

    @pl.when(pl.program_id(0) > 0)
    def _():
        out_ref[...] += term


def turn(order_ref, x_refs, whole_ref, turned_ref):
    rows, tokens = turned_ref.shape[0] * 2 // PIECES, turned_ref.shape[1] // 2
    for side in range(2):
        whole_ref[...] = x_refs[side][...].T
        for j in range(PIECES // 2):
            start = pl.multiple_of(order_ref[j] * rows, 16)
            turned_ref[pl.ds(j * rows, rows), pl.ds(side * tokens, tokens)] = whole_ref[
                pl.ds(start, rows), :
            ]


def deal_out(grad, *out_refs):
    rows = out_refs[0].shape[2]
    for j in range(PIECES // 2):
        out_refs[j // 2][j % 2, 0] = grad[j * rows : (j + 1) * rows]


def grad_kernel(order_ref, x_ref, x_other, y_ref, y_other, *refs):
    whole_ref, turned_ref = refs[2:]

    @pl.when(pl.program_id(0) == 0)
    def _():
        turn(order_ref, (x_ref, x_other), whole_ref, turned_ref)

    tokens = x_ref.shape[0]
    grad = contract(turned_ref[:, :tokens], y_ref[...], 1, 0)
    grad += contract(turned_ref[:, tokens:], y_other[...], 1, 0)
    deal_out(grad.astype(jnp.bfloat16), *refs[:2])


def attn_grad_kernel(order_ref, *refs):
    x_refs, b_refs, y_refs, a_refs = (refs[2 * j : 2 * j + 2] for j in range(4))
    out_refs, (whole_ref, x_turned, b_turned, grad_ref) = refs[8:10], refs[10:]

    @pl.when(pl.program_id(0) == 0)
    def _():
        turn(order_ref, x_refs, whole_ref, x_turned)
        turn(order_ref, b_refs, whole_ref, b_turned)

    tokens, split = y_refs[0].shape[2], y_refs[0].shape[1]
    for turned, pair, lanes in (
        (x_turned, y_refs, slice(0, split)),
        (b_turned, a_refs, slice(split, grad_ref.shape[1])),
    ):
        grad = contract(turned[:, :tokens], pair[0][0], 1, 1)
        grad += contract(turned[:, tokens:], pair[1][0], 1, 1)
        grad_ref[:, lanes] = grad.astype(jnp.bfloat16)
    deal_out(grad_ref[...], *out_refs)


def masked_scores(queries, keys, group):
    scores = contract(queries, keys, 0, 0) * HD ** (-0.5)
    if group:
        place = lax.broadcasted_iota(jnp.int32, scores.shape, 0) % group
        other = lax.broadcasted_iota(jnp.int32, scores.shape, 1) % group
        scores = jnp.where(place == other, scores, -3e38)
    expo = jnp.exp(scores - jnp.max(scores, axis=-1, keepdims=True))
    return expo / jnp.sum(expo, axis=-1, keepdims=True)


def attend_kernel(group, projected_ref, out_ref):
    part = out_ref.shape[1]
    for start in range(0, part, HD):
        queries, keys, values = (
            projected_ref[0, pl.ds(j * part + start, HD), :] for j in range(3)
        )
        probs = masked_scores(queries, keys, group).astype(jnp.bfloat16)
        out_ref[0, pl.ds(start, HD), :] = contract(values, probs, 1, 1).astype(jnp.bfloat16)


def attend_back_kernel(group, projected_ref, upstream_ref, out_ref):
    part = upstream_ref.shape[1]
    scale_factor = HD ** (-0.5)
    for start in range(0, part, HD):
        queries, keys, values = (
            projected_ref[0, pl.ds(j * part + start, HD), :] for j in range(3)
        )
        upstream = upstream_ref[0, pl.ds(start, HD), :]
        probs = masked_scores(queries, keys, group)
        d_probs = contract(upstream, values, 0, 0)
        row_inner = jnp.sum(probs * d_probs, axis=-1, keepdims=True)
        d_scores = (probs * (d_probs - row_inner)).astype(jnp.bfloat16)
        grads = (
            contract(keys, d_scores, 1, 1) * scale_factor,
            contract(queries, d_scores, 1, 0) * scale_factor,
            contract(upstream, probs.astype(jnp.bfloat16), 1, 0),
        )
        for j in range(3):
            out_ref[0, pl.ds(j * part + start, HD), :] = grads[j].astype(jnp.bfloat16)


def call(kernel, grid, in_specs, out_specs, out_shape, scratch, flops, args):
    moved = sum(a.size * a.dtype.itemsize for a in args)
    moved += sum(o.size * o.dtype.itemsize for o in jax.tree.leaves(out_shape))
    return pl.pallas_call(
        kernel,
        out_shape=out_shape,
        grid_spec=pltpu.PrefetchScalarGridSpec(
            num_scalar_prefetch=1 if scratch else 0,
            grid=grid,
            in_specs=in_specs,
            out_specs=out_specs,
            scratch_shapes=scratch,
        ),
        compiler_params=pltpu.CompilerParams(vmem_limit_bytes=VMEM_BYTES),
        cost_estimate=pl.CostEstimate(
            flops=flops // COST_SHARE, bytes_accessed=moved // COST_SHARE, transcendentals=0
        ),
    )(*args)


def still(shape):
    return pl.BlockSpec(shape, lambda z, *_: (0,) * len(shape))


def lead(shape):
    return pl.BlockSpec((1,) + shape, lambda z, *_: (z,) + (0,) * len(shape))


def column(tokens, width):
    return pl.BlockSpec((tokens, width), lambda z, *_: (0, z))


def sizes(pieces, groups_first):
    groups = pieces[0].shape[0 if groups_first else 1]
    rows, width = pieces[0].shape[2:]
    return groups, rows, width, rows * PIECES


def piece_specs(pieces, groups_first):
    rows, width = pieces[0].shape[2:]
    if groups_first:
        return [lead((2, rows, width))] * PAIRS
    return pair_specs(rows, width, PAIRS)


def pair_specs(rows, width, count):
    return [pl.BlockSpec((2, 1, rows, width), lambda z, *_: (0, z, 0, 0))] * count


def times_up(order, x, pieces, groups_first):
    groups, rows, width, depth = sizes(pieces, groups_first)
    tokens = x.shape[0]
    shape = (tokens, groups * width)
    return call(
        up_kernel,
        (groups,),
        [still(x.shape)] + piece_specs(pieces, groups_first),
        [column(tokens, width)] * 2,
        [jax.ShapeDtypeStruct(shape, jnp.float32), jax.ShapeDtypeStruct(shape, jnp.bfloat16)],
        [pltpu.VMEM((depth, width), jnp.bfloat16)],
        2 * tokens * depth * width * groups,
        (order, x) + pieces,
    )


def times_slope(order, x, pre, pieces, groups_first=False):
    groups, rows, width, depth = sizes(pieces, groups_first)
    tokens = x.shape[0]
    return call(
        slope_kernel,
        (groups,),
        [still(x.shape), column(tokens, width)] + piece_specs(pieces, groups_first),
        column(tokens, width),
        jax.ShapeDtypeStruct(pre.shape, jnp.bfloat16),
        [pltpu.VMEM((depth, width), jnp.bfloat16)],
        2 * tokens * depth * width * groups,
        (order, x, pre) + pieces,
    )


def times_turned(order, x, pieces, low, high, groups_first=False):
    groups, rows, width, depth = sizes(pieces, groups_first)
    tokens = x.shape[0]
    return call(
        functools.partial(turned_kernel, low, high),
        (groups,),
        [still(x.shape)] + piece_specs(pieces, groups_first),
        lead((high - low, tokens)),
        jax.ShapeDtypeStruct((groups, high - low, tokens), jnp.bfloat16),
        [pltpu.VMEM((depth, width), jnp.bfloat16)],
        2 * tokens * depth * width * groups,
        (order, x) + pieces,
    )


def collect(order, y, pieces, low, high, turned, groups_first=False):
    groups, rows, width, depth = sizes(pieces, groups_first)
    tokens = y.shape[2] if turned else y.shape[0]
    return call(
        functools.partial(collect_kernel, low, high, turned),
        (groups,),
        [lead(y.shape[1:]) if turned else column(tokens, width)]
        + piece_specs(pieces, groups_first),
        still((tokens, depth)),
        jax.ShapeDtypeStruct((tokens, depth), jnp.float32),
        [pltpu.VMEM((depth, width), jnp.bfloat16)],
        2 * tokens * depth * (high - low) * groups,
        (order, y) + pieces,
    )


def grad_call(kernel, args, specs, groups, depth, width, scratch):
    rows = depth // PIECES
    tokens = args[1].shape[0]
    return call(
        kernel,
        (groups,),
        specs,
        pair_specs(rows, width, 2),
        [jax.ShapeDtypeStruct((2, groups, rows, width), jnp.bfloat16)] * 2,
        [pltpu.VMEM((depth, tokens), jnp.bfloat16)]
        + [pltpu.VMEM(shape, jnp.bfloat16) for shape in scratch],
        2 * tokens * depth * width * groups,
        args,
    )


def grad_of(order, x, x_other, y, y_other, groups):
    tokens, width = x.shape[0], y.shape[1] // groups
    depth = x.shape[1]
    specs = [still(x.shape)] * 2 + [column(tokens, width)] * 2
    args = (order, x, x_other, y, y_other)
    scratch = [(depth // 2, 2 * tokens)]
    return grad_call(grad_kernel, args, specs, groups, depth, width, scratch)


def attn_grad_of(order, *args):
    x, y, a = args[0], args[4], args[6]
    groups, wide_part, tokens = y.shape
    part, depth = a.shape[1], x.shape[1]
    specs = [still(x.shape)] * 4 + [lead((wide_part, tokens))] * 2 + [lead((part, tokens))] * 2
    scratch = [(depth // 2, 2 * tokens)] * 2 + [(depth // 2, wide_part + part)]
    return grad_call(
        attn_grad_kernel, (order, *args), specs, groups, depth, wide_part + part, scratch
    )


def attend_call(projected, group):
    groups, wide, tokens = projected.shape
    part = wide // 3
    return call(
        functools.partial(attend_kernel, group),
        (groups,),
        [lead((wide, tokens))],
        lead((part, tokens)),
        jax.ShapeDtypeStruct((groups, part, tokens), jnp.bfloat16),
        [],
        4 * tokens * tokens * part * groups,
        (projected,),
    )


def attend_back_call(projected, upstream, group):
    groups, wide, tokens = projected.shape
    part = wide // 3
    return call(
        functools.partial(attend_back_kernel, group),
        (groups,),
        [lead((wide, tokens)), lead((part, tokens))],
        lead((wide, tokens)),
        jax.ShapeDtypeStruct((groups, wide, tokens), jnp.bfloat16),
        [],
        10 * tokens * tokens * part * groups,
        (projected, upstream),
    )


class Layer:
    def __init__(self, line, order, modulation, group):
        self.line = line
        self.order = order
        self.modulation = modulation
        self.group = group
        self.others = {}

    def share(self, *arrays):
        for array in arrays:
            self.others[id(array)] = self.line.hop(array, 0)

    def both(self, array):
        return array, self.others[id(array)]

    def project(self, stream, attn):
        self.stream = stream
        self.attn = attn
        self.width = attn[0].shape[-1]
        self.part = self.width // 4
        rows = self.modulation

        def work(stream, attn):
            normed, inv_scale = layer_norm(stream)
            modulated = low(normed * (1.0 + rows[1]) + rows[0])
            projected = times_turned(self.order, modulated, attn, 0, 3 * self.part)
            return normed, inv_scale, modulated, projected

        made = self.line(work, stream, attn)
        self.normed, self.inv_scale, self.modulated, self.projected = made

    def attend(self):
        self.attended = self.line(
            lambda projected: attend_call(projected, self.group), self.projected
        )

    def attention_out(self):
        rows = self.modulation

        def work(attended, stream, attn):
            branch_attn = collect(self.order, attended, attn, 3 * self.part, self.width, True)
            middle = stream + rows[2] * branch_attn
            normed_mlp, inv_mlp = layer_norm(middle)
            modulated_mlp = low(normed_mlp * (1.0 + rows[4]) + rows[3])
            return branch_attn, middle, normed_mlp, inv_mlp, modulated_mlp

        made = self.line(work, self.attended, self.stream, self.attn)
        self.branch_attn, self.middle, self.normed_mlp, self.inv_mlp, self.modulated_mlp = made

    def mlp_up(self, up, groups_first):
        self.up = up
        self.up_first = groups_first
        work = lambda rows, up: times_up(self.order, rows, up, self.up_first)
        self.hidden_pre, self.hidden_act = self.line(work, self.modulated_mlp, up)

    def mlp_down(self, down, last):
        rows = self.modulation

        def work(act, middle, down):
            branch_mlp = collect(self.order, act, down, 0, self.width, False)
            return branch_mlp, last(middle + rows[5] * branch_mlp)

        self.branch_mlp, result = self.line(work, self.hidden_act, self.middle, down)
        return result

    def turn_back(self, upstream):
        rows = self.modulation
        self.upstream = upstream
        self.d_branch_mlp = self.line(lambda rows_in: low(rows_in * rows[5]), upstream)

    def gradient(self, *args):
        groups = self.attn[0].shape[1]
        work = lambda *rows: grad_of(self.order, *rows, groups)
        return Scatter(self.line, self.line(work, *args))

    def grad_down(self):
        return self.gradient(*self.both(self.d_branch_mlp), *self.both(self.hidden_act))

    def slope(self, down):
        work = lambda rows, pre, down: times_slope(self.order, rows, pre, down)
        self.d_pre = self.line(work, self.d_branch_mlp, self.hidden_pre, down)

    def grad_up(self):
        return self.gradient(*self.both(self.modulated_mlp), *self.both(self.d_pre))

    def back_up(self):
        rows = self.modulation

        def work(d_pre, upstream, normed, inv_mlp, up):
            d_mod_mlp = collect(
                self.order, d_pre, up, 0, self.width, False, self.up_first
            )
            d_middle = upstream + norm_back(normed, inv_mlp, d_mod_mlp * (1.0 + rows[4]))
            return d_mod_mlp, d_middle, low(d_middle * rows[2])

        made = self.line(
            work, self.d_pre, self.upstream, self.normed_mlp, self.inv_mlp, self.up
        )
        self.d_mod_mlp, self.d_middle, self.d_branch_attn = made

    def back_out(self):
        work = lambda rows, attn: times_turned(
            self.order, rows, attn, 3 * self.part, self.width
        )
        self.d_attended = self.line(work, self.d_branch_attn, self.attn)

    def back_attend(self):
        work = lambda projected, upstream: attend_back_call(projected, upstream, self.group)
        self.d_projected = self.line(work, self.projected, self.d_attended)

    def grad_attn(self):
        work = lambda *rows: attn_grad_of(self.order, *rows)
        rows = (self.modulated, self.d_branch_attn, self.d_projected, self.attended)
        grad = self.line(work, *(one for array in rows for one in self.both(array)))
        return Scatter(self.line, grad)

    def back_project(self, last):
        rows = self.modulation

        def work(d_projected, d_middle, normed, inv_scale, attn):
            d_modulated = collect(self.order, d_projected, attn, 0, 3 * self.part, True)
            back = norm_back(normed, inv_scale, d_modulated * (1.0 + rows[1]))
            return d_modulated, last(d_middle + back)

        self.d_modulated, result = self.line(
            work, self.d_projected, self.d_middle, self.normed, self.inv_scale, self.attn
        )
        return result

    def d_modulation(self):
        terms = (
            self.d_modulated,
            self.d_modulated * self.normed,
            self.d_middle * self.branch_attn,
            self.d_mod_mlp,
            self.d_mod_mlp * self.normed_mlp,
            self.upstream * self.branch_mlp,
        )
        return jnp.stack([jnp.sum(term, axis=0) for term in terms])


def finish_grads(attn_piece, up_piece, down_piece):
    rows, width = attn_piece.shape
    part = width // 4
    qkv = attn_piece[:, : 3 * part].reshape(rows, 3, part).astype(jnp.float32)
    attn = attn_piece[:, 3 * part :].T.astype(jnp.float32)
    return qkv, attn, up_piece.astype(jnp.float32), down_piece.T.astype(jnp.float32)


def deal_rows(rows, axes):
    return lax.all_to_all(rows, axes, split_axis=0, concat_axis=0, tiled=True)


def swap_blocks(rows, outer, inner):
    return rows.reshape(outer, inner, -1, rows.shape[1]).swapaxes(0, 1).reshape(rows.shape)


def local_whole(
    x_in,
    cond,
    mod_weight_one,
    qkv_weight_one,
    attn_out_one,
    mlp_up_one,
    mlp_down_one,
    mod_weight_two,
    qkv_weight_two,
    attn_out_two,
    mlp_up_two,
    mlp_down_two,
    out_cotangent,
):
    rows, _, part = qkv_weight_one.shape
    width = x_in.shape[-1]
    packed = [
        pack_layer((qkv_weight_one, attn_out_one, mlp_up_one, mlp_down_one)),
        pack_layer((qkv_weight_two, attn_out_two, mlp_up_two, mlp_down_two)),
    ]
    cond_every = lax.all_gather(cond, CLIP, axis=0, tiled=True).astype(jnp.float32)
    clip_count = cond_every.shape[0]
    silu_every = jax.nn.silu(cond_every).astype(jnp.bfloat16)
    silu_rows = lax.dynamic_slice_in_dim(silu_every, shard_index() * rows, rows, axis=1)
    mod_weights = (mod_weight_one.astype(jnp.bfloat16), mod_weight_two.astype(jnp.bfloat16))
    partial_value = jnp.stack(
        [
            jnp.einsum("cd,dkz->ckz", silu_rows, weight, preferred_element_type=jnp.float32)
            for weight in mod_weights
        ],
        axis=1,
    )
    devices, tensors = lax.axis_size(FRAME), lax.axis_size(TENSOR)
    own_frames = x_in.shape[1]
    own_places = x_in.shape[2] // devices
    cotangent = deal_rows(swap_blocks(out_cotangent.reshape(-1, width), own_frames, devices), FRAME)
    cotangent = swap_blocks(cotangent, devices, own_frames)
    line = Line()
    up_one = MidGather(line, packed[0][1])
    up_one.send()
    line.tick()
    summed = line.exchange_sum(line.exchange_sum(partial_value, FRAME), CLIP)
    line.wait(cotangent)
    summed = lax.dynamic_index_in_dim(summed, lax.axis_index(CLIP), 0, keepdims=False)
    placed = line.place_along(summed, TENSOR)
    modulations = placed.transpose(1, 2, 0, 3).reshape(summed.shape[:2] + (-1,))

    order = piece_order()
    attn_one, down_one = (Gather(line, piece) for piece in packed[0][::2])
    attn_two, up_two, down_two = (Gather(line, piece) for piece in packed[1])
    one = Layer(line, order, modulations[0], 0)
    two = Layer(line, order, modulations[1], own_places)

    line.wait(packed)
    up_one.join()
    line.wait(attn_one.whole)
    attn_one.send()
    line.tick()
    attn_one.relay()
    line.under_way.append(up_one.pair)
    line.tick()
    attn_one.end()
    up_one.relay()
    frames_in = line.send(x_in.reshape(-1, width), lambda held: deal_rows(held, TENSOR))
    one.project(line(wide, frames_in), attn_one.pieces)
    down_one.send()
    one.attend()
    one.attention_out()
    line.tick()
    up_one.end()
    down_one.relay()
    one.mlp_up(up_one.pieces, True)
    cotangent = line(wide, cotangent)
    attn_two.send()
    line.tick()
    down_one.end()
    attn_two.relay()
    between = one.mlp_down(down_one.pieces, low)
    between = line.send(between, lambda held: deal_rows(held, (TENSOR, FRAME)))
    two.turn_back(cotangent)
    up_two.send()
    line.tick()
    attn_two.end()
    up_two.relay()
    two.share(two.d_branch_mlp)
    between = line(wide, between)
    two.project(between, attn_two.pieces)
    down_two.send()
    two.attend()
    two.attention_out()
    line.tick()
    up_two.end()
    down_two.relay()
    two.mlp_up(up_two.pieces, False)
    two.share(two.hidden_act)
    down_grad = two.grad_down()
    line.tick()
    down_two.end()
    two.share(two.modulated_mlp, two.modulated)
    two.slope(down_two.pieces)
    two.share(two.d_pre)
    two.back_up()
    up_grad = two.grad_up()
    line.tick()
    down_grad.relay()
    two.share(two.d_branch_attn, two.attended)
    two.back_out()
    two.back_attend()
    two.share(two.d_projected)
    d_second = two.back_project(low)
    d_second = line.send_ahead(d_second, lambda held: deal_rows(held, (TENSOR, FRAME)))
    attn_grad = two.grad_attn()
    line.tick()
    up_grad.relay()
    one.share(one.hidden_act, one.attended)
    d_second = line(wide, d_second)
    down_grad.finish()
    one.turn_back(d_second)
    one.share(one.d_branch_mlp)
    one.slope(down_one.pieces)
    down_last = one.grad_down()
    line.tick()
    attn_grad.relay()
    one.share(one.d_pre, one.modulated_mlp, one.modulated)
    up_grad.finish()
    one.back_up()
    up_last = one.grad_up()
    one.back_out()
    one.back_attend()
    line.tick()
    down_last.relay()
    one.share(one.d_branch_attn, one.d_projected)
    attn_grad.finish()
    d_first = one.back_project(low)
    result = two.mlp_down(
        down_two.pieces, lambda rows: swap_blocks(low(rows), own_frames, devices)
    )
    d_mods = line(lambda: jnp.stack([one.d_modulation(), two.d_modulation()]))
    d_mods = line(jnp.add, d_mods, flip(d_mods, FRAME, 1))
    attn_last = one.grad_attn()
    d_mods = line(jnp.add, d_mods, flip(d_mods, TENSOR, 1))
    near_mods = flip(d_mods, TENSOR, 2)
    line.tick()
    up_last.relay()
    down_last.finish()
    input_grad = deal_rows(d_first, TENSOR)
    line.under_way.append(input_grad)
    d_mods = line(jnp.add, d_mods, near_mods)
    near_mods = line.send(d_mods, lambda held: flip(held, FRAME, 2))
    line.tick()
    attn_last.relay()
    up_last.finish()
    input_grad = line(wide, input_grad).reshape(x_in.shape)
    line.tick()
    attn_last.finish()
    layer_out = swap_blocks(deal_rows(result, FRAME), devices, own_frames).reshape(x_in.shape)
    d_mods = line(jnp.add, d_mods, near_mods)
    d_mods = lax.dynamic_slice_in_dim(d_mods, lax.axis_index(TENSOR) * part, part, axis=2)
    d_every = line.place_along(d_mods, CLIP)
    silu_float = silu_rows.astype(jnp.float32)
    grad_mods = [
        sum(
            silu_float[c][:, None, None] * d_every[c, layer][None] for c in range(clip_count)
        )
        for layer in range(2)
    ]
    d_silu = jnp.stack(
        [
            sum(
                jnp.sum(
                    d_every[c, layer][None] * mod_weights[layer].astype(jnp.float32), axis=(1, 2)
                )
                for layer in range(2)
            )
            for c in range(clip_count)
        ]
    )
    d_silu = line.exchange_sum(d_silu, TENSOR)
    d_silu = line.place_along(line.place_along(d_silu, FRAME), CLIP)
    d_silu = d_silu.transpose(2, 0, 1, 3).reshape(clip_count, -1)
    d_silu = lax.dynamic_slice_in_dim(d_silu, lax.axis_index(CLIP), 1, axis=0)
    cond_float = cond.astype(jnp.float32)
    sigmoid_cond = jax.nn.sigmoid(cond_float)
    cond_grad = d_silu * (sigmoid_cond * (1.0 + cond_float * (1.0 - sigmoid_cond)))
    first_out = finish_grads(attn_last.piece, up_last.piece, down_last.piece)
    second_out = finish_grads(attn_grad.piece, up_grad.piece, down_grad.piece)
    return (
        layer_out,
        input_grad,
        cond_grad,
        grad_mods[0],
        *first_out,
        grad_mods[1],
        *second_out,
    )


def holds_whole(mesh):
    tensors = mesh.shape[TENSOR]
    return (
        mesh.shape[CLIP] == 2
        and mesh.shape[FRAME] == 4
        and FRAMES % (4 * tensors) == 0
        and tensors & (tensors - 1) == 0
    )


def solution(mesh):
    return jax.shard_map(
        local_whole if holds_whole(mesh) else local,
        mesh=mesh,
        in_specs=(
            P(CLIP, FRAME, TENSOR, None),
            P(CLIP, None),
            P(SHARDS, None, TENSOR),
            P(SHARDS, None, TENSOR),
            P(TENSOR, SHARDS),
            P(SHARDS, TENSOR),
            P(TENSOR, SHARDS),
            P(SHARDS, None, TENSOR),
            P(SHARDS, None, TENSOR),
            P(TENSOR, SHARDS),
            P(SHARDS, TENSOR),
            P(TENSOR, SHARDS),
            P(CLIP, FRAME, TENSOR, None),
        ),
        out_specs=(
            P(CLIP, FRAME, TENSOR, None),
            P(CLIP, FRAME, TENSOR, None),
            P(CLIP, None),
            P(SHARDS, None, TENSOR),
            P(SHARDS, None, TENSOR),
            P(TENSOR, SHARDS),
            P(SHARDS, TENSOR),
            P(TENSOR, SHARDS),
            P(SHARDS, None, TENSOR),
            P(SHARDS, None, TENSOR),
            P(TENSOR, SHARDS),
            P(SHARDS, TENSOR),
            P(TENSOR, SHARDS),
        ),
        check_vma=False,
    )
```

```python
import functools

import jax
import jax.numpy as jnp
from jax import lax
from jax.experimental import pallas as pl
from jax.experimental.pallas import tpu as pltpu
from jax.sharding import PartitionSpec as P

HD = 72
FRAMES = 16
CLIP, FRAME, TENSOR = "clip", "frame", "tensor"
SHARDS = (CLIP, FRAME)


HIGHEST_PRECISION = lax.Precision.HIGHEST
SCORE_FORMS = {True: "cfphe,cfqhe->cfhpq", False: "cfphe,cgphe->cphfg"}
APPLY_FORMS = {True: "cfhpq,cfqhe->cfphe", False: "cphfg,cgphe->cfphe"}
BACK_FORMS = {True: "cfhpq,cfphe->cfqhe", False: "cphfg,cfphe->cgphe"}
GELU_COEFF = 0.7978845608028654
CUBIC_COEFF = 0.044715


def layer_norm(stream):
    centre = stream - jnp.mean(stream, axis=-1, keepdims=True)
    inv_scale = lax.rsqrt(jnp.mean(centre * centre, axis=-1, keepdims=True) + 1e-06)
    return (centre * inv_scale, inv_scale)


def norm_back(normed, inv_scale, upstream):
    return inv_scale * (
        upstream
        - jnp.mean(upstream, axis=-1, keepdims=True)
        - normed * jnp.mean(upstream * normed, axis=-1, keepdims=True)
    )


def gelu_tanh(inputs):
    return (
        0.5
        * inputs
        * (1.0 + jnp.tanh(GELU_COEFF * (inputs + CUBIC_COEFF * inputs * inputs * inputs)))
    )


def gelu_slope(inputs):
    tangent = jnp.tanh(GELU_COEFF * (inputs + CUBIC_COEFF * inputs * inputs * inputs))
    return 0.5 * (1.0 + tangent) + 0.5 * inputs * (1.0 - tangent * tangent) * GELU_COEFF * (
        1.0 + 3.0 * CUBIC_COEFF * inputs * inputs
    )


def choose(modulation, column):
    return modulation[:, column][:, None, None, :]


def split_heads(projected):
    leading = projected.shape[:3]
    row_width = projected.shape[-1]
    head_count = row_width // HD
    queries = projected[:, :, :, 0].reshape(leading + (head_count, HD))
    key_rows = projected[:, :, :, 1].reshape(leading + (head_count, HD))
    values = projected[:, :, :, 2].reshape(leading + (head_count, HD))
    return (queries, key_rows, values, leading, row_width)


def attend(projected, spatial):
    queries, key_rows, values, leading, row_width = split_heads(projected)
    scores = jnp.einsum(
        SCORE_FORMS[spatial], queries, key_rows, preferred_element_type=jnp.float32
    ) * HD ** (-0.5)
    highest = jnp.max(scores, axis=-1, keepdims=True)
    expo = jnp.exp(scores - highest)
    denominator = jnp.sum(expo, axis=-1, keepdims=True)
    probs = (expo / denominator).astype(jnp.bfloat16)
    log_total = highest + jnp.log(denominator)
    attended = jnp.einsum(APPLY_FORMS[spatial], probs, values, preferred_element_type=jnp.float32)
    return (attended.reshape(leading + (row_width,)).astype(jnp.bfloat16), log_total)


def attend_back(projected, log_total, d_attended, spatial):
    queries, key_rows, values, leading, row_width = split_heads(projected)
    scale_factor = HD ** (-0.5)
    scores = (
        jnp.einsum(SCORE_FORMS[spatial], queries, key_rows, preferred_element_type=jnp.float32)
        * scale_factor
    )
    probs = jnp.exp(scores - log_total)
    upstream = d_attended.reshape(leading + (row_width // HD, HD))
    d_probs = jnp.einsum(SCORE_FORMS[spatial], upstream, values, preferred_element_type=jnp.float32)
    d_values = jnp.einsum(
        BACK_FORMS[spatial],
        probs.astype(jnp.bfloat16),
        upstream,
        preferred_element_type=jnp.float32,
    )
    row_inner = jnp.sum(probs * d_probs, axis=-1, keepdims=True)
    d_scores = (probs * (d_probs - row_inner)).astype(jnp.bfloat16)
    d_queries = (
        jnp.einsum(APPLY_FORMS[spatial], d_scores, key_rows, preferred_element_type=jnp.float32)
        * scale_factor
    )
    d_keys = (
        jnp.einsum(BACK_FORMS[spatial], d_scores, queries, preferred_element_type=jnp.float32)
        * scale_factor
    )
    stacked = jnp.stack([d_queries, d_keys, d_values], axis=3)
    return stacked.reshape(leading + (3, row_width)).astype(jnp.bfloat16)


def fetch_weights(weights):
    cast = tuple((weight.astype(jnp.bfloat16) for weight in weights))
    return (
        lax.all_gather(cast[0], SHARDS, axis=0, tiled=True),
        lax.all_gather(cast[1], SHARDS, axis=0, tiled=True),
        lax.all_gather(cast[2], SHARDS, axis=1, tiled=True),
        lax.all_gather(cast[3], SHARDS, axis=0, tiled=True),
        lax.all_gather(cast[4], SHARDS, axis=1, tiled=True),
    )


def backward_weights(weights):
    cast = tuple((weight.astype(jnp.bfloat16) for weight in weights))
    return (
        lax.all_gather(cast[0], SHARDS, axis=0, tiled=True),
        lax.all_gather(cast[1], SHARDS, axis=0, tiled=True),
        lax.all_gather(cast[2], SHARDS, axis=1, tiled=True),
        lax.all_gather(cast[3], SHARDS, axis=0, tiled=True),
        lax.all_gather(cast[4], SHARDS, axis=1, tiled=True),
    )


def spread_rows(rows):
    return lax.all_gather(rows, TENSOR, axis=2, tiled=True)


def collect_rows(term):
    return lax.psum_scatter(term, TENSOR, scatter_dimension=2, tiled=True)


def attention_output(attended, attn_weight):
    return collect_rows(
        jnp.einsum("cfpz,zd->cfpd", attended, attn_weight, preferred_element_type=jnp.float32)
    )


def layer_forward(stream, silu_cond, gathered, spatial):
    mod_weight, qkv_weight, attn_weight, up_weight, down_weight = gathered
    partial_value = jnp.einsum(
        "cd,dkz->ckz", silu_cond, mod_weight, preferred_element_type=jnp.float32
    )
    modulation = lax.all_gather(partial_value, TENSOR, axis=2, tiled=True)
    normed, inv_scale = layer_norm(stream)
    modulated = (normed * (1.0 + choose(modulation, 1)) + choose(modulation, 0)).astype(
        jnp.bfloat16
    )
    gathered_rows = spread_rows(modulated)
    projected = jnp.einsum(
        "cfpd,dkz->cfpkz", gathered_rows, qkv_weight, preferred_element_type=jnp.float32
    ).astype(jnp.bfloat16)
    if spatial:
        project_held = projected
        attended, log_total = attend(project_held, True)
    else:
        project_held = lax.all_to_all(projected, FRAME, split_axis=2, concat_axis=1, tiled=True)
        placed, log_total = attend(project_held, False)
        attended = lax.all_to_all(placed, FRAME, split_axis=1, concat_axis=2, tiled=True)
    branch_attn = attention_output(attended, attn_weight)
    middle = stream + choose(modulation, 2) * branch_attn
    normed_mlp, inv_mlp = layer_norm(middle)
    modulated_mlp = (normed_mlp * (1.0 + choose(modulation, 4)) + choose(modulation, 3)).astype(
        jnp.bfloat16
    )
    gathered_mlp = spread_rows(modulated_mlp)
    hidden_pre = jnp.einsum(
        "cfpd,dz->cfpz", gathered_mlp, up_weight, preferred_element_type=jnp.float32
    )
    hidden_act = gelu_tanh(hidden_pre).astype(jnp.bfloat16)
    branch_mlp = collect_rows(
        jnp.einsum("cfpz,zd->cfpd", hidden_act, down_weight, preferred_element_type=jnp.float32)
    )
    result = middle + choose(modulation, 5) * branch_mlp
    stored = (
        modulation,
        normed,
        inv_scale,
        gathered_rows,
        project_held,
        log_total,
        attended,
        branch_attn,
        normed_mlp,
        inv_mlp,
        gathered_mlp,
        hidden_pre,
        hidden_act,
        branch_mlp,
    )
    return (result, stored)


def layer_backward(upstream, silu_cond, gathered, stored, spatial):
    mod_weight, qkv_weight, attn_weight, up_weight, down_weight = gathered
    (
        modulation,
        normed,
        inv_scale,
        gathered_rows,
        project_held,
        log_total,
        attended,
        branch_attn,
        normed_mlp,
        inv_mlp,
        gathered_mlp,
        hidden_pre,
        hidden_act,
        branch_mlp,
    ) = stored
    d_branch_mlp = (upstream * choose(modulation, 5)).astype(jnp.bfloat16)
    d_gate_mlp = jnp.sum(upstream * branch_mlp, axis=(1, 2))
    d_branch_all = spread_rows(d_branch_mlp)
    grad_down = jnp.einsum(
        "cfpz,cfpd->zd", hidden_act, d_branch_all, preferred_element_type=jnp.float32
    )
    d_act = jnp.einsum(
        "cfpd,zd->cfpz", d_branch_all, down_weight, preferred_element_type=jnp.float32
    )
    d_pre = (d_act * gelu_slope(hidden_pre)).astype(jnp.bfloat16)
    grad_up = jnp.einsum("cfpd,cfpz->dz", gathered_mlp, d_pre, preferred_element_type=jnp.float32)
    d_mod_mlp = collect_rows(
        jnp.einsum("cfpz,dz->cfpd", d_pre, up_weight, preferred_element_type=jnp.float32)
    )
    d_shift_mlp = jnp.sum(d_mod_mlp, axis=(1, 2))
    d_scale_mlp = jnp.sum(d_mod_mlp * normed_mlp, axis=(1, 2))
    d_middle = upstream + norm_back(normed_mlp, inv_mlp, d_mod_mlp * (1.0 + choose(modulation, 4)))
    d_branch_attn = (d_middle * choose(modulation, 2)).astype(jnp.bfloat16)
    d_gate_attn = jnp.sum(d_middle * branch_attn, axis=(1, 2))
    d_attn_all = spread_rows(d_branch_attn)
    grad_attn = jnp.einsum(
        "cfpz,cfpd->zd", attended, d_attn_all, preferred_element_type=jnp.float32
    )
    d_attended = jnp.einsum(
        "cfpd,zd->cfpz", d_attn_all, attn_weight, preferred_element_type=jnp.float32
    ).astype(jnp.bfloat16)
    if spatial:
        d_projected = attend_back(project_held, log_total, d_attended, True)
    else:
        d_placed = lax.all_to_all(d_attended, FRAME, split_axis=2, concat_axis=1, tiled=True)
        d_projected = lax.all_to_all(
            attend_back(project_held, log_total, d_placed, False),
            FRAME,
            split_axis=1,
            concat_axis=2,
            tiled=True,
        )
    grad_qkv = jnp.einsum(
        "cfpd,cfpkz->dkz", gathered_rows, d_projected, preferred_element_type=jnp.float32
    )
    d_modulated = collect_rows(
        jnp.einsum("cfpkz,dkz->cfpd", d_projected, qkv_weight, preferred_element_type=jnp.float32)
    )
    d_shift_attn = jnp.sum(d_modulated, axis=(1, 2))
    d_scale_attn = jnp.sum(d_modulated * normed, axis=(1, 2))
    d_stream = d_middle + norm_back(normed, inv_scale, d_modulated * (1.0 + choose(modulation, 1)))
    d_modulation = jnp.stack(
        [d_shift_attn, d_scale_attn, d_gate_attn, d_shift_mlp, d_scale_mlp, d_gate_mlp], axis=1
    )
    d_mod_own = lax.psum_scatter(d_modulation, TENSOR, scatter_dimension=2, tiled=True)
    grad_mod = jnp.einsum(
        "cd,ckz->dkz", silu_cond.astype(jnp.float32), d_mod_own, precision=HIGHEST_PRECISION
    )
    d_silu = jnp.einsum(
        "ckz,dkz->cd", d_mod_own, mod_weight.astype(jnp.float32), precision=HIGHEST_PRECISION
    )
    grads = (
        lax.psum_scatter(
            grad_mod.astype(jnp.bfloat16), SHARDS, scatter_dimension=0, tiled=True
        ).astype(jnp.float32),
        lax.psum_scatter(
            grad_qkv.astype(jnp.bfloat16), SHARDS, scatter_dimension=0, tiled=True
        ).astype(jnp.float32),
        lax.psum_scatter(
            grad_attn.astype(jnp.bfloat16), SHARDS, scatter_dimension=1, tiled=True
        ).astype(jnp.float32),
        lax.psum_scatter(
            grad_up.astype(jnp.bfloat16), SHARDS, scatter_dimension=0, tiled=True
        ).astype(jnp.float32),
        lax.psum_scatter(
            grad_down.astype(jnp.bfloat16), SHARDS, scatter_dimension=1, tiled=True
        ).astype(jnp.float32),
    )
    return (d_stream, d_silu, grads)


def local(
    x_in,
    cond,
    mod_weight_one,
    qkv_weight_one,
    attn_out_one,
    mlp_up_one,
    mlp_down_one,
    mod_weight_two,
    qkv_weight_two,
    attn_out_two,
    mlp_up_two,
    mlp_down_two,
    out_cotangent,
):
    weights_first = (mod_weight_one, qkv_weight_one, attn_out_one, mlp_up_one, mlp_down_one)
    weights_second = (mod_weight_two, qkv_weight_two, attn_out_two, mlp_up_two, mlp_down_two)
    cond_float = cond.astype(jnp.float32)
    silu_cond = jax.nn.silu(cond_float).astype(jnp.bfloat16)
    gathered_first = fetch_weights(weights_first)
    middle_stream, stored_first = layer_forward(
        x_in.astype(jnp.float32), silu_cond, gathered_first, True
    )
    gathered_second = fetch_weights(weights_second)
    result, stored_second = layer_forward(middle_stream, silu_cond, gathered_second, False)
    back_second = backward_weights(weights_second)
    d_middle_stream, d_silu_second, grads_second = layer_backward(
        out_cotangent.astype(jnp.float32), silu_cond, back_second, stored_second, False
    )
    back_first = backward_weights(weights_first)
    input_grad, d_silu_first, grads_first = layer_backward(
        d_middle_stream, silu_cond, back_first, stored_first, True
    )
    d_silu_total = lax.psum(d_silu_first + d_silu_second, (FRAME, TENSOR))
    sigmoid_cond = jax.nn.sigmoid(cond_float)
    cond_grad = d_silu_total * (sigmoid_cond * (1.0 + cond_float * (1.0 - sigmoid_cond)))
    return (
        result.astype(jnp.bfloat16),
        input_grad,
        cond_grad,
        grads_first[0],
        grads_first[1],
        grads_first[2],
        grads_first[3],
        grads_first[4],
        grads_second[0],
        grads_second[1],
        grads_second[2],
        grads_second[3],
        grads_second[4],
    )

def flip(array, axis, bit):
    count = lax.axis_size(axis)
    return lax.ppermute(array, axis, [(i, i ^ bit) for i in range(count)])


def first_flip(shard):
    return 2 if shard % 2 == 0 else 4


def hop(array, which):
    if which == 0:
        pairs = [(i, i ^ 1) for i in range(8)]
    elif which == 1:
        pairs = [(i, i ^ first_flip(i)) for i in range(8)]
    else:
        pairs = [(i, i ^ (6 - first_flip(i))) for i in range(8)]
    return lax.ppermute(array, SHARDS, pairs)


class Line:
    def __init__(self):
        self.last = ()
        self.awaited = []
        self.under_way = []
        self.under_way_next = []

    def held(self, value):
        return lax.optimization_barrier((value, self.last, self.awaited))[0]

    def __call__(self, work, *inputs):
        self.last = work(*self.held(inputs))
        self.awaited = []
        return self.last

    def wait(self, value):
        self.awaited.append(value)
        return value

    def send(self, array, move):
        self.under_way.append(move(self.held(array)))
        return self.under_way[-1]

    def hop(self, array, which):
        return self.send(array, lambda held: hop(held, which))

    def exchange_sum(self, array, axis):
        bit = 1
        while bit < lax.axis_size(axis):
            array = self(jnp.add, array, flip(array, axis, bit))
            bit *= 2
        return array

    def place_along(self, array, axis):
        count = lax.axis_size(axis)
        own = (jnp.arange(count) == lax.axis_index(axis)).reshape((count,) + (1,) * array.ndim)
        return self.exchange_sum(jnp.where(own, array[None], 0.0), axis)

    def send_ahead(self, array, move):
        self.under_way_next.append(move(self.held(array)))
        return self.under_way_next[-1]

    def tick(self):
        self.awaited += self.under_way
        self.under_way = self.under_way_next
        self.under_way_next = []


def shard_index():
    return lax.axis_index(CLIP) * lax.axis_size(FRAME) + lax.axis_index(FRAME)


def piece_order():
    shard = shard_index()
    first = jnp.where(shard % 2 == 0, 2, 4)
    second = 6 - first
    masks = [0, first, second, 6, 1, 1 ^ second, 1 ^ first, 7]
    return jnp.stack([shard ^ mask for mask in masks]).astype(jnp.int32)


class Gather:
    def __init__(self, line, piece):
        self.line = line
        self.whole = lax.all_gather(piece, TENSOR, axis=0, tiled=False)

    def send(self):
        self.line.wait(self.whole)
        self.near = self.line.hop(self.whole, 1)

    def relay(self):
        self.pair = self.line(lambda *pair: jnp.stack(pair), self.whole, self.near)
        self.far = self.line.hop(self.pair, 2)
        self.other_pair = self.line.hop(self.pair, 0)

    def end(self):
        other_far = self.line.hop(self.far, 0)
        self.pieces = (self.pair, self.far, self.other_pair, other_far)


class MidGather:
    def __init__(self, line, piece):
        self.line = line
        self.piece = piece

    def send(self):
        self.near = self.line.hop(self.piece, 1)

    def join(self):
        pair = self.line(lambda *pair: jnp.stack(pair), self.piece, self.near)
        self.pair = lax.all_gather(pair, TENSOR, axis=0, tiled=False)

    def relay(self):
        self.far = self.line.hop(self.pair, 2)
        self.other_pair = self.line.hop(self.pair, 0)

    def end(self):
        other_far = self.line.hop(self.far, 0)
        self.pieces = (self.pair, self.far, self.other_pair, other_far)


def wide(array):
    return array.astype(jnp.float32)


def low(array):
    return array.astype(jnp.bfloat16)


def total(*arrays):
    return low(sum(wide(array) for array in arrays))


class Scatter:
    def __init__(self, line, grad):
        self.line = line
        self.keep, away = grad
        self.far = line.send_ahead(away, lambda held: hop(held, 2))

    def relay(self):
        work = lambda keep, far: total(keep[1], far[1])
        self.near = self.line.hop(self.line(work, self.keep, self.far), 1)

    def finish(self):
        work = lambda keep, far, near: total(keep[0], far[0], near)
        own = self.line(work, self.keep, self.far, self.near)
        self.piece = lax.psum_scatter(own, TENSOR, scatter_dimension=0, tiled=False)


def pack_layer(weights):
    qkv, attn, up, down = (weight.astype(jnp.bfloat16) for weight in weights)
    rows = qkv.shape[0]
    attn_part = jnp.concatenate([qkv.reshape(rows, -1), attn.T], axis=1)
    return attn_part, up, down.T


PIECES = 8
PAIRS = 4
VMEM_BYTES = 48 << 20
COST_SHARE = 8


def contract(left, right, left_dim, right_dim):
    return lax.dot_general(
        left, right, (((left_dim,), (right_dim,)), ((), ())), preferred_element_type=jnp.float32
    )


def assemble(order_ref, piece_refs, whole_ref):
    for j in range(PIECES):
        ref = piece_refs[j // 2]
        rows = ref.shape[2]
        start = pl.multiple_of(order_ref[j] * rows, 16)
        whole_ref[pl.ds(start, rows), :] = ref[(0, j % 2) if ref.shape[0] == 1 else (j % 2, 0)]


def up_kernel(order_ref, x_ref, *refs):
    pre_ref, act_ref, whole_ref = refs[PAIRS:]
    assemble(order_ref, refs[:PAIRS], whole_ref)
    pre = contract(x_ref[...], whole_ref[...], 1, 0)
    pre_ref[...] = pre
    act_ref[...] = gelu_tanh(pre).astype(jnp.bfloat16)


def slope_kernel(order_ref, x_ref, pre_ref, *refs):
    out_ref, whole_ref = refs[PAIRS:]
    assemble(order_ref, refs[:PAIRS], whole_ref)
    d_act = contract(x_ref[...], whole_ref[...], 1, 0)
    out_ref[...] = (d_act * gelu_slope(pre_ref[...])).astype(jnp.bfloat16)


def turned_kernel(low, high, order_ref, x_ref, *refs):
    out_ref, whole_ref = refs[PAIRS:]
    assemble(order_ref, refs[:PAIRS], whole_ref)
    whole = contract(x_ref[...], whole_ref[...], 1, 0)
    out_ref[0] = whole[:, low:high].astype(jnp.bfloat16).T


def collect_kernel(low, high, turned, order_ref, y_ref, *refs):
    out_ref, whole_ref = refs[PAIRS:]
    assemble(order_ref, refs[:PAIRS], whole_ref)
    rows = y_ref[0].T if turned else y_ref[...]
    term = contract(rows, whole_ref[:, low:high], 1, 1)

    @pl.when(pl.program_id(0) == 0)
    def _():
        out_ref[...] = term

    @pl.when(pl.program_id(0) > 0)
    def _():
        out_ref[...] += term


def turn(order_ref, x_refs, whole_ref, turned_ref):
    rows, tokens = turned_ref.shape[0] * 2 // PIECES, turned_ref.shape[1] // 2
    for side in range(2):
        whole_ref[...] = x_refs[side][...].T
        for j in range(PIECES // 2):
            start = pl.multiple_of(order_ref[j] * rows, 16)
            turned_ref[pl.ds(j * rows, rows), pl.ds(side * tokens, tokens)] = whole_ref[
                pl.ds(start, rows), :
            ]


def deal_out(grad, *out_refs):
    rows = out_refs[0].shape[2]
    for j in range(PIECES // 2):
        out_refs[j // 2][j % 2, 0] = grad[j * rows : (j + 1) * rows]


def grad_kernel(order_ref, x_ref, x_other, y_ref, y_other, *refs):
    whole_ref, turned_ref = refs[2:]

    @pl.when(pl.program_id(0) == 0)
    def _():
        turn(order_ref, (x_ref, x_other), whole_ref, turned_ref)

    tokens = x_ref.shape[0]
    grad = contract(turned_ref[:, :tokens], y_ref[...], 1, 0)
    grad += contract(turned_ref[:, tokens:], y_other[...], 1, 0)
    deal_out(grad.astype(jnp.bfloat16), *refs[:2])


def attn_grad_kernel(order_ref, *refs):
    x_refs, b_refs, y_refs, a_refs = (refs[2 * j : 2 * j + 2] for j in range(4))
    out_refs, (whole_ref, x_turned, b_turned, grad_ref) = refs[8:10], refs[10:]

    @pl.when(pl.program_id(0) == 0)
    def _():
        turn(order_ref, x_refs, whole_ref, x_turned)
        turn(order_ref, b_refs, whole_ref, b_turned)

    tokens, split = y_refs[0].shape[2], y_refs[0].shape[1]
    for turned, pair, lanes in (
        (x_turned, y_refs, slice(0, split)),
        (b_turned, a_refs, slice(split, grad_ref.shape[1])),
    ):
        grad = contract(turned[:, :tokens], pair[0][0], 1, 1)
        grad += contract(turned[:, tokens:], pair[1][0], 1, 1)
        grad_ref[:, lanes] = grad.astype(jnp.bfloat16)
    deal_out(grad_ref[...], *out_refs)


def masked_scores(queries, keys, group):
    scores = contract(queries, keys, 0, 0) * HD ** (-0.5)
    if group:
        place = lax.broadcasted_iota(jnp.int32, scores.shape, 0) % group
        other = lax.broadcasted_iota(jnp.int32, scores.shape, 1) % group
        scores = jnp.where(place == other, scores, -3e38)
    expo = jnp.exp(scores - jnp.max(scores, axis=-1, keepdims=True))
    return expo / jnp.sum(expo, axis=-1, keepdims=True)


def attend_kernel(group, projected_ref, out_ref):
    part = out_ref.shape[1]
    for start in range(0, part, HD):
        queries, keys, values = (
            projected_ref[0, pl.ds(j * part + start, HD), :] for j in range(3)
        )
        probs = masked_scores(queries, keys, group).astype(jnp.bfloat16)
        out_ref[0, pl.ds(start, HD), :] = contract(values, probs, 1, 1).astype(jnp.bfloat16)


def attend_back_kernel(group, projected_ref, upstream_ref, out_ref):
    part = upstream_ref.shape[1]
    scale_factor = HD ** (-0.5)
    for start in range(0, part, HD):
        queries, keys, values = (
            projected_ref[0, pl.ds(j * part + start, HD), :] for j in range(3)
        )
        upstream = upstream_ref[0, pl.ds(start, HD), :]
        probs = masked_scores(queries, keys, group)
        d_probs = contract(upstream, values, 0, 0)
        row_inner = jnp.sum(probs * d_probs, axis=-1, keepdims=True)
        d_scores = (probs * (d_probs - row_inner)).astype(jnp.bfloat16)
        grads = (
            contract(keys, d_scores, 1, 1) * scale_factor,
            contract(queries, d_scores, 1, 0) * scale_factor,
            contract(upstream, probs.astype(jnp.bfloat16), 1, 0),
        )
        for j in range(3):
            out_ref[0, pl.ds(j * part + start, HD), :] = grads[j].astype(jnp.bfloat16)


def call(kernel, grid, in_specs, out_specs, out_shape, scratch, flops, args):
    moved = sum(a.size * a.dtype.itemsize for a in args)
    moved += sum(o.size * o.dtype.itemsize for o in jax.tree.leaves(out_shape))
    return pl.pallas_call(
        kernel,
        out_shape=out_shape,
        grid_spec=pltpu.PrefetchScalarGridSpec(
            num_scalar_prefetch=1 if scratch else 0,
            grid=grid,
            in_specs=in_specs,
            out_specs=out_specs,
            scratch_shapes=scratch,
        ),
        compiler_params=pltpu.CompilerParams(vmem_limit_bytes=VMEM_BYTES),
        cost_estimate=pl.CostEstimate(
            flops=flops // COST_SHARE, bytes_accessed=moved // COST_SHARE, transcendentals=0
        ),
    )(*args)


def still(shape):
    return pl.BlockSpec(shape, lambda z, *_: (0,) * len(shape))


def lead(shape):
    return pl.BlockSpec((1,) + shape, lambda z, *_: (z,) + (0,) * len(shape))


def column(tokens, width):
    return pl.BlockSpec((tokens, width), lambda z, *_: (0, z))


def sizes(pieces, groups_first):
    groups = pieces[0].shape[0 if groups_first else 1]
    rows, width = pieces[0].shape[2:]
    return groups, rows, width, rows * PIECES


def piece_specs(pieces, groups_first):
    rows, width = pieces[0].shape[2:]
    if groups_first:
        return [lead((2, rows, width))] * PAIRS
    return pair_specs(rows, width, PAIRS)


def pair_specs(rows, width, count):
    return [pl.BlockSpec((2, 1, rows, width), lambda z, *_: (0, z, 0, 0))] * count


def times_up(order, x, pieces, groups_first):
    groups, rows, width, depth = sizes(pieces, groups_first)
    tokens = x.shape[0]
    shape = (tokens, groups * width)
    return call(
        up_kernel,
        (groups,),
        [still(x.shape)] + piece_specs(pieces, groups_first),
        [column(tokens, width)] * 2,
        [jax.ShapeDtypeStruct(shape, jnp.float32), jax.ShapeDtypeStruct(shape, jnp.bfloat16)],
        [pltpu.VMEM((depth, width), jnp.bfloat16)],
        2 * tokens * depth * width * groups,
        (order, x) + pieces,
    )


def times_slope(order, x, pre, pieces, groups_first=False):
    groups, rows, width, depth = sizes(pieces, groups_first)
    tokens = x.shape[0]
    return call(
        slope_kernel,
        (groups,),
        [still(x.shape), column(tokens, width)] + piece_specs(pieces, groups_first),
        column(tokens, width),
        jax.ShapeDtypeStruct(pre.shape, jnp.bfloat16),
        [pltpu.VMEM((depth, width), jnp.bfloat16)],
        2 * tokens * depth * width * groups,
        (order, x, pre) + pieces,
    )


def times_turned(order, x, pieces, low, high, groups_first=False):
    groups, rows, width, depth = sizes(pieces, groups_first)
    tokens = x.shape[0]
    return call(
        functools.partial(turned_kernel, low, high),
        (groups,),
        [still(x.shape)] + piece_specs(pieces, groups_first),
        lead((high - low, tokens)),
        jax.ShapeDtypeStruct((groups, high - low, tokens), jnp.bfloat16),
        [pltpu.VMEM((depth, width), jnp.bfloat16)],
        2 * tokens * depth * width * groups,
        (order, x) + pieces,
    )


def collect(order, y, pieces, low, high, turned, groups_first=False):
    groups, rows, width, depth = sizes(pieces, groups_first)
    tokens = y.shape[2] if turned else y.shape[0]
    return call(
        functools.partial(collect_kernel, low, high, turned),
        (groups,),
        [lead(y.shape[1:]) if turned else column(tokens, width)]
        + piece_specs(pieces, groups_first),
        still((tokens, depth)),
        jax.ShapeDtypeStruct((tokens, depth), jnp.float32),
        [pltpu.VMEM((depth, width), jnp.bfloat16)],
        2 * tokens * depth * (high - low) * groups,
        (order, y) + pieces,
    )


def grad_call(kernel, args, specs, groups, depth, width, scratch):
    rows = depth // PIECES
    tokens = args[1].shape[0]
    return call(
        kernel,
        (groups,),
        specs,
        pair_specs(rows, width, 2),
        [jax.ShapeDtypeStruct((2, groups, rows, width), jnp.bfloat16)] * 2,
        [pltpu.VMEM((depth, tokens), jnp.bfloat16)]
        + [pltpu.VMEM(shape, jnp.bfloat16) for shape in scratch],
        2 * tokens * depth * width * groups,
        args,
    )


def grad_of(order, x, x_other, y, y_other, groups):
    tokens, width = x.shape[0], y.shape[1] // groups
    depth = x.shape[1]
    specs = [still(x.shape)] * 2 + [column(tokens, width)] * 2
    args = (order, x, x_other, y, y_other)
    scratch = [(depth // 2, 2 * tokens)]
    return grad_call(grad_kernel, args, specs, groups, depth, width, scratch)


def attn_grad_of(order, *args):
    x, y, a = args[0], args[4], args[6]
    groups, wide_part, tokens = y.shape
    part, depth = a.shape[1], x.shape[1]
    specs = [still(x.shape)] * 4 + [lead((wide_part, tokens))] * 2 + [lead((part, tokens))] * 2
    scratch = [(depth // 2, 2 * tokens)] * 2 + [(depth // 2, wide_part + part)]
    return grad_call(
        attn_grad_kernel, (order, *args), specs, groups, depth, wide_part + part, scratch
    )


def attend_call(projected, group):
    groups, wide, tokens = projected.shape
    part = wide // 3
    return call(
        functools.partial(attend_kernel, group),
        (groups,),
        [lead((wide, tokens))],
        lead((part, tokens)),
        jax.ShapeDtypeStruct((groups, part, tokens), jnp.bfloat16),
        [],
        4 * tokens * tokens * part * groups,
        (projected,),
    )


def attend_back_call(projected, upstream, group):
    groups, wide, tokens = projected.shape
    part = wide // 3
    return call(
        functools.partial(attend_back_kernel, group),
        (groups,),
        [lead((wide, tokens)), lead((part, tokens))],
        lead((wide, tokens)),
        jax.ShapeDtypeStruct((groups, wide, tokens), jnp.bfloat16),
        [],
        10 * tokens * tokens * part * groups,
        (projected, upstream),
    )


class Layer:
    def __init__(self, line, order, modulation, group):
        self.line = line
        self.order = order
        self.modulation = modulation
        self.group = group
        self.others = {}

    def share(self, *arrays):
        for array in arrays:
            self.others[id(array)] = self.line.hop(array, 0)

    def both(self, array):
        return array, self.others[id(array)]

    def project(self, stream, attn):
        self.stream = stream
        self.attn = attn
        self.width = attn[0].shape[-1]
        self.part = self.width // 4
        rows = self.modulation

        def work(stream, attn):
            normed, inv_scale = layer_norm(stream)
            modulated = low(normed * (1.0 + rows[1]) + rows[0])
            projected = times_turned(self.order, modulated, attn, 0, 3 * self.part)
            return normed, inv_scale, modulated, projected

        made = self.line(work, stream, attn)
        self.normed, self.inv_scale, self.modulated, self.projected = made

    def attend(self):
        self.attended = self.line(
            lambda projected: attend_call(projected, self.group), self.projected
        )

    def attention_out(self):
        rows = self.modulation

        def work(attended, stream, attn):
            branch_attn = collect(self.order, attended, attn, 3 * self.part, self.width, True)
            middle = stream + rows[2] * branch_attn
            normed_mlp, inv_mlp = layer_norm(middle)
            modulated_mlp = low(normed_mlp * (1.0 + rows[4]) + rows[3])
            return branch_attn, middle, normed_mlp, inv_mlp, modulated_mlp

        made = self.line(work, self.attended, self.stream, self.attn)
        self.branch_attn, self.middle, self.normed_mlp, self.inv_mlp, self.modulated_mlp = made

    def mlp_up(self, up, groups_first):
        self.up = up
        self.up_first = groups_first
        work = lambda rows, up: times_up(self.order, rows, up, self.up_first)
        self.hidden_pre, self.hidden_act = self.line(work, self.modulated_mlp, up)

    def mlp_down(self, down, last):
        rows = self.modulation

        def work(act, middle, down):
            branch_mlp = collect(self.order, act, down, 0, self.width, False)
            return branch_mlp, last(middle + rows[5] * branch_mlp)

        self.branch_mlp, result = self.line(work, self.hidden_act, self.middle, down)
        return result

    def turn_back(self, upstream):
        rows = self.modulation
        self.upstream = upstream
        self.d_branch_mlp = self.line(lambda rows_in: low(rows_in * rows[5]), upstream)

    def gradient(self, *args):
        groups = self.attn[0].shape[1]
        work = lambda *rows: grad_of(self.order, *rows, groups)
        return Scatter(self.line, self.line(work, *args))

    def grad_down(self):
        return self.gradient(*self.both(self.d_branch_mlp), *self.both(self.hidden_act))

    def slope(self, down):
        work = lambda rows, pre, down: times_slope(self.order, rows, pre, down)
        self.d_pre = self.line(work, self.d_branch_mlp, self.hidden_pre, down)

    def grad_up(self):
        return self.gradient(*self.both(self.modulated_mlp), *self.both(self.d_pre))

    def back_up(self):
        rows = self.modulation

        def work(d_pre, upstream, normed, inv_mlp, up):
            d_mod_mlp = collect(
                self.order, d_pre, up, 0, self.width, False, self.up_first
            )
            d_middle = upstream + norm_back(normed, inv_mlp, d_mod_mlp * (1.0 + rows[4]))
            return d_mod_mlp, d_middle, low(d_middle * rows[2])

        made = self.line(
            work, self.d_pre, self.upstream, self.normed_mlp, self.inv_mlp, self.up
        )
        self.d_mod_mlp, self.d_middle, self.d_branch_attn = made

    def back_out(self):
        work = lambda rows, attn: times_turned(
            self.order, rows, attn, 3 * self.part, self.width
        )
        self.d_attended = self.line(work, self.d_branch_attn, self.attn)

    def back_attend(self):
        work = lambda projected, upstream: attend_back_call(projected, upstream, self.group)
        self.d_projected = self.line(work, self.projected, self.d_attended)

    def grad_attn(self):
        work = lambda *rows: attn_grad_of(self.order, *rows)
        rows = (self.modulated, self.d_branch_attn, self.d_projected, self.attended)
        grad = self.line(work, *(one for array in rows for one in self.both(array)))
        return Scatter(self.line, grad)

    def back_project(self, last):
        rows = self.modulation

        def work(d_projected, d_middle, normed, inv_scale, attn):
            d_modulated = collect(self.order, d_projected, attn, 0, 3 * self.part, True)
            back = norm_back(normed, inv_scale, d_modulated * (1.0 + rows[1]))
            return d_modulated, last(d_middle + back)

        self.d_modulated, result = self.line(
            work, self.d_projected, self.d_middle, self.normed, self.inv_scale, self.attn
        )
        return result

    def d_modulation(self):
        terms = (
            self.d_modulated,
            self.d_modulated * self.normed,
            self.d_middle * self.branch_attn,
            self.d_mod_mlp,
            self.d_mod_mlp * self.normed_mlp,
            self.upstream * self.branch_mlp,
        )
        return jnp.stack([jnp.sum(term, axis=0) for term in terms])


def finish_grads(attn_piece, up_piece, down_piece):
    rows, width = attn_piece.shape
    part = width // 4
    qkv = attn_piece[:, : 3 * part].reshape(rows, 3, part).astype(jnp.float32)
    attn = attn_piece[:, 3 * part :].T.astype(jnp.float32)
    return qkv, attn, up_piece.astype(jnp.float32), down_piece.T.astype(jnp.float32)


def deal_rows(rows, axes):
    return lax.all_to_all(rows, axes, split_axis=0, concat_axis=0, tiled=True)


def swap_blocks(rows, outer, inner):
    return rows.reshape(outer, inner, -1, rows.shape[1]).swapaxes(0, 1).reshape(rows.shape)


def local_whole(
    x_in,
    cond,
    mod_weight_one,
    qkv_weight_one,
    attn_out_one,
    mlp_up_one,
    mlp_down_one,
    mod_weight_two,
    qkv_weight_two,
    attn_out_two,
    mlp_up_two,
    mlp_down_two,
    out_cotangent,
):
    rows, _, part = qkv_weight_one.shape
    width = x_in.shape[-1]
    packed = [
        pack_layer((qkv_weight_one, attn_out_one, mlp_up_one, mlp_down_one)),
        pack_layer((qkv_weight_two, attn_out_two, mlp_up_two, mlp_down_two)),
    ]
    cond_every = lax.all_gather(cond, CLIP, axis=0, tiled=True).astype(jnp.float32)
    clip_count = cond_every.shape[0]
    silu_every = jax.nn.silu(cond_every).astype(jnp.bfloat16)
    silu_rows = lax.dynamic_slice_in_dim(silu_every, shard_index() * rows, rows, axis=1)
    mod_weights = (mod_weight_one.astype(jnp.bfloat16), mod_weight_two.astype(jnp.bfloat16))
    partial_value = jnp.stack(
        [
            jnp.einsum("cd,dkz->ckz", silu_rows, weight, preferred_element_type=jnp.float32)
            for weight in mod_weights
        ],
        axis=1,
    )
    devices, tensors = lax.axis_size(FRAME), lax.axis_size(TENSOR)
    own_frames = x_in.shape[1]
    own_places = x_in.shape[2] // devices
    cotangent = deal_rows(swap_blocks(out_cotangent.reshape(-1, width), own_frames, devices), FRAME)
    cotangent = swap_blocks(cotangent, devices, own_frames)
    line = Line()
    up_one = MidGather(line, packed[0][1])
    up_one.send()
    line.tick()
    summed = line.exchange_sum(line.exchange_sum(partial_value, FRAME), CLIP)
    line.wait(cotangent)
    summed = lax.dynamic_index_in_dim(summed, lax.axis_index(CLIP), 0, keepdims=False)
    order = piece_order()
    attn_one, down_one = (Gather(line, piece) for piece in packed[0][::2])
    attn_two, up_two, down_two = (Gather(line, piece) for piece in packed[1])
    line.wait(packed)
    up_one.join()
    line.wait(attn_one.whole)
    attn_one.send()
    placed = line.place_along(summed, TENSOR)
    modulations = placed.transpose(1, 2, 0, 3).reshape(summed.shape[:2] + (-1,))

    line.tick()
    attn_one.relay()
    line.under_way.append(up_one.pair)
    line.tick()
    attn_one.end()
    up_one.relay()
    one = Layer(line, order, modulations[0], 0)
    two = Layer(line, order, modulations[1], own_places)

    frames_in = line.send(x_in.reshape(-1, width), lambda held: deal_rows(held, TENSOR))
    one.project(line(wide, frames_in), attn_one.pieces)
    down_one.send()
    one.attend()
    one.attention_out()
    line.tick()
    up_one.end()
    down_one.relay()
    one.mlp_up(up_one.pieces, True)
    cotangent = line(wide, cotangent)
    attn_two.send()
    line.tick()
    down_one.end()
    attn_two.relay()
    between = one.mlp_down(down_one.pieces, low)
    between = line.send(between, lambda held: deal_rows(held, (TENSOR, FRAME)))
    two.turn_back(cotangent)
    up_two.send()
    line.tick()
    attn_two.end()
    up_two.relay()
    two.share(two.d_branch_mlp)
    between = line(wide, between)
    two.project(between, attn_two.pieces)
    down_two.send()
    two.attend()
    two.attention_out()
    line.tick()
    up_two.end()
    down_two.relay()
    two.mlp_up(up_two.pieces, False)
    two.share(two.hidden_act)
    down_grad = two.grad_down()
    line.tick()
    down_two.end()
    two.share(two.modulated_mlp, two.modulated)
    two.slope(down_two.pieces)
    two.share(two.d_pre)
    two.back_up()
    up_grad = two.grad_up()
    line.tick()
    down_grad.relay()
    two.share(two.d_branch_attn, two.attended)
    two.back_out()
    two.back_attend()
    two.share(two.d_projected)
    d_second = two.back_project(low)
    d_second = line.send_ahead(d_second, lambda held: deal_rows(held, (TENSOR, FRAME)))
    attn_grad = two.grad_attn()
    line.tick()
    up_grad.relay()
    one.share(one.hidden_act, one.attended)
    d_second = line(wide, d_second)
    down_grad.finish()
    one.turn_back(d_second)
    one.share(one.d_branch_mlp)
    one.slope(down_one.pieces)
    down_last = one.grad_down()
    line.tick()
    attn_grad.relay()
    one.share(one.d_pre, one.modulated_mlp, one.modulated)
    up_grad.finish()
    one.back_up()
    up_last = one.grad_up()
    one.back_out()
    one.back_attend()
    line.tick()
    down_last.relay()
    one.share(one.d_branch_attn, one.d_projected)
    attn_grad.finish()
    d_first = one.back_project(low)
    result = two.mlp_down(
        down_two.pieces, lambda rows: swap_blocks(low(rows), own_frames, devices)
    )
    d_mods = line(lambda: jnp.stack([one.d_modulation(), two.d_modulation()]))
    d_mods = line(jnp.add, d_mods, flip(d_mods, FRAME, 1))
    attn_last = one.grad_attn()
    d_mods = line(jnp.add, d_mods, flip(d_mods, TENSOR, 1))
    near_mods = flip(d_mods, TENSOR, 2)
    line.tick()
    up_last.relay()
    down_last.finish()
    input_grad = deal_rows(d_first, TENSOR)
    line.under_way.append(input_grad)
    d_mods = line(jnp.add, d_mods, near_mods)
    near_mods = line.send(d_mods, lambda held: flip(held, FRAME, 2))
    line.tick()
    attn_last.relay()
    up_last.finish()
    input_grad = line(wide, input_grad).reshape(x_in.shape)
    line.tick()
    attn_last.finish()
    layer_out = swap_blocks(deal_rows(result, FRAME), devices, own_frames).reshape(x_in.shape)
    d_mods = line(jnp.add, d_mods, near_mods)
    d_mods = lax.dynamic_slice_in_dim(d_mods, lax.axis_index(TENSOR) * part, part, axis=2)
    d_every = line.place_along(d_mods, CLIP)
    silu_float = silu_rows.astype(jnp.float32)
    grad_mods = [
        sum(
            silu_float[c][:, None, None] * d_every[c, layer][None] for c in range(clip_count)
        )
        for layer in range(2)
    ]
    d_silu = jnp.stack(
        [
            sum(
                jnp.sum(
                    d_every[c, layer][None] * mod_weights[layer].astype(jnp.float32), axis=(1, 2)
                )
                for layer in range(2)
            )
            for c in range(clip_count)
        ]
    )
    d_silu = line.exchange_sum(d_silu, TENSOR)
    d_silu = line.place_along(line.place_along(d_silu, FRAME), CLIP)
    d_silu = d_silu.transpose(2, 0, 1, 3).reshape(clip_count, -1)
    d_silu = lax.dynamic_slice_in_dim(d_silu, lax.axis_index(CLIP), 1, axis=0)
    cond_float = cond.astype(jnp.float32)
    sigmoid_cond = jax.nn.sigmoid(cond_float)
    cond_grad = d_silu * (sigmoid_cond * (1.0 + cond_float * (1.0 - sigmoid_cond)))
    first_out = finish_grads(attn_last.piece, up_last.piece, down_last.piece)
    second_out = finish_grads(attn_grad.piece, up_grad.piece, down_grad.piece)
    return (
        layer_out,
        input_grad,
        cond_grad,
        grad_mods[0],
        *first_out,
        grad_mods[1],
        *second_out,
    )


def holds_whole(mesh):
    tensors = mesh.shape[TENSOR]
    return (
        mesh.shape[CLIP] == 2
        and mesh.shape[FRAME] == 4
        and FRAMES % (4 * tensors) == 0
        and tensors & (tensors - 1) == 0
    )


def solution(mesh):
    return jax.shard_map(
        local_whole if holds_whole(mesh) else local,
        mesh=mesh,
        in_specs=(
            P(CLIP, FRAME, TENSOR, None),
            P(CLIP, None),
            P(SHARDS, None, TENSOR),
            P(SHARDS, None, TENSOR),
            P(TENSOR, SHARDS),
            P(SHARDS, TENSOR),
            P(TENSOR, SHARDS),
            P(SHARDS, None, TENSOR),
            P(SHARDS, None, TENSOR),
            P(TENSOR, SHARDS),
            P(SHARDS, TENSOR),
            P(TENSOR, SHARDS),
            P(CLIP, FRAME, TENSOR, None),
        ),
        out_specs=(
            P(CLIP, FRAME, TENSOR, None),
            P(CLIP, FRAME, TENSOR, None),
            P(CLIP, None),
            P(SHARDS, None, TENSOR),
            P(SHARDS, None, TENSOR),
            P(TENSOR, SHARDS),
            P(SHARDS, TENSOR),
            P(TENSOR, SHARDS),
            P(SHARDS, None, TENSOR),
            P(SHARDS, None, TENSOR),
            P(TENSOR, SHARDS),
            P(SHARDS, TENSOR),
            P(TENSOR, SHARDS),
        ),
        check_vma=False,
    )
```
